32 devices in a mesh: tm: 4 (over x, core), rows: 8 (over z, y).
Axes of the slice: x: 2, y: 2, z: 4, core: 2. Of those that a mesh axis runs over, the one named last changes fastest.
Arguments:
- features: bfloat16 [8, 16, 128, 384], P('tm', 'rows'), may hold values from -6 to 6
- block_gain: float32 [384], replicated, may hold values from 0.5 to 1.5
- conv_weight: bfloat16 [3, 3, 3, 384, 384], replicated, may hold values from -0.0625 to 0.0625
- conv_bias: float32 [384], replicated, may hold values from -3 to 3
- latent_weight: bfloat16 [384, 16], replicated, may hold values from -0.3125 to 0.3125
- latent_bias: float32 [16], replicated, may hold values from -3 to 3
- patch_weight: bfloat16 [64, 5120], replicated, may hold values from -0.75 to 0.75
- patch_bias: float32 [5120], replicated, may hold values from -3 to 3
- shift_mod: float32 [5120], replicated, may hold values from -4 to 4
- scale_mod: float32 [5120], replicated, may hold values from -2 to 2
- query_weight: bfloat16 [5120, 5120], P(None, 'tm'), may hold values from -0.078125 to 0.078125
- query_bias: float32 [5120], P('tm'), may hold values from -4 to 4
- query_gain: float32 [5120], P('tm'), may hold values from 0.5 to 1.5
- key_weight: bfloat16 [5120, 5120], P(None, 'tm'), may hold values from -0.078125 to 0.078125
- key_bias: float32 [5120], P('tm'), may hold values from -4 to 4
- key_gain: float32 [5120], P('tm'), may hold values from 0.5 to 1.5
- packing: int32 [32], replicated, may hold values from 0 to 31, each once
Outputs:
- queries: bfloat16 [4096, 5120], P('rows', 'tm')
- keys: bfloat16 [4096, 5120], P('rows', 'tm')
The draws below stay inside these ranges and needn't reach their ends.
All inputs are finite; a program needn't handle non-finite values.
Results may differ from the reference program's by a relative error of at most 0.0054.
Values may be sent and summed in bfloat16 or wider, within the bound.
A program may use at most 128 MiB of HBM per device.

```python
import jax
import jax.numpy as jnp
from jax import lax

C = 384
LAT = 16
D = 5120
FR_DEV = 2
ROW_DEV = 2
COLS = 128
TOK_DEV = 128
FRAMES = 8
ROWS_ALL = 16
BLOCKS = 32
TOKENS = 4096
N_TM = 4
N_ROWS = 8


def level_of(own_key, shape, shards, smallest, top_value):
    level, own = 1.0, jax.random.fold_in(own_key, 6)
    for axis_at, parts in shards:
        heights = jnp.exp(jax.random.uniform(jax.random.fold_in(own, axis_at), (parts,), jnp.float32, smallest / len(shards), top_value / len(shards)))
        level = level * jnp.repeat(heights, shape[axis_at] // parts).reshape([-1 if axis == axis_at else 1 for axis in range(len(shape))])
    return level


def noise(rng, extent, deviation, limit, cuts=(), kind=jnp.bfloat16):
    values = deviation * jax.random.normal(rng, extent, jnp.float32)
    if cuts:
        values = values * level_of(rng, extent, cuts, -0.22, 0.18)
    return jnp.clip(values, -limit, limit).astype(kind)


def setup_inputs(seed: int = 0) -> dict:
    seeds = jax.random.split(jax.random.key(seed), 18)
    return {
        "features": noise(seeds[0], (FRAMES, ROWS_ALL, COLS, C), 1.0, 6.0, ((0, 4), (1, 8))),
        "block_gain": jnp.clip(jax.random.uniform(seeds[1], (C,), jnp.float32, 0.5, 1.5), 0.5, 1.5),
        "conv_weight": noise(seeds[2], (3, 3, 3, C, C), (27 * C) ** -0.5, 0.0625),
        "conv_bias": noise(seeds[3], (C,), 0.5, 3.0, (), jnp.float32),
        "latent_weight": noise(seeds[4], (C, LAT), C ** -0.5, 0.3125),
        "latent_bias": noise(seeds[5], (LAT,), 0.5, 3.0, (), jnp.float32),
        "patch_weight": noise(seeds[6], (4 * LAT, D), (4 * LAT) ** -0.5, 0.75),
        "patch_bias": noise(seeds[7], (D,), 0.5, 3.0, (), jnp.float32),
        "shift_mod": noise(seeds[8], (D,), 1.0, 4.0, (), jnp.float32),
        "scale_mod": noise(seeds[9], (D,), 0.5, 2.0, (), jnp.float32),
        "query_weight": noise(seeds[10], (D, D), D ** -0.5, 0.078125, ((1, 4),)),
        "query_bias": noise(seeds[11], (D,), 1.0, 4.0, ((0, 4),), jnp.float32),
        "query_gain": jnp.clip(0.5 + 1.0 * jax.random.uniform(seeds[12], (D,), jnp.float32) ** level_of(seeds[12], (D,), ((0, 4),), -0.2, 0.2), 0.5, 1.5),
        "key_weight": noise(seeds[13], (D, D), D ** -0.5, 0.078125, ((1, 4),)),
        "key_bias": noise(seeds[14], (D,), 1.0, 4.0, ((0, 4),), jnp.float32),
        "key_gain": jnp.clip(0.5 + 1.0 * jax.random.uniform(seeds[15], (D,), jnp.float32) ** level_of(seeds[15], (D,), ((0, 4),), -0.2, 0.2), 0.5, 1.5),
        "packing": jax.random.permutation(seeds[16], BLOCKS).astype(jnp.int32),
    }


epsilon = 1e-06

def normed_act(features, block_gain):
    values = features.astype(jnp.float32)
    square_mean = lax.optimization_barrier(jnp.mean(values * values, axis=-1, keepdims=True))
    return jax.nn.silu(values * lax.rsqrt(square_mean + epsilon) * block_gain).astype(jnp.bfloat16)

def causal_conv(padded, conv_weight, frames, rows_count, cols_count, channels):
    total = jnp.zeros((frames * rows_count * cols_count, channels), jnp.float32)
    for depth_at in range(3):
        for row_at in range(3):
            slab_part = padded[depth_at:depth_at + frames, row_at:row_at + rows_count]
            joined = jnp.concatenate([slab_part[:, :, 0:cols_count], slab_part[:, :, 1:cols_count + 1], slab_part[:, :, 2:cols_count + 2]], axis=-1)
            kernel = conv_weight[depth_at, row_at].reshape(3 * channels, channels)
            total = total + jnp.dot(joined.reshape(-1, 3 * channels), kernel, preferred_element_type=jnp.float32)
    return total.reshape(frames, rows_count, cols_count, channels)

def project_norm(modulated, weight, bias, gain):
    values = jnp.dot(modulated, weight, preferred_element_type=jnp.float32) + bias
    square_mean = lax.optimization_barrier(jnp.mean(values * values, axis=-1, keepdims=True))
    return (values * lax.rsqrt(square_mean + epsilon) * gain).astype(jnp.bfloat16)

def reference(features, block_gain, conv_weight, conv_bias, latent_weight, latent_bias, patch_weight, patch_bias, shift_mod, scale_mod, query_weight, query_bias, query_gain, key_weight, key_bias, key_gain, packing):
    act = normed_act(features, block_gain)
    padded = jnp.pad(act, ((2, 0), (1, 1), (1, 1), (0, 0)))
    conv = causal_conv(padded, conv_weight, FRAMES, ROWS_ALL, COLS, C)
    block_out = (features.astype(jnp.float32) + conv + conv_bias).astype(jnp.bfloat16)
    latent = (jnp.dot(block_out.reshape(-1, C), latent_weight, preferred_element_type=jnp.float32) + latent_bias).astype(jnp.bfloat16)
    latent = latent.reshape(N_TM, FR_DEV, N_ROWS, ROW_DEV // 2, 2, COLS // 2, 2, LAT)
    blocks = jnp.transpose(latent, (0, 2, 7, 4, 6, 1, 3, 5)).reshape(BLOCKS, 4 * LAT, TOK_DEV)
    chosen = jnp.take(blocks, packing.astype(jnp.int32), axis=0)
    packed = jnp.transpose(chosen, (0, 2, 1)).reshape(TOKENS, 4 * LAT)
    embedded = jnp.dot(packed, patch_weight, preferred_element_type=jnp.float32) + patch_bias
    center = lax.optimization_barrier(jnp.mean(embedded, axis=-1, keepdims=True))
    spread = lax.optimization_barrier(jnp.mean((embedded - center) ** 2, axis=-1, keepdims=True))
    modulated = ((embedded - center) * lax.rsqrt(spread + epsilon) * (1.0 + scale_mod) + shift_mod).astype(jnp.bfloat16)
    queries = project_norm(modulated, query_weight, query_bias, query_gain)
    keys = project_norm(modulated, key_weight, key_bias, key_gain)
    return (queries, keys)
```

```python
import functools

import jax
import jax.numpy as jnp
from jax import lax
from jax.experimental import pallas as pl
from jax.experimental.pallas import tpu as pltpu
from jax.sharding import PartitionSpec as P

epsilon = 1e-06
MESH = pl.DeviceIdType.MESH
F32, BF16 = jnp.float32, jnp.bfloat16
HIGH = lax.Precision.HIGHEST


def dot(a, b, **kw):
    return jnp.dot(a, b, preferred_element_type=F32, **kw)


def split(v):
    hi = v.astype(BF16)
    return hi, (v - hi.astype(F32)).astype(BF16)


def kernel(
    count_t, count_r,
    packing, feat_h, gain_h, conv_h, cbias_h, lw_h, lbias_h, pw_h, pb_h, shift_h, scale_h,
    wq_h, qb_h, qg_h, wk_h, kb_h, kg_h,
    x_out, mat, vec, gram_out,
    feat, gain, conv, cbias, lw, lbias, pw, pb, shift, scale, wq, qb, qg, wk, kb, kg,
    rb, km, lhs, y_ref, fold, snd, rcv, tot, lat_all, mod, cen, m_all, gram_s, gram_r,
    lsem, wsem, hs_sem, hr_sem, as_sem, ar_sem, ss_sem, sr_sem,
):
    t, r = lax.axis_index("tm"), lax.axis_index("rows")
    count = count_t * count_r
    own = t * count_r + r
    _, _, cols, chans = feat.shape
    feats, width = pw.shape
    half = cols // 2

    small = [(feat_h, feat), (gain_h, gain), (lw_h, lw), (cbias_h, cbias), (lbias_h, lbias)]
    late = [
        (pw_h, pw), (pb_h, pb), (shift_h, shift), (scale_h, scale), (qb_h, qb), (kb_h, kb), (qg_h, qg), (kg_h, kg),
    ]
    copies = [pltpu.make_async_copy(s, d, lsem.at[i]) for i, (s, d) in enumerate(small + late)]
    early, later = copies[: len(small)], copies[len(small) :]
    for c in early + later:
        c.start()
    conv_copies = [pltpu.make_async_copy(conv_h.at[:, b], conv.at[:, b], wsem.at[b]) for b in range(3)]
    for c in conv_copies:
        c.start()
    wq_copy = pltpu.make_async_copy(wq_h, wq, wsem.at[3])
    wk_copy = pltpu.make_async_copy(wk_h, wk, wsem.at[4])

    barrier = pltpu.get_barrier_semaphore()

    def greet(i, c):
        other = lax.rem(own + i, count)
        pl.semaphore_signal(barrier, inc=1, device_id=(other // count_r, lax.rem(other, count_r)), device_id_type=MESH)
        return c

    lax.fori_loop(1, count, greet, 0)

    for c in early:
        c.wait()

    def lanes_sum(v):
        out = v[:, 0:128]
        for i in range(1, v.shape[1] // 128):
            out = out + v[:, i * 128 : (i + 1) * 128]
        return out

    lats = lw.shape[0]
    tn = (((0,), (0,)), ((), ()))
    li = lax.broadcasted_iota(jnp.int32, (lats, 2 * feats), 0)
    lj = lax.broadcasted_iota(jnp.int32, (lats, 2 * feats), 1)
    both = ((lj % feats) // 4) == li
    e_both = jnp.where(both, 1.0, 0.0)
    e_low = jnp.where(both & (lj < feats), 1.0, 0.0)
    e_high = jnp.where(both & (lj >= feats), 1.0, 0.0)
    lwv = lw[...]
    lw_low = lax.dot_general(lwv, e_low.astype(BF16), tn, preferred_element_type=F32).astype(BF16)
    lw_high = lax.dot_general(lwv, e_high.astype(BF16), tn, preferred_element_type=F32).astype(BF16)
    lw_both = lax.dot_general(lwv, e_both.astype(BF16), tn, preferred_element_type=F32).astype(BF16)
    span = 2 * feats
    rb[...] = jnp.zeros(rb.shape, BF16)
    rb[pl.ds(0, chans), pl.ds(0, span)] = lw_low
    rb[pl.ds(chans, chans), pl.ds(0, span)] = lw_high
    rb[pl.ds(2 * chans, chans), pl.ds(span, span)] = lw_both
    km[pl.ds(3 * chans, chans), :] = jnp.zeros((chans, km.shape[1]), BF16)
    km[pl.ds(3 * chans, chans), pl.ds(2 * span, span)] = lw_low
    cb8 = jnp.broadcast_to(cbias[...].reshape(1, chans), (8, chans))
    lb8 = jnp.broadcast_to(lbias[...].reshape(1, lats), (8, lats))
    bias8 = dot(cb8, lw_both.astype(F32), precision=HIGH) + dot(lb8, e_both, precision=HIGH)

    gain_v = gain[...].reshape(1, chans)
    row_at = lax.broadcasted_iota(jnp.int32, (cols, chans), 0)
    for f in range(2):
        for w in range(2):
            raw = feat[f, w]
            v = raw.astype(F32)
            sm = jnp.mean(v * v, axis=-1, keepdims=True)
            x = v * lax.rsqrt(sm + epsilon) * gain_v
            act = (x / (1.0 + jnp.exp(-x))).astype(BF16)
            a32 = act.astype(F32)
            prev = jnp.where(row_at == 0, 0.0, pltpu.roll(a32, 1, 0))
            nxt = jnp.where(row_at == cols - 1, 0.0, pltpu.roll(a32, cols - 1, 0))
            at = pl.ds((f * 2 + w) * cols, cols)
            lhs[at, pl.ds(0, chans)] = prev.astype(BF16)
            lhs[at, pl.ds(chans, chans)] = act
            lhs[at, pl.ds(2 * chans, chans)] = nxt.astype(BF16)
            lhs[at, pl.ds(3 * chans, chans)] = raw

    for c in later:
        c.wait()
    rows_m = mod.shape[0] // 2
    step = 512
    total = jnp.zeros((feats, 128), F32)
    total_b = jnp.zeros((1, 128), F32)
    for c in range(0, width, step):
        total = total + lanes_sum(pw[:, c : c + step].astype(F32))
        total_b = total_b + lanes_sum(pb[pl.ds(c, step)].reshape(1, step))
    mean = jnp.sum(total, axis=1, keepdims=True) / width
    mean_b = jnp.sum(total_b, axis=1, keepdims=True) / width
    at16 = lax.broadcasted_iota(jnp.int32, (16, step), 0)
    for c in range(0, width, step):
        gains = 1.0 + scale[pl.ds(c, step)].reshape(1, step)
        center = pw[:, c : c + step].astype(F32) - mean
        center_b = pb[pl.ds(c, step)].reshape(1, step) - mean_b
        moved = shift[pl.ds(c, step)].reshape(1, step)
        last = jnp.where(at16 == 0, center_b * gains, jnp.where(at16 == 1, moved, 0.0))
        for k, part in enumerate(split(center * gains)):
            mod[pl.ds(k * rows_m, feats), c : c + step] = part
        for k, part in enumerate(split(last)):
            mod[pl.ds(k * rows_m + feats, 16), c : c + step] = part
        last = jnp.where(at16 == 0, center_b, 0.0)
        for k, part in enumerate(split(center)):
            cen[pl.ds(k * rows_m, feats), c : c + step] = part
        for k, part in enumerate(split(last)):
            cen[pl.ds(k * rows_m + feats, 16), c : c + step] = part
    nt = (((1,), (1,)), ((), ()))

    def gram_of(v):
        g = lax.dot_general(v, v, nt, preferred_element_type=F32)
        return g[0:rows_m, 0:rows_m] + g[0:rows_m, rows_m:] + g[rows_m:, 0:rows_m] + g[rows_m:, rows_m:]

    gram_s[...] = jnp.zeros(gram_s.shape, F32)
    gram_out[...] = jnp.zeros(gram_out.shape, F32)
    gram_out[0, :, 0:rows_m] = gram_of(cen[...])

    rbv = rb[...]
    for b in range(3):
        conv_copies[b].wait()
        if b == 1:
            wq_copy.start()
        if b == 2:
            wk_copy.start()
        for e in range(3):
            w3 = jnp.concatenate([conv[2, b, e], conv[1, b, e], conv[0, b, e]], axis=1)
            km[pl.ds(e * chans, chans), pl.ds(b * 2 * span, 2 * span)] = dot(w3, rbv).astype(BF16)
        at = pl.ds(b * 2 * span, 2 * span)
        y_ref[:, at] = dot(lhs[...], km[:, at])

    lane = lax.broadcasted_iota(jnp.int32, (cols, span), 1)
    row = lax.broadcasted_iota(jnp.int32, (cols, span), 0)
    even_row = (lane & 2) == 0
    low = lane < feats
    parity = (lane & 1) == (row & 1)

    def y(f, w, b, z):
        return y_ref[pl.ds((f * 2 + w) * cols, cols), pl.ds(b * 2 * span + z * span, span)]

    def mid(f, z):
        return jnp.where(even_row, y(f, 0, 1, z) + y(f, 1, 2, z), y(f, 0, 0, z) + y(f, 1, 1, z))

    def up(f, z):
        return jnp.where(even_row, 0.0, y(f, 0, 2, z))

    def down(f, z):
        return jnp.where(even_row, y(f, 1, 0, z), 0.0)

    for i, part in enumerate((mid, up, down)):
        x0, x1 = part(0, 0), pltpu.roll(part(1, 0), feats, 1)
        mine = jnp.where(low, x0, x0 + x1)
        after = jnp.where(low, x1 + part(0, 1), part(1, 1))
        fold[i] = jnp.where(parity, mine, 0.0)
        fold[3 + i] = jnp.where(parity, after, 0.0)
    for i in range(6):
        snd[i] = fold[i, pl.ds(0, half, 2), :] + fold[i, pl.ds(1, half, 2), :]

    pl.semaphore_wait(barrier, count - 1)

    has_up, has_down = r > 0, r < count_r - 1
    has_next, has_prev = t < count_t - 1, t > 0
    plan = [
        (1, 0, t, r - 1, has_up, has_down),
        (2, 1, t, r + 1, has_down, has_up),
        (3, 2, t + 1, r, has_next, has_prev),
        (4, 3, t + 1, r - 1, has_next & has_up, has_prev & has_down),
        (5, 4, t + 1, r + 1, has_next & has_down, has_prev & has_up),
    ]
    halo = [
        pltpu.make_async_remote_copy(
            src_ref=snd.at[s], dst_ref=rcv.at[d], send_sem=hs_sem.at[d], recv_sem=hr_sem.at[d],
            device_id=(dt, dr), device_id_type=MESH,
        )
        for s, d, dt, dr, _, _ in plan
    ]
    for copy, (_, _, _, _, sends, _) in zip(halo, plan):
        pl.when(sends)(copy.start)
    part = wq.shape[1]
    tile = 256 if part % 256 == 0 else 128
    at_row = lax.broadcasted_iota(jnp.int32, (rows_m, tile), 0)
    heads = ((wq_copy, wq, qb, qg), (wk_copy, wk, kb, kg))

    def project(i):
        copy, w, bias, scaler = heads[i]
        copy.wait()

        def one(n, carry):
            at = pl.ds(pl.multiple_of(n * tile, tile), tile)
            to = pl.ds(pl.multiple_of(i * part + n * tile, 128), tile)
            v = dot(mod[...], w[:, at])
            v = v[0:rows_m] + v[rows_m:] + jnp.where(at_row == feats + 1, bias[at].reshape(1, tile), 0.0)
            for k, piece in enumerate(split(v)):
                m_all[pl.ds(k * rows_m, rows_m), at] = piece
            v = v * scaler[at].reshape(1, tile)
            hi, lo = split(v[0:feats])
            mat[pl.ds(0, feats), to] = hi
            mat[pl.ds(feats, feats), to] = hi
            mat[pl.ds(2 * feats, feats), to] = lo
            mat[pl.ds(3 * feats, feats), to] = lo
            vec[:, to] = v[feats : feats + 8]
            return carry

        lax.fori_loop(0, part // tile, one, 0)
        gram_s[i, :, 0:rows_m] = gram_of(m_all[...])

    project(0)
    tot[...] = snd[0] + bias8[0:1, :]
    for copy, (_, d, _, _, _, gets) in zip(halo, plan):
        def take(copy=copy, d=d):
            copy.wait_recv()
            tot[...] += rcv[d]
        pl.when(gets)(take)
    lat_all[own] = tot[...].astype(BF16)

    side = lax.rem(t, 2)
    mate = t + 1 - 2 * side
    group = count // 2
    place = (t // 2) * count_r + r

    def device(p):
        return (p // count_r) * 2 + side, lax.rem(p, count_r)

    def spread(i):
        dt, dr = device(lax.rem(place + i, group))
        return pltpu.make_async_remote_copy(
            src_ref=lat_all.at[own], dst_ref=lat_all.at[own], send_sem=as_sem.at[i], recv_sem=ar_sem.at[own],
            device_id=(dt, dr), device_id_type=MESH,
        )

    def pass_on(i):
        ft, fr = device(lax.rem(place + group - i, group))
        ident = ft * count_r + fr
        return pltpu.make_async_remote_copy(
            src_ref=lat_all.at[ident], dst_ref=lat_all.at[ident], send_sem=as_sem.at[group + i],
            recv_sem=ar_sem.at[ident], device_id=(mate, r), device_id_type=MESH,
        )

    def from_mate(i):
        ft, fr = device(lax.rem(place + group - i, group))
        ident = (ft + 1 - 2 * side) * count_r + fr
        return pltpu.make_async_remote_copy(
            src_ref=lat_all.at[ident], dst_ref=lat_all.at[ident], send_sem=as_sem.at[group + i],
            recv_sem=ar_sem.at[ident], device_id=(mate, r), device_id_type=MESH,
        )

    def send(i, c):
        spread(i).start()
        return c

    lax.fori_loop(1, group, send, 0)
    pass_on(0).start()
    project(1)
    shares = [
        pltpu.make_async_remote_copy(
            src_ref=gram_s, dst_ref=gram_r.at[i - 1], send_sem=ss_sem.at[i - 1], recv_sem=sr_sem.at[i - 1],
            device_id=(lax.rem(t + i, count_t), r), device_id_type=MESH,
        )
        for i in range(1, count_t)
    ]
    for c in shares:
        c.start()

    def relay(i, c):
        copy = pass_on(i)
        copy.wait_recv()
        copy.start()
        return c

    lax.fori_loop(1, group, relay, 0)

    def arrive(i, c):
        from_mate(i).wait_recv()
        return c

    lax.fori_loop(0, group, arrive, 0)

    for i in range(2):
        gram_out[1 + i] = gram_s[i]
    for i, c in enumerate(shares):
        c.wait_recv()
        for h in range(2):
            gram_out[1 + h] += gram_r[i, h]

    def pick(j, carry):
        x_out[j] = lat_all[packing[r * count_t + j]]
        return carry

    lax.fori_loop(0, count_t, pick, 0)

    for copy, (_, _, _, _, sends, _) in zip(halo, plan):
        pl.when(sends)(copy.wait_send)

    def sent(i, c):
        spread(i).wait_send()
        return c

    lax.fori_loop(1, group, sent, 0)

    def passed(i, c):
        pass_on(i).wait_send()
        return c

    lax.fori_loop(0, group, passed, 0)
    for c in shares:
        c.wait_send()


def per_device(
    features, block_gain, conv_weight, conv_bias, latent_weight, latent_bias, patch_weight, patch_bias,
    shift_mod, scale_mod, query_weight, query_bias, query_gain, key_weight, key_bias, key_gain, packing,
):
    count_t, count_r = lax.axis_size("tm"), lax.axis_size("rows")
    count = count_t * count_r
    _, _, cols, chans = features.shape
    feats, width = patch_weight.shape
    part = query_weight.shape[1]
    half = cols // 2
    span = 2 * feats
    V = pltpu.VMEM
    rows_m = feats + 16
    operands = (
        packing, features, block_gain, conv_weight, conv_bias, latent_weight.T, latent_bias, patch_weight, patch_bias,
        shift_mod, scale_mod, query_weight, query_bias, query_gain, key_weight, key_bias, key_gain,
    )
    like = lambda a: V(a.shape, a.dtype)
    scratch = [like(a) for a in operands[1:]]
    scratch += [
        V((3 * chans, 2 * span), BF16),
        V((4 * chans, 6 * span), BF16),
        V((4 * cols, 4 * chans), BF16),
        V((4 * cols, 6 * span), F32),
        V((6, cols, span), F32),
        V((6, half, span), F32),
        V((5, half, span), F32),
        V((half, span), F32),
        V((count, half, span), BF16),
        V((2 * rows_m, width), BF16),
        V((2 * rows_m, width), BF16),
        V((2 * rows_m, part), BF16),
        V((2, rows_m, 128), F32),
        V((count_t - 1, 2, rows_m, 128), F32),
    ]
    dma = pltpu.SemaphoreType.DMA
    scratch += [dma((13,)), dma((5,)), dma((5,)), dma((5,)), dma((count,)), dma((count,)), dma((count_t - 1,)), dma((count_t - 1,))]
    outs = (
        jax.ShapeDtypeStruct((count_t, half, span), BF16),
        jax.ShapeDtypeStruct((4 * feats, 2 * part), BF16),
        jax.ShapeDtypeStruct((8, 2 * part), F32),
        jax.ShapeDtypeStruct((3, rows_m, 128), F32),
    )
    x, mat, vec, gram = pl.pallas_call(
        functools.partial(kernel, count_t, count_r),
        out_shape=outs,
        in_specs=[pl.BlockSpec(memory_space=pltpu.SMEM)] + [pl.BlockSpec(memory_space=pltpu.HBM)] * 16,
        out_specs=(pl.BlockSpec(memory_space=V),) * 4,
        scratch_shapes=scratch,
        compiler_params=pltpu.CompilerParams(collective_id=0, has_side_effects=True, vmem_limit_bytes=50 * 2**20),
    )(*operands)
    return finish(width, x, mat, vec, gram)


def final(width, x_ref, mat, vec, gram, q_h, k_h, left, coef, tiles, osem):
    count_t, half, span = x_ref.shape
    feats = span // 2
    part = mat.shape[1] // 2
    tokens = left.shape[0]
    tile = tiles.shape[2]
    plane = lax.broadcasted_iota(jnp.int32, (half, span), 1)
    for j in range(count_t):
        p32 = x_ref[j].astype(F32)
        low = jnp.where(plane < feats, p32, 0.0).astype(BF16)
        high = jnp.where(plane < feats, 0.0, p32).astype(BF16)
        for k in range(2):
            left[pl.ds(j * 2 * half, half), pl.ds(k * span, span)] = low
            left[pl.ds(j * 2 * half + half, half), pl.ds(k * span, span)] = high
    lane = lax.broadcasted_iota(jnp.int32, (1, span), 1)

    def quad(g):
        rows = g.shape[0]
        lane_g = lax.broadcasted_iota(jnp.int32, (rows, span), 1)
        twice = jnp.where(lane_g < feats, g, pltpu.roll(g, feats, 1))
        hi, lo = split(jnp.concatenate([twice[0:feats], twice[0:feats]], axis=0))
        return jnp.concatenate([hi, lo], axis=0), twice[feats : feats + 1], twice[feats + 1 : feats + 2]

    def entry(row, at):
        return jnp.sum(jnp.where(lane == at, row, 0.0), axis=1, keepdims=True)

    ge, gq, gk = gram[0], gram[1], gram[2]
    quads = [quad(g) for g in (ge, gq, gk)]
    stacked = jnp.concatenate([q[0] for q in quads], axis=1)
    rows = 128
    for c in range(0, tokens, rows):
        at = pl.ds(c, rows)
        y2 = left[at, :]
        prod = dot(y2, stacked)
        y = y2[:, 0:span].astype(F32)
        e = jnp.sum(y * (prod[:, 0:span] + 2.0 * quads[0][1]), axis=1, keepdims=True) + entry(ge[feats : feats + 1], feats)
        inv = lax.rsqrt(e / width + epsilon)
        for i, g in enumerate((gq, gk)):
            body = inv * (prod[:, (1 + i) * span : (2 + i) * span] + 2.0 * quads[1 + i][1]) + 2.0 * quads[1 + i][2]
            ss = inv * jnp.sum(y * body, axis=1, keepdims=True)
            ss = ss + inv * inv * entry(g[feats : feats + 1], feats)
            ss = ss + 2.0 * inv * entry(g[feats : feats + 1], feats + 1) + entry(g[feats + 1 : feats + 2], feats + 1)
            norm = lax.rsqrt(ss / width + epsilon)
            coef[2 * i, at, :] = jnp.broadcast_to(norm * inv, (rows, 128))
            coef[2 * i + 1, at, :] = jnp.broadcast_to(norm, (rows, 128))
    count_n = part // tile

    def out_copy(i, n, dst):
        return pltpu.make_async_copy(tiles.at[i * count_n + n], dst.at[:, pl.ds(n * tile, tile)], osem.at[i, n])

    for i, dst in enumerate((q_h, k_h)):
        for n in range(count_n):
            for c in range(0, tokens, 256):
                at = pl.ds(c, 256)
                v = dot(left[at, :], mat[:, pl.ds(i * part + n * tile, tile)])
                for l in range(0, tile, 128):
                    to = pl.ds(i * part + n * tile + l, 128)
                    o = coef[2 * i, at, :] * (v[:, l : l + 128] + vec[0:1, to]) + coef[2 * i + 1, at, :] * vec[1:2, to]
                    tiles[i * count_n + n, at, pl.ds(l, 128)] = o.astype(BF16)
            out_copy(i, n, dst).start()
    for i, dst in enumerate((q_h, k_h)):
        for n in range(count_n):
            out_copy(i, n, dst).wait()


def finish(width, x, mat, vec, gram):
    count_t, half, span = x.shape
    tokens, part = count_t * 2 * half, mat.shape[1] // 2
    tile = 256 if part % 256 == 0 else 128
    out = jax.ShapeDtypeStruct((tokens, part), BF16)
    V, dma = pltpu.VMEM, pltpu.SemaphoreType.DMA
    return pl.pallas_call(
        functools.partial(final, width),
        out_shape=(out, out),
        in_specs=[pl.BlockSpec(memory_space=V)] * 4,
        out_specs=(pl.BlockSpec(memory_space=pl.ANY),) * 2,
        scratch_shapes=[
            V((tokens, 2 * span), BF16), V((4, tokens, 128), F32), V((2 * part // tile, tokens, tile), BF16),
            dma((2, part // tile)),
        ],
        compiler_params=pltpu.CompilerParams(vmem_limit_bytes=24 * 2**20),
    )(x, mat, vec, gram)


def solution(mesh):
    in_specs = (
        P("tm", "rows", None, None), P(), P(), P(), P(), P(), P(), P(), P(), P(),
        P(None, "tm"), P("tm"), P("tm"), P(None, "tm"), P("tm"), P("tm"), P(),
    )
    out_specs = (P("rows", "tm"), P("rows", "tm"))
    return jax.shard_map(per_device, mesh=mesh, in_specs=in_specs, out_specs=out_specs, check_vma=False)
```

```python
import functools

import jax
import jax.numpy as jnp
from jax import lax
from jax.experimental import pallas as pl
from jax.experimental.pallas import tpu as pltpu
from jax.sharding import PartitionSpec as P

epsilon = 1e-06
MESH = pl.DeviceIdType.MESH
F32, BF16 = jnp.float32, jnp.bfloat16


def dot(a, b, **kw):
    return jnp.dot(a, b, preferred_element_type=F32, **kw)


def split(v):
    hi = v.astype(BF16)
    return hi, (v - hi.astype(F32)).astype(BF16)


def kernel(
    count_t, count_r,
    packing_h, feat_h, gain_h, conv_h, cbias_h, lw_h, lbias_h, pw_h, pb_h, shift_h, scale_h,
    wq_h, qb_h, qg_h, wk_h, kb_h, kg_h,
    x_out, mat, gram_out,
    packing, feat, gain, conv, cbias, lw, lbias, pw, pb, shift, scale, w_all, qb, kb, qg, kg, rows_qk,
    scr, km, lhs, y_ref, snd, rcv, tot, lat_all, pwf, bounce, mod, cen, m_all, gram, gram_s, gram_r,
    lsem, csem, wsem, hs_sem, hr_sem, as_sem, ar_sem, ss_sem, sr_sem,
):
    t, r = lax.axis_index("tm"), lax.axis_index("rows")
    count = count_t * count_r
    own = t * count_r + r
    _, _, cols, chans = feat.shape
    feats, width = pw.shape
    lats = lw.shape[0]
    half = cols // 2
    part = wq_h.shape[1]
    tile = w_all.shape[2]
    count_n = part // tile
    rows_m = mod.shape[0] // 2

    early = [(feat_h, feat), (gain_h, gain), (lw_h, lw)]
    late = [
        (pw_h, pw), (pb_h, pb), (shift_h, shift), (scale_h, scale), (cbias_h, cbias), (lbias_h, lbias),
        (qb_h, qb), (kb_h, kb), (qg_h, qg), (kg_h, kg), (packing_h, packing),
    ]
    copies = [pltpu.make_async_copy(s, d, lsem.at[i]) for i, (s, d) in enumerate(early + late)]
    first, later = copies[: len(early)], copies[len(early) :]
    taps = [pltpu.make_async_copy(conv_h.at[i // 3, i % 3], conv.at[i // 3, i % 3], csem.at[i]) for i in range(9)]
    for c in first + taps + later:
        c.start()
    loads = [
        pltpu.make_async_copy(w.at[:, pl.ds(n * tile, tile)], w_all.at[h * count_n + n], wsem.at[h * count_n + n])
        for h, w in enumerate((wq_h, wk_h)) for n in range(count_n)
    ]

    barrier = pltpu.get_barrier_semaphore()

    def greet(i, c):
        other = lax.rem(own + i, count)
        pl.semaphore_signal(barrier, inc=1, device_id=(other // count_r, lax.rem(other, count_r)), device_id_type=MESH)
        return c

    lax.fori_loop(1, count, greet, 0)
    nt = (((1,), (1,)), ((), ()))

    for c in first:
        c.wait()
    lwv = lw[...]
    gain_v = gain[...].reshape(1, chans)
    row_at = lax.broadcasted_iota(jnp.int32, (half, 128), 0)
    for f in range(2):
        for w in range(2):
            v = feat[f, w].astype(F32)
            sm = jnp.mean(v * v, axis=-1, keepdims=True)
            x = v * lax.rsqrt(sm + epsilon) * gain_v
            act = (x / (1.0 + jnp.exp(-x))).astype(BF16).astype(F32)
            base = (f * 2 + w) * cols
            for l in range(chans // 128):
                scr[0, l] = act[:, l * 128 : (l + 1) * 128]
                scr[1, l] = v[:, l * 128 : (l + 1) * 128]
                even, odd = scr[0, l, pl.ds(0, half, 2), :], scr[0, l, pl.ds(1, half, 2), :]
                before = jnp.where(row_at == 0, 0.0, pltpu.roll(odd, 1, 0))
                after = jnp.where(row_at == half - 1, 0.0, pltpu.roll(even, half - 1, 0))
                plain = (scr[1, l, pl.ds(0, half, 2), :], scr[1, l, pl.ds(1, half, 2), :])
                for k, (low, high) in enumerate(((before, even), (even, odd), (odd, after), plain)):
                    lhs[pl.ds(base, half), pl.ds(k * chans + l * 128, 128)] = low.astype(BF16)
                    lhs[pl.ds(base + half, half), pl.ds(k * chans + l * 128, 128)] = high.astype(BF16)

    none = jnp.zeros((lats, chans), BF16)
    pair = jnp.concatenate(
        [jnp.concatenate([lwv, none], axis=1), jnp.concatenate([none, lwv], axis=1)], axis=0
    )
    km[:, pl.ds(3 * chans, chans)] = jnp.zeros((9 * lats, chans), BF16)
    km[pl.ds(7 * lats, lats), pl.ds(3 * chans, chans)] = lwv
    started = 0
    for p in range(5):
        ids = [i for i in (2 * p, 2 * p + 1) if i < 9]
        for i in ids:
            taps[i].wait()
        more = min(len(loads), (p + 1) * -(-len(loads) // 5))
        for c in loads[started:more]:
            c.start()
        started = more
        for e in range(3):
            rhs = jnp.concatenate([conv[i // 3, i % 3, e] for i in ids], axis=1)
            left = pair if len(ids) == 2 else lwv
            folded = lax.dot_general(left, rhs, nt, preferred_element_type=F32)
            km[pl.ds(ids[0] * lats, lats * len(ids)), pl.ds(e * chans, chans)] = folded.astype(BF16)
    y_ref[...] = lax.dot_general(km[...], lhs[...], nt, preferred_element_type=F32)

    def total(d, q):
        out = None
        for f in range(2):
            for w in range(2):
                a, b = f + 2 - d, w + 1 - q
                if 0 <= a < 3 and 0 <= b < 3:
                    term = y_ref[pl.ds((a * 3 + b) * lats, lats), pl.ds((f * 2 + w) * cols, cols)]
                    out = term if out is None else out + term
        return out

    sent = [(0, -1), (1, -1), (0, 2), (1, 2), (2, 0), (2, 1), (3, 0), (3, 1), (2, -1), (3, -1), (2, 2), (3, 2)]
    for i, (d, q) in enumerate(sent):
        snd[pl.ds(i * lats, lats), :] = total(d, q)

    pl.semaphore_wait(barrier, count - 1)

    has_up, has_down = r > 0, r < count_r - 1
    has_next, has_prev = t < count_t - 1, t > 0
    plan = [
        (0, 2, t, r - 1, has_up, has_down, (1, 3)),
        (2, 2, t, r + 1, has_down, has_up, (0, 2)),
        (4, 4, t + 1, r, has_next, has_prev, (0, 1, 2, 3)),
        (8, 2, t + 1, r - 1, has_next & has_up, has_prev & has_down, (1, 3)),
        (10, 2, t + 1, r + 1, has_next & has_down, has_prev & has_up, (0, 2)),
    ]
    halo = []
    for k, (at, n, dt, dr, _, _, _) in enumerate(plan):
        rows = pl.ds(at * lats, n * lats)
        halo.append(pltpu.make_async_remote_copy(
            src_ref=snd.at[rows], dst_ref=rcv.at[rows], send_sem=hs_sem.at[k], recv_sem=hr_sem.at[k],
            device_id=(dt, dr), device_id_type=MESH,
        ))
    for copy, p in zip(halo, plan):
        pl.when(p[4])(copy.start)

    for c in later:
        c.wait()
    offset = jnp.sum(lwv.astype(F32) * cbias[...].reshape(1, chans), axis=1, keepdims=True)
    at_l = lax.broadcasted_iota(jnp.int32, (lats, lats), 0) == lax.broadcasted_iota(jnp.int32, (lats, lats), 1)
    offset = offset + jnp.sum(jnp.where(at_l, lbias[...].reshape(1, lats), 0.0), axis=1, keepdims=True)
    for i, (d, q) in enumerate(((0, 0), (0, 1), (1, 0), (1, 1))):
        tot[pl.ds(i * lats, lats), :] = total(d, q) + offset

    step = 512

    def lanes_sum(v):
        out = v[:, 0:128]
        for i in range(1, v.shape[1] // 128):
            out = out + v[:, i * 128 : (i + 1) * 128]
        return out

    total_w = jnp.zeros((feats, 128), F32)
    total_b = jnp.zeros((1, 128), F32)
    groups = feats // lats
    for c in range(0, width, step):
        for l in range(step // 128):
            bounce[l] = pw[:, c + l * 128 : c + (l + 1) * 128].astype(F32)
        mixed = jnp.concatenate([
            jnp.concatenate([bounce[l, pl.ds(k, lats, groups), :] for k in range(groups)], axis=0)
            for l in range(step // 128)
        ], axis=1)
        pwf[:, c : c + step] = mixed
        total_w = total_w + lanes_sum(mixed)
        total_b = total_b + lanes_sum(pb[pl.ds(c, step)].reshape(1, step))
    mean = jnp.sum(total_w, axis=1, keepdims=True) / width
    mean_b = jnp.sum(total_b, axis=1, keepdims=True) / width
    at16 = lax.broadcasted_iota(jnp.int32, (16, step), 0)
    for c in range(0, width, step):
        gains = 1.0 + scale[pl.ds(c, step)].reshape(1, step)
        center = pwf[:, c : c + step] - mean
        center_b = pb[pl.ds(c, step)].reshape(1, step) - mean_b
        moved = shift[pl.ds(c, step)].reshape(1, step)
        last = jnp.where(at16 == 0, center_b * gains, jnp.where(at16 == 1, moved, 0.0))
        for k, piece in enumerate(split(center * gains)):
            mod[pl.ds(k * rows_m, feats), c : c + step] = piece
        for k, piece in enumerate(split(last)):
            mod[pl.ds(k * rows_m + feats, 16), c : c + step] = piece
        last = jnp.where(at16 == 0, center_b, 0.0)
        for k, piece in enumerate(split(center)):
            cen[pl.ds(k * rows_m, feats), c : c + step] = piece
        for k, piece in enumerate(split(last)):
            cen[pl.ds(k * rows_m + feats, 16), c : c + step] = piece

    def gram_of(v):
        g = lax.dot_general(v, v, nt, preferred_element_type=F32)
        return g[0:rows_m, 0:rows_m] + g[0:rows_m, rows_m:] + g[rows_m:, 0:rows_m] + g[rows_m:, rows_m:]

    lower = lax.broadcasted_iota(jnp.int32, (feats // 2, 128), 1) < feats

    def pack(v, ref):
        gram[:, 0:rows_m] = gram_of(v)
        ref[pl.ds(0, feats // 2), :] = jnp.where(
            lower, gram[0 : feats // 2, :], pltpu.roll(gram[feats // 2 : feats, :], feats, 1)
        )
        ref[pl.ds(feats // 2, 8), :] = gram[feats : feats + 8, :]

    gram[...] = jnp.zeros(gram.shape, F32)
    pack(cen[...], gram_out.at[0])
    for h, (bias, gains) in enumerate(((qb, qg), (kb, kg))):
        for n in range(count_n):
            at = pl.ds(n * tile, tile)
            rows_qk[h * count_n + n, 0:1, :] = bias[at].reshape(1, tile)
            rows_qk[h * count_n + n, 1:2, :] = gains[at].reshape(1, tile)
    mat[pl.ds(2 * feats + 16, 2 * feats - 16), :] = jnp.zeros((2 * feats - 16, 2 * part), BF16)
    at_row = lax.broadcasted_iota(jnp.int32, (rows_m, tile), 0)
    at_last = lax.broadcasted_iota(jnp.int32, (16, tile), 0)

    def project(g):
        to = pl.ds(pl.multiple_of(g * tile, tile), tile)
        v = dot(mod[...], w_all[g])
        v = v[0:rows_m] + v[rows_m:] + jnp.where(at_row == feats + 1, rows_qk[g, 0:1, :], 0.0)
        for k, piece in enumerate(split(v)):
            m_all[pl.ds(k * rows_m, rows_m), to] = piece
        v = v * rows_qk[g, 1:2, :]
        for k, piece in enumerate(split(v[0:feats])):
            mat[pl.ds(k * feats, feats), to] = piece
        m, c = v[feats : feats + 1], v[feats + 1 : feats + 2]
        m_hi, c_hi = m.astype(BF16).astype(F32), c.astype(BF16).astype(F32)
        last = jnp.where(at_last % 2 == 0, c_hi, c - c_hi)
        last = jnp.where(at_last == 0, m_hi, jnp.where(at_last == 1, m - m_hi, last))
        mat[pl.ds(2 * feats, 16), to] = jnp.where(at_last < 8, last, 0.0).astype(BF16)

    def both(p, carry):
        for g in (2 * p, 2 * p + 1):
            pltpu.make_async_copy(wq_h.at[:, pl.ds(0, tile)], w_all.at[g], wsem.at[g]).wait()
        for g in (2 * p, 2 * p + 1):
            project(g)
        return carry

    def share(h):
        pack(m_all[:, pl.ds(h * part, part)], gram_s.at[h])
        out = [
            pltpu.make_async_remote_copy(
                src_ref=gram_s.at[h], dst_ref=gram_r.at[i - 1, h], send_sem=ss_sem.at[h, i - 1],
                recv_sem=sr_sem.at[h, i - 1], device_id=(lax.rem(t + i, count_t), r), device_id_type=MESH,
            )
            for i in range(1, count_t)
        ]
        for c in out:
            c.start()
        return out

    lax.fori_loop(0, 1, both, 0)
    for copy, p in zip(halo, plan):
        def take(copy=copy, p=p):
            copy.wait_recv()
            for k, i in enumerate(p[6]):
                tot[pl.ds(i * lats, lats), :] += rcv[pl.ds((p[0] + k) * lats, lats), :]
        pl.when(p[5])(take)

    lane = lax.broadcasted_iota(jnp.int32, (lats, cols), 1)
    for q in range(2):
        f0, f1 = tot[pl.ds(q * lats, lats), :], tot[pl.ds((2 + q) * lats, lats), :]
        lat_all[own, pl.ds(2 * q * lats, lats), :] = jnp.where(lane < half, f0, pltpu.roll(f1, half, 1)).astype(BF16)
        lat_all[own, pl.ds((2 * q + 1) * lats, lats), :] = jnp.where(lane < half, pltpu.roll(f0, half, 1), f1).astype(BF16)

    inner = 1
    while inner * inner * 4 <= count_r and count_r % (inner * 2) == 0:
        inner *= 2
    outer = count_r // inner
    chips = count_t // 2
    flat = chips * inner
    side, chip = lax.rem(t, 2), t // 2
    far, near = r // inner, lax.rem(r, inner)
    spot = chip * inner + near
    turn = 1 - 2 * lax.min(far // max(outer // 2, 1), 1)

    def line_at(i):
        return lax.rem(far + turn * i + outer, outer)

    def device(z, p):
        return (p // inner) * 2 + side, z * inner + lax.rem(p, inner)

    def ident_of(z, p, s):
        return ((p // inner) * 2 + s) * count_r + z * inner + lax.rem(p, inner)

    def send(ident, dt, dr, sem):
        return pltpu.make_async_remote_copy(
            src_ref=lat_all.at[ident], dst_ref=lat_all.at[ident], send_sem=as_sem.at[sem], recv_sem=ar_sem.at[ident],
            device_id=(dt, dr), device_id_type=MESH,
        )

    def to_line(i):
        dt, dr = device(line_at(i), spot)
        return send(own, dt, dr, i - 1)

    def to_plane(i, k):
        dt, dr = device(far, lax.rem(spot + k, flat))
        return send(ident_of(line_at(i), spot, side), dt, dr, outer - 1 + i * flat + k)

    def to_mate(i, k):
        ident = ident_of(line_at(i), lax.rem(spot + flat - k, flat), side)
        return send(ident, t + 1 - 2 * side, r, outer - 1 + outer * flat + i * flat + k)

    def from_mate(i, k):
        return send(ident_of(line_at(i), lax.rem(spot + k, flat), 1 - side), t, r, 0)

    for i in range(1, outer):
        to_line(i).start()
    for k in range(1, flat):
        to_plane(0, k).start()
    to_mate(0, 0).start()

    def relay_line(i):
        to_mate(i, 0).wait_recv()
        for k in range(1, flat):
            to_plane(i, k).start()
        to_mate(i, 0).start()

    def relay_plane(i):
        def one(k, c):
            copy = to_mate(i, k)
            copy.wait_recv()
            copy.start()
            return c

        lax.fori_loop(1, flat, one, 0)

    middle = -(-count_n // 2)
    lax.fori_loop(1, middle, both, 0)
    if outer > 1:
        relay_line(1)
    shares = [share(0)]
    between = (middle + count_n) // 2
    lax.fori_loop(middle, between, both, 0)
    for i in range(2, outer - 1):
        relay_line(i)
    lax.fori_loop(between, count_n, both, 0)
    shares.append(share(1))
    if outer > 2:
        relay_line(outer - 1)

    for i in range(outer):
        relay_plane(i)
    for i in range(outer):
        lax.fori_loop(0, flat, lambda k, c, i=i: (from_mate(i, k).wait_recv(), c)[1], 0)

    for h in range(2):
        gram_out[1 + h] = gram_s[h]
        for i, c in enumerate(shares[h]):
            c.wait_recv()
            gram_out[1 + h] += gram_r[i, h]

    def pick(j, carry):
        x_out[j] = lat_all[packing[r * count_t + j]]
        return carry

    lax.fori_loop(0, count_t, pick, 0)

    for copy, p in zip(halo, plan):
        pl.when(p[4])(copy.wait_send)
    for i in range(1, outer):
        to_line(i).wait_send()
    for i in range(outer):
        for k in range(1, flat):
            to_plane(i, k).wait_send()
        for k in range(flat):
            to_mate(i, k).wait_send()
    for c in shares[0] + shares[1]:
        c.wait_send()


def per_device(
    features, block_gain, conv_weight, conv_bias, latent_weight, latent_bias, patch_weight, patch_bias,
    shift_mod, scale_mod, query_weight, query_bias, query_gain, key_weight, key_bias, key_gain, packing,
):
    count_t, count_r = lax.axis_size("tm"), lax.axis_size("rows")
    count = count_t * count_r
    _, _, cols, chans = features.shape
    feats, width = patch_weight.shape
    lats = latent_weight.shape[1]
    part = query_weight.shape[1]
    tile = 256 if part % 256 == 0 else 128
    V = pltpu.VMEM
    rows_m = feats + 16
    operands = (
        packing, features, block_gain, conv_weight, conv_bias, latent_weight.T, latent_bias, patch_weight, patch_bias,
        shift_mod, scale_mod, query_weight, query_bias, query_gain, key_weight, key_bias, key_gain,
    )
    like = lambda a: V(a.shape, a.dtype)
    scratch = [pltpu.SMEM(packing.shape, packing.dtype)] + [like(a) for a in operands[1:11]]
    scratch += [
        V((2 * part // tile, width, tile), BF16),
        V((part,), F32),
        V((part,), F32),
        V((part,), F32),
        V((part,), F32),
        V((2 * part // tile, 8, tile), F32),
        V((2, chans // 128, cols, 128), F32),
        V((9 * lats, 4 * chans), BF16),
        V((4 * cols, 4 * chans), BF16),
        V((9 * lats, 4 * cols), F32),
        V((12 * lats, cols), F32),
        V((12 * lats, cols), F32),
        V((4 * lats, cols), F32),
        V((count, feats, cols), BF16),
        V((feats, width), F32),
        V((4, feats, 128), F32),
        V((2 * rows_m, width), BF16),
        V((2 * rows_m, width), BF16),
        V((2 * rows_m, 2 * part), BF16),
        V((rows_m, 128), F32),
        V((2, feats // 2 + 8, 128), F32),
        V((count_t - 1, 2, feats // 2 + 8, 128), F32),
    ]
    dma = pltpu.SemaphoreType.DMA
    scratch += [
        dma((14,)), dma((9,)), dma((2 * part // tile,)), dma((5,)), dma((5,)), dma((count + count_r,)), dma((count,)),
        dma((2, count_t - 1)), dma((2, count_t - 1)),
    ]
    outs = (
        jax.ShapeDtypeStruct((count_t, feats, cols), BF16),
        jax.ShapeDtypeStruct((4 * feats, 2 * part), BF16),
        jax.ShapeDtypeStruct((3, feats // 2 + 8, 128), F32),
    )
    x, mat, gram = pl.pallas_call(
        functools.partial(kernel, count_t, count_r),
        out_shape=outs,
        in_specs=[pl.BlockSpec(memory_space=pltpu.HBM)] * 17,
        out_specs=(pl.BlockSpec(memory_space=V),) * 3,
        scratch_shapes=scratch,
        compiler_params=pltpu.CompilerParams(collective_id=0, has_side_effects=True, vmem_limit_bytes=52 * 2**20),
    )(*[pltpu.with_memory_space_constraint(a, pltpu.HBM) for a in operands])
    return finish(width, x, mat, gram)


def final(width, x_ref, mat, gram, q_h, k_h, left, coef, tiles, osem):
    count_t, feats, cols = x_ref.shape
    part = mat.shape[1] // 2
    tokens = left.shape[0]
    tile = tiles.shape[2]
    for j in range(count_t):
        x = x_ref[j].astype(F32)
        left[pl.ds(j * cols, cols), 0:128] = jnp.concatenate([x, x], axis=0).T.astype(BF16)
    lane = lax.broadcasted_iota(jnp.int32, (1, 128), 1)
    hf = feats // 2

    def entry(h, row, at):
        return jnp.sum(jnp.where(lane == at, gram[h, hf + row : hf + row + 1, :], 0.0), axis=1, keepdims=True)

    def cross(h, row):
        return jnp.where(lane < feats, 2.0 * gram[h, hf + row : hf + row + 1, :], 0.0)

    quads = []
    for h in range(3):
        top = gram[h, 0:hf, :]
        square = jnp.where(lane < feats, jnp.concatenate([top, pltpu.roll(top, feats, 1)], axis=0), 0.0)
        quads.append(jnp.concatenate(split(square), axis=0))
    stacked = jnp.concatenate(quads, axis=1)
    rows = 128
    at_lane = lax.broadcasted_iota(jnp.int32, (rows, 128), 1)
    for c in range(0, tokens, rows):
        at = pl.ds(c, rows)
        prod = dot(left[at, 0:128], stacked)
        y = left[at, 0:128].astype(F32)
        e = jnp.sum(y * (prod[:, 0:128] + cross(0, 0)), axis=1, keepdims=True) + entry(0, 0, feats)
        var = e / width + epsilon
        inv = lax.rsqrt(var)
        sigma = jnp.broadcast_to(var * inv, (rows, 128))
        high = sigma.astype(BF16).astype(F32)
        mid = (sigma - high).astype(BF16).astype(F32)
        ends = jnp.where(at_lane < 6, mid, sigma - high - mid)
        ends = jnp.where(at_lane < 2, 1.0, jnp.where(at_lane < 4, high, ends))
        left[at, 128:256] = jnp.where(at_lane < 8, ends, 0.0).astype(BF16)
        for h in range(1, 3):
            body = inv * (prod[:, h * 128 : (h + 1) * 128] + cross(h, 0)) + cross(h, 1)
            ss = inv * jnp.sum(y * body, axis=1, keepdims=True) + inv * inv * entry(h, 0, feats)
            ss = ss + 2.0 * inv * entry(h, 0, feats + 1) + entry(h, 1, feats + 1)
            coef[h - 1, at, :] = jnp.broadcast_to(lax.rsqrt(ss / width + epsilon) * inv, (rows, 128))
    count_n = part // tile

    def out_copy(i, n, dst):
        return pltpu.make_async_copy(tiles.at[i * count_n + n], dst.at[:, pl.ds(n * tile, tile)], osem.at[i, n])

    for i, dst in enumerate((q_h, k_h)):
        for n in range(count_n):
            for c in range(0, tokens, 256):
                at = pl.ds(c, 256)
                v = dot(left[at, :], mat[:, pl.ds(i * part + n * tile, tile)])
                for l in range(0, tile, 128):
                    o = coef[i, at, :] * v[:, l : l + 128]
                    tiles[i * count_n + n, at, pl.ds(l, 128)] = o.astype(BF16)
            out_copy(i, n, dst).start()
    for i, dst in enumerate((q_h, k_h)):
        for n in range(count_n):
            out_copy(i, n, dst).wait()


def finish(width, x, mat, gram):
    count_t, feats, cols = x.shape
    tokens, part = count_t * cols, mat.shape[1] // 2
    tile = 256 if part % 256 == 0 else 128
    out = jax.ShapeDtypeStruct((tokens, part), BF16)
    V, dma = pltpu.VMEM, pltpu.SemaphoreType.DMA
    return pl.pallas_call(
        functools.partial(final, width),
        out_shape=(out, out),
        in_specs=[pl.BlockSpec(memory_space=V)] * 3,
        out_specs=(pl.BlockSpec(memory_space=pl.ANY),) * 2,
        scratch_shapes=[
            V((tokens, 4 * feats), BF16), V((2, tokens, 128), F32), V((2 * part // tile, tokens, tile), BF16),
            dma((2, part // tile)),
        ],
        compiler_params=pltpu.CompilerParams(vmem_limit_bytes=24 * 2**20),
    )(x, mat, gram)


def solution(mesh):
    in_specs = (
        P("tm", "rows", None, None), P(), P(), P(), P(), P(), P(), P(), P(), P(),
        P(None, "tm"), P("tm"), P("tm"), P(None, "tm"), P("tm"), P("tm"), P(),
    )
    out_specs = (P("rows", "tm"), P("rows", "tm"))
    return jax.shard_map(per_device, mesh=mesh, in_specs=in_specs, out_specs=out_specs, check_vma=False)
```

```python
import functools

import jax
import jax.numpy as jnp
from jax import lax
from jax.experimental import pallas as pl
from jax.experimental.pallas import tpu as pltpu
from jax.sharding import PartitionSpec as P

epsilon = 1e-06
MESH = pl.DeviceIdType.MESH
F32, BF16 = jnp.float32, jnp.bfloat16


def dot(a, b, **kw):
    return jnp.dot(a, b, preferred_element_type=F32, **kw)


def split(v):
    hi = v.astype(BF16)
    return hi, (v - hi.astype(F32)).astype(BF16)


def kernel(
    count_t, count_r,
    packing_h, feat_h, gain_h, conv_h, cbias_h, lw_h, lbias_h, pw_h, pb_h, shift_h, scale_h,
    wq_h, qb_h, qg_h, wk_h, kb_h, kg_h,
    x_out, mat, gram_out,
    packing, feat, gain, conv, cbias, lw, lbias, pw, pb, shift, scale, w_all, qb, kb, qg, kg, rows_qk,
    scr, km, lhs, y_ref, snd, rcv, tot, lat_all, pwf, bounce, mod, cen, m_all, gram, gram_s, gram_r,
    lsem, csem, wsem, hs_sem, hr_sem, as_sem, ar_sem, ss_sem, sr_sem,
):
    t, r = lax.axis_index("tm"), lax.axis_index("rows")
    count = count_t * count_r
    own = t * count_r + r
    _, _, cols, chans = feat.shape
    feats, width = pw.shape
    lats = lw.shape[0]
    half = cols // 2
    part = wq_h.shape[1]
    tile = w_all.shape[2]
    count_n = part // tile
    rows_m = mod.shape[0] // 2

    early = [(feat_h, feat), (gain_h, gain), (lw_h, lw)]
    late = [
        (pw_h, pw), (pb_h, pb), (shift_h, shift), (scale_h, scale), (cbias_h, cbias), (lbias_h, lbias),
        (qb_h, qb), (kb_h, kb), (qg_h, qg), (kg_h, kg), (packing_h, packing),
    ]
    copies = [pltpu.make_async_copy(s, d, lsem.at[i]) for i, (s, d) in enumerate(early + late)]
    first, later = copies[: len(early)], copies[len(early) :]
    taps = [pltpu.make_async_copy(conv_h.at[i // 3, i % 3], conv.at[i // 3, i % 3], csem.at[i]) for i in range(9)]
    for c in first + taps + later:
        c.start()
    loads = [
        pltpu.make_async_copy(w.at[:, pl.ds(n * tile, tile)], w_all.at[h * count_n + n], wsem.at[h * count_n + n])
        for h, w in enumerate((wq_h, wk_h)) for n in range(count_n)
    ]

    barrier = pltpu.get_barrier_semaphore()

    def greet(i, c):
        other = lax.rem(own + i, count)
        pl.semaphore_signal(barrier, inc=1, device_id=(other // count_r, lax.rem(other, count_r)), device_id_type=MESH)
        return c

    lax.fori_loop(1, count, greet, 0)
    nt = (((1,), (1,)), ((), ()))

    for c in first:
        c.wait()
    lwv = lw[...]
    gain_v = gain[...].reshape(1, chans)
    row_at = lax.broadcasted_iota(jnp.int32, (half, 128), 0)
    for f in range(2):
        for w in range(2):
            v = feat[f, w].astype(F32)
            sm = jnp.mean(v * v, axis=-1, keepdims=True)
            x = v * lax.rsqrt(sm + epsilon) * gain_v
            act = (x / (1.0 + jnp.exp(-x))).astype(BF16).astype(F32)
            base = (f * 2 + w) * cols
            for l in range(chans // 128):
                scr[0, l] = act[:, l * 128 : (l + 1) * 128]
                scr[1, l] = v[:, l * 128 : (l + 1) * 128]
                even, odd = scr[0, l, pl.ds(0, half, 2), :], scr[0, l, pl.ds(1, half, 2), :]
                before = jnp.where(row_at == 0, 0.0, pltpu.roll(odd, 1, 0))
                after = jnp.where(row_at == half - 1, 0.0, pltpu.roll(even, half - 1, 0))
                plain = (scr[1, l, pl.ds(0, half, 2), :], scr[1, l, pl.ds(1, half, 2), :])
                for k, (low, high) in enumerate(((before, even), (even, odd), (odd, after), plain)):
                    lhs[pl.ds(base, half), pl.ds(k * chans + l * 128, 128)] = low.astype(BF16)
                    lhs[pl.ds(base + half, half), pl.ds(k * chans + l * 128, 128)] = high.astype(BF16)

    none = jnp.zeros((lats, chans), BF16)
    pair = jnp.concatenate(
        [jnp.concatenate([lwv, none], axis=1), jnp.concatenate([none, lwv], axis=1)], axis=0
    )
    km[:, pl.ds(3 * chans, chans)] = jnp.zeros((9 * lats, chans), BF16)
    km[pl.ds(7 * lats, lats), pl.ds(3 * chans, chans)] = lwv
    started = 0
    for p in range(5):
        ids = [i for i in (2 * p, 2 * p + 1) if i < 9]
        for i in ids:
            taps[i].wait()
        more = min(len(loads), (p + 1) * -(-len(loads) // 5))
        for c in loads[started:more]:
            c.start()
        started = more
        for e in range(3):
            rhs = jnp.concatenate([conv[i // 3, i % 3, e] for i in ids], axis=1)
            left = pair if len(ids) == 2 else lwv
            folded = lax.dot_general(left, rhs, nt, preferred_element_type=F32)
            km[pl.ds(ids[0] * lats, lats * len(ids)), pl.ds(e * chans, chans)] = folded.astype(BF16)
    y_ref[...] = lax.dot_general(km[...], lhs[...], nt, preferred_element_type=F32)

    def total(d, q):
        out = None
        for f in range(2):
            for w in range(2):
                a, b = f + 2 - d, w + 1 - q
                if 0 <= a < 3 and 0 <= b < 3:
                    term = y_ref[pl.ds((a * 3 + b) * lats, lats), pl.ds((f * 2 + w) * cols, cols)]
                    out = term if out is None else out + term
        return out

    sent = [(0, -1), (1, -1), (0, 2), (1, 2), (2, 0), (2, 1), (3, 0), (3, 1), (2, -1), (3, -1), (2, 2), (3, 2)]
    for i, (d, q) in enumerate(sent):
        snd[pl.ds(i * lats, lats), :] = total(d, q)

    pl.semaphore_wait(barrier, count - 1)

    has_up, has_down = r > 0, r < count_r - 1
    has_next, has_prev = t < count_t - 1, t > 0
    plan = [
        (0, 2, t, r - 1, has_up, has_down, (1, 3)),
        (2, 2, t, r + 1, has_down, has_up, (0, 2)),
        (4, 4, t + 1, r, has_next, has_prev, (0, 1, 2, 3)),
        (8, 2, t + 1, r - 1, has_next & has_up, has_prev & has_down, (1, 3)),
        (10, 2, t + 1, r + 1, has_next & has_down, has_prev & has_up, (0, 2)),
    ]
    halo = []
    for k, (at, n, dt, dr, _, _, _) in enumerate(plan):
        rows = pl.ds(at * lats, n * lats)
        halo.append(pltpu.make_async_remote_copy(
            src_ref=snd.at[rows], dst_ref=rcv.at[rows], send_sem=hs_sem.at[k], recv_sem=hr_sem.at[k],
            device_id=(dt, dr), device_id_type=MESH,
        ))
    for copy, p in zip(halo, plan):
        pl.when(p[4])(copy.start)

    for c in later:
        c.wait()
    offset = jnp.sum(lwv.astype(F32) * cbias[...].reshape(1, chans), axis=1, keepdims=True)
    at_l = lax.broadcasted_iota(jnp.int32, (lats, lats), 0) == lax.broadcasted_iota(jnp.int32, (lats, lats), 1)
    offset = offset + jnp.sum(jnp.where(at_l, lbias[...].reshape(1, lats), 0.0), axis=1, keepdims=True)
    for i, (d, q) in enumerate(((0, 0), (0, 1), (1, 0), (1, 1))):
        tot[pl.ds(i * lats, lats), :] = total(d, q) + offset

    step = 512

    def lanes_sum(v):
        out = v[:, 0:128]
        for i in range(1, v.shape[1] // 128):
            out = out + v[:, i * 128 : (i + 1) * 128]
        return out

    total_w = jnp.zeros((feats, 128), F32)
    total_b = jnp.zeros((1, 128), F32)
    groups = feats // lats
    for c in range(0, width, step):
        for l in range(step // 128):
            bounce[l] = pw[:, c + l * 128 : c + (l + 1) * 128].astype(F32)
        mixed = jnp.concatenate([
            jnp.concatenate([bounce[l, pl.ds(k, lats, groups), :] for k in range(groups)], axis=0)
            for l in range(step // 128)
        ], axis=1)
        pwf[:, c : c + step] = mixed
        total_w = total_w + lanes_sum(mixed)
        total_b = total_b + lanes_sum(pb[pl.ds(c, step)].reshape(1, step))
    mean = jnp.sum(total_w, axis=1, keepdims=True) / width
    mean_b = jnp.sum(total_b, axis=1, keepdims=True) / width
    at16 = lax.broadcasted_iota(jnp.int32, (16, step), 0)
    for c in range(0, width, step):
        gains = 1.0 + scale[pl.ds(c, step)].reshape(1, step)
        center = pwf[:, c : c + step] - mean
        center_b = pb[pl.ds(c, step)].reshape(1, step) - mean_b
        moved = shift[pl.ds(c, step)].reshape(1, step)
        last = jnp.where(at16 == 0, center_b * gains, jnp.where(at16 == 1, moved, 0.0))
        for k, piece in enumerate(split(center * gains)):
            mod[pl.ds(k * rows_m, feats), c : c + step] = piece
        for k, piece in enumerate(split(last)):
            mod[pl.ds(k * rows_m + feats, 16), c : c + step] = piece
        last = jnp.where(at16 == 0, center_b, 0.0)
        for k, piece in enumerate(split(center)):
            cen[pl.ds(k * rows_m, feats), c : c + step] = piece
        for k, piece in enumerate(split(last)):
            cen[pl.ds(k * rows_m + feats, 16), c : c + step] = piece

    def gram_of(v):
        g = lax.dot_general(v, v, nt, preferred_element_type=F32)
        return g[0:rows_m, 0:rows_m] + g[0:rows_m, rows_m:] + g[rows_m:, 0:rows_m] + g[rows_m:, rows_m:]

    lower = lax.broadcasted_iota(jnp.int32, (feats // 2, 128), 1) < feats

    def pack(v, ref):
        gram[:, 0:rows_m] = gram_of(v)
        ref[pl.ds(0, feats // 2), :] = jnp.where(
            lower, gram[0 : feats // 2, :], pltpu.roll(gram[feats // 2 : feats, :], feats, 1)
        )
        ref[pl.ds(feats // 2, 8), :] = gram[feats : feats + 8, :]

    gram[...] = jnp.zeros(gram.shape, F32)
    for h, (bias, gains) in enumerate(((qb, qg), (kb, kg))):
        for n in range(count_n):
            at = pl.ds(n * tile, tile)
            rows_qk[h * count_n + n, 0:1, :] = bias[at].reshape(1, tile)
            rows_qk[h * count_n + n, 1:2, :] = gains[at].reshape(1, tile)
    mat[pl.ds(2 * feats + 16, 2 * feats - 16), :] = jnp.zeros((2 * feats - 16, 2 * part), BF16)
    at_row = lax.broadcasted_iota(jnp.int32, (rows_m, tile), 0)
    at_last = lax.broadcasted_iota(jnp.int32, (16, tile), 0)

    def project(g):
        to = pl.ds(pl.multiple_of(g * tile, tile), tile)
        v = dot(mod[...], w_all[g])
        v = v[0:rows_m] + v[rows_m:] + jnp.where(at_row == feats + 1, rows_qk[g, 0:1, :], 0.0)
        for k, piece in enumerate(split(v)):
            m_all[pl.ds(k * rows_m, rows_m), to] = piece
        v = v * rows_qk[g, 1:2, :]
        for k, piece in enumerate(split(v[0:feats])):
            mat[pl.ds(k * feats, feats), to] = piece
        m, c = v[feats : feats + 1], v[feats + 1 : feats + 2]
        m_hi, c_hi = m.astype(BF16).astype(F32), c.astype(BF16).astype(F32)
        last = jnp.where(at_last % 2 == 0, c_hi, c - c_hi)
        last = jnp.where(at_last == 0, m_hi, jnp.where(at_last == 1, m - m_hi, last))
        mat[pl.ds(2 * feats, 16), to] = jnp.where(at_last < 8, last, 0.0).astype(BF16)

    def both(p, carry):
        for g in (2 * p, 2 * p + 1):
            pltpu.make_async_copy(wq_h.at[:, pl.ds(0, tile)], w_all.at[g], wsem.at[g]).wait()
        for g in (2 * p, 2 * p + 1):
            project(g)
        return carry

    def share(h):
        pack(m_all[:, pl.ds(h * part, part)], gram_s.at[h])
        out = [
            pltpu.make_async_remote_copy(
                src_ref=gram_s.at[h], dst_ref=gram_r.at[i - 1, h], send_sem=ss_sem.at[h, i - 1],
                recv_sem=sr_sem.at[h, i - 1], device_id=(lax.rem(t + i, count_t), r), device_id_type=MESH,
            )
            for i in range(1, count_t)
        ]
        for c in out:
            c.start()
        return out

    middle = -(-count_n // 2)
    ahead = min(2, middle)
    lax.fori_loop(0, ahead, both, 0)
    for copy, p in zip(halo, plan):
        def take(copy=copy, p=p):
            copy.wait_recv()
            for k, i in enumerate(p[6]):
                tot[pl.ds(i * lats, lats), :] += rcv[pl.ds((p[0] + k) * lats, lats), :]
        pl.when(p[5])(take)

    lane = lax.broadcasted_iota(jnp.int32, (lats, cols), 1)
    for q in range(2):
        f0, f1 = tot[pl.ds(q * lats, lats), :], tot[pl.ds((2 + q) * lats, lats), :]
        lat_all[own, pl.ds(2 * q * lats, lats), :] = jnp.where(lane < half, f0, pltpu.roll(f1, half, 1)).astype(BF16)
        lat_all[own, pl.ds((2 * q + 1) * lats, lats), :] = jnp.where(lane < half, pltpu.roll(f0, half, 1), f1).astype(BF16)

    inner = 1
    while inner * inner * 4 <= count_r and count_r % (inner * 2) == 0:
        inner *= 2
    outer = count_r // inner
    chips = count_t // 2
    flat = chips * inner
    side, chip = lax.rem(t, 2), t // 2
    far, near = r // inner, lax.rem(r, inner)
    spot = chip * inner + near
    flip = lax.min(far // max(outer // 2, 1), 1)
    mirror = far + flip * (outer - 1 - 2 * far)

    def line_at(i):
        v = lax.rem(mirror + i, outer)
        if outer == 4:
            v = (mirror, mirror + 1, 2 - 2 * mirror, mirror * 0 + 3)[i]
        return v + flip * (outer - 1 - 2 * v)

    def device(z, p):
        return (p // inner) * 2 + side, z * inner + lax.rem(p, inner)

    def ident_of(z, p, s):
        return ((p // inner) * 2 + s) * count_r + z * inner + lax.rem(p, inner)

    def send(ident, dt, dr, sem):
        return pltpu.make_async_remote_copy(
            src_ref=lat_all.at[ident], dst_ref=lat_all.at[ident], send_sem=as_sem.at[sem], recv_sem=ar_sem.at[ident],
            device_id=(dt, dr), device_id_type=MESH,
        )

    def to_line(i):
        dt, dr = device(line_at(i), spot)
        return send(own, dt, dr, i - 1)

    def to_plane(i, k):
        dt, dr = device(far, lax.rem(spot + k, flat))
        return send(ident_of(line_at(i), spot, side), dt, dr, outer - 1 + i * flat + k)

    def to_mate(i, k):
        ident = ident_of(line_at(i), lax.rem(spot + flat - k, flat), side)
        return send(ident, t + 1 - 2 * side, r, outer - 1 + outer * flat + i * flat + k)

    def from_mate(i, k):
        return send(ident_of(line_at(i), lax.rem(spot + k, flat), 1 - side), t, r, 0)

    def to_far(k):
        dt, dr = device(line_at(outer - 1), lax.rem(spot + k, flat))
        return send(own, dt, dr, outer - 1 + (outer - 1) * flat + k)

    for i in range(1, outer):
        to_line(i).start()
    for k in range(1, flat):
        to_plane(0, k).start()
    if outer > 1:
        @pl.when(mirror == 0)
        def _():
            for k in range(1, flat):
                to_far(k).start()
    to_mate(0, 0).start()

    def relay_line(i):
        to_mate(i, 0).wait_recv()

        def forward():
            for k in range(1, flat):
                to_plane(i, k).start()

        if i == outer - 1:
            pl.when(mirror > 0)(forward)
        else:
            forward()
        to_mate(i, 0).start()

    def relay_plane(i):
        def one(k, c):
            copy = to_mate(i, k)
            copy.wait_recv()
            copy.start()
            return c

        lax.fori_loop(1, flat, one, 0)

    lax.fori_loop(ahead, middle, both, 0)
    shares = [share(0)]
    if outer > 1:
        relay_line(1)
    between = (middle + count_n) // 2
    lax.fori_loop(middle, between, both, 0)
    if outer > 2:
        relay_line(2)
    lax.fori_loop(between, count_n, both, 0)
    shares.append(share(1))
    for i in range(3, outer):
        relay_line(i)
    relay_plane(0)
    pack(cen[...], gram_out.at[0])

    for i in range(1, outer):
        relay_plane(i)
    for i in range(outer):
        lax.fori_loop(0, flat, lambda k, c, i=i: (from_mate(i, k).wait_recv(), c)[1], 0)

    for h in range(2):
        gram_out[1 + h] = gram_s[h]
        for i, c in enumerate(shares[h]):
            c.wait_recv()
            gram_out[1 + h] += gram_r[i, h]

    def pick(j, carry):
        x_out[j] = lat_all[packing[r * count_t + j]]
        return carry

    lax.fori_loop(0, count_t, pick, 0)

    for copy, p in zip(halo, plan):
        pl.when(p[4])(copy.wait_send)
    for i in range(1, outer):
        to_line(i).wait_send()
    for i in range(outer):
        for k in range(1, flat):
            to_plane(i, k).wait_send()
        for k in range(flat):
            to_mate(i, k).wait_send()
    for c in shares[0] + shares[1]:
        c.wait_send()


def per_device(
    features, block_gain, conv_weight, conv_bias, latent_weight, latent_bias, patch_weight, patch_bias,
    shift_mod, scale_mod, query_weight, query_bias, query_gain, key_weight, key_bias, key_gain, packing,
):
    count_t, count_r = lax.axis_size("tm"), lax.axis_size("rows")
    count = count_t * count_r
    _, _, cols, chans = features.shape
    feats, width = patch_weight.shape
    lats = latent_weight.shape[1]
    part = query_weight.shape[1]
    tile = 256 if part % 256 == 0 else 128
    V = pltpu.VMEM
    rows_m = feats + 16
    operands = (
        packing, features, block_gain, conv_weight, conv_bias, latent_weight.T, latent_bias, patch_weight, patch_bias,
        shift_mod, scale_mod, query_weight, query_bias, query_gain, key_weight, key_bias, key_gain,
    )
    like = lambda a: V(a.shape, a.dtype)
    scratch = [pltpu.SMEM(packing.shape, packing.dtype)] + [like(a) for a in operands[1:11]]
    scratch += [
        V((2 * part // tile, width, tile), BF16),
        V((part,), F32),
        V((part,), F32),
        V((part,), F32),
        V((part,), F32),
        V((2 * part // tile, 8, tile), F32),
        V((2, chans // 128, cols, 128), F32),
        V((9 * lats, 4 * chans), BF16),
        V((4 * cols, 4 * chans), BF16),
        V((9 * lats, 4 * cols), F32),
        V((12 * lats, cols), F32),
        V((12 * lats, cols), F32),
        V((4 * lats, cols), F32),
        V((count, feats, cols), BF16),
        V((feats, width), F32),
        V((4, feats, 128), F32),
        V((2 * rows_m, width), BF16),
        V((2 * rows_m, width), BF16),
        V((2 * rows_m, 2 * part), BF16),
        V((rows_m, 128), F32),
        V((2, feats // 2 + 8, 128), F32),
        V((count_t - 1, 2, feats // 2 + 8, 128), F32),
    ]
    dma = pltpu.SemaphoreType.DMA
    scratch += [
        dma((14,)), dma((9,)), dma((2 * part // tile,)), dma((5,)), dma((5,)), dma((count + count_r,)), dma((count,)),
        dma((2, count_t - 1)), dma((2, count_t - 1)),
    ]
    outs = (
        jax.ShapeDtypeStruct((count_t, feats, cols), BF16),
        jax.ShapeDtypeStruct((4 * feats, 2 * part), BF16),
        jax.ShapeDtypeStruct((3, feats // 2 + 8, 128), F32),
    )
    x, mat, gram = pl.pallas_call(
        functools.partial(kernel, count_t, count_r),
        out_shape=outs,
        in_specs=[pl.BlockSpec(memory_space=pltpu.HBM)] * 17,
        out_specs=(pl.BlockSpec(memory_space=V),) * 3,
        scratch_shapes=scratch,
        compiler_params=pltpu.CompilerParams(collective_id=0, has_side_effects=True, vmem_limit_bytes=52 * 2**20),
    )(*[pltpu.with_memory_space_constraint(a, pltpu.HBM) for a in operands])
    return finish(width, x, mat, gram)


def final(width, x_ref, mat, gram, q_h, k_h, left, coef, tiles, osem):
    count_t, feats, cols = x_ref.shape
    part = mat.shape[1] // 2
    tokens = left.shape[0]
    tile = tiles.shape[2]
    lane = lax.broadcasted_iota(jnp.int32, (1, 128), 1)
    hf = feats // 2
    quads, ends = [], []
    for h in range(3):
        top, tail = gram[h, 0:hf, :], gram[h, hf : hf + 8, :]
        square = jnp.where(lane < feats, jnp.concatenate([top, pltpu.roll(top, feats, 1)], axis=0), 0.0)
        quads.append(square)
        ends.append(jnp.where(lane < feats, tail, 0.0))

    def entry(h, row, at):
        return jnp.sum(jnp.where(lane == at, gram[h, hf + row : hf + row + 1, :], 0.0), axis=1, keepdims=True)

    hi, lo = split(jnp.concatenate(quads + ends, axis=0))
    lo_at = pltpu.roll(lo.astype(F32), feats, 1).astype(BF16)
    stacked = hi + lo_at
    at16 = lax.broadcasted_iota(jnp.int32, (16, cols), 0)
    for j in range(count_t):
        x = x_ref[j]
        prod = dot(stacked, jnp.concatenate([x, x], axis=0))
        x = x.astype(F32)
        line = lambda h, row: prod[3 * feats + 8 * h + row : 3 * feats + 8 * h + row + 1, :]
        square = lambda h: jnp.sum(x * prod[h * feats : (h + 1) * feats, :], axis=0, keepdims=True)
        var = (square(0) + 2.0 * line(0, 0) + entry(0, 0, feats)) / width + epsilon
        inv = lax.rsqrt(var)
        sigma = var * inv
        high = sigma.astype(BF16).astype(F32)
        mid = (sigma - high).astype(BF16).astype(F32)
        more = jnp.where(at16 < 4, high, jnp.where(at16 < 6, mid, sigma - high - mid))
        more = jnp.where(at16 < 2, 1.0, jnp.where(at16 < 8, more, 0.0))
        at = pl.ds(j * cols, cols)
        rest = jnp.zeros((2 * feats - 16, cols), F32)
        left[at, :] = jnp.concatenate([x, x, more, rest], axis=0).T.astype(BF16)
        for h in range(1, 3):
            ss = inv * inv * (square(h) + 2.0 * line(h, 0) + entry(h, 0, feats))
            ss = ss + 2.0 * inv * (line(h, 1) + entry(h, 0, feats + 1)) + entry(h, 1, feats + 1)
            coef[h - 1, at, :] = jnp.broadcast_to(lax.rsqrt(ss / width + epsilon) * inv, (128, cols)).T
    count_n = part // tile

    def out_copy(i, n, dst):
        return pltpu.make_async_copy(tiles.at[i * count_n + n], dst.at[:, pl.ds(n * tile, tile)], osem.at[i, n])

    for i, dst in enumerate((q_h, k_h)):
        for n in range(count_n):
            for c in range(0, tokens, 256):
                at = pl.ds(c, 256)
                v = dot(left[at, :], mat[:, pl.ds(i * part + n * tile, tile)])
                for l in range(0, tile, 128):
                    o = coef[i, at, :] * v[:, l : l + 128]
                    tiles[i * count_n + n, at, pl.ds(l, 128)] = o.astype(BF16)
            out_copy(i, n, dst).start()
    for i, dst in enumerate((q_h, k_h)):
        for n in range(count_n):
            out_copy(i, n, dst).wait()


def finish(width, x, mat, gram):
    count_t, feats, cols = x.shape
    tokens, part = count_t * cols, mat.shape[1] // 2
    tile = 256 if part % 256 == 0 else 128
    out = jax.ShapeDtypeStruct((tokens, part), BF16)
    V, dma = pltpu.VMEM, pltpu.SemaphoreType.DMA
    return pl.pallas_call(
        functools.partial(final, width),
        out_shape=(out, out),
        in_specs=[pl.BlockSpec(memory_space=V)] * 3,
        out_specs=(pl.BlockSpec(memory_space=pl.ANY),) * 2,
        scratch_shapes=[
            V((tokens, 4 * feats), BF16), V((2, tokens, 128), F32), V((2 * part // tile, tokens, tile), BF16),
            dma((2, part // tile)),
        ],
        compiler_params=pltpu.CompilerParams(vmem_limit_bytes=24 * 2**20),
    )(x, mat, gram)


def solution(mesh):
    in_specs = (
        P("tm", "rows", None, None), P(), P(), P(), P(), P(), P(), P(), P(), P(),
        P(None, "tm"), P("tm"), P("tm"), P(None, "tm"), P("tm"), P("tm"), P(),
    )
    out_specs = (P("rows", "tm"), P("rows", "tm"))
    return jax.shard_map(per_device, mesh=mesh, in_specs=in_specs, out_specs=out_specs, check_vma=False)
```

```python
import functools

import jax
import jax.numpy as jnp
from jax import lax
from jax.experimental import pallas as pl
from jax.experimental.pallas import tpu as pltpu
from jax.sharding import PartitionSpec as P

epsilon = 1e-06
MESH = pl.DeviceIdType.MESH
F32, BF16 = jnp.float32, jnp.bfloat16


def dot(a, b, **kw):
    return jnp.dot(a, b, preferred_element_type=F32, **kw)


def split(v):
    hi = v.astype(BF16)
    return hi, (v - hi.astype(F32)).astype(BF16)


def kernel(
    count_t, count_r,
    packing_h, feat_h, gain_h, conv_h, cbias_h, lw_h, lbias_h, pw_h, pb_h, shift_h, scale_h,
    wq_h, qb_h, qg_h, wk_h, kb_h, kg_h,
    x_out, mat, gram_out,
    packing, feat, gain, conv, cbias, lw, lbias, pw, pb, shift, scale, w_all, qb, kb, qg, kg, rows_qk,
    scr, km, lhs, y_ref, snd, rcv, tot, lat_all, pwf, bounce, mod, cen, m_all, gram, gram_s, gram_r,
    lsem, csem, wsem, hs_sem, hr_sem, as_sem, ar_sem, ss_sem, sr_sem,
):
    t, r = lax.axis_index("tm"), lax.axis_index("rows")
    count = count_t * count_r
    own = t * count_r + r
    _, _, cols, chans = feat.shape
    feats, width = pw.shape
    lats = lw.shape[0]
    half = cols // 2
    part = wq_h.shape[1]
    tile = w_all.shape[2]
    count_n = part // tile
    rows_m = mod.shape[0] // 2

    early = [(feat_h, feat), (gain_h, gain), (lw_h, lw)]
    late = [
        (pw_h, pw), (pb_h, pb), (shift_h, shift), (scale_h, scale), (cbias_h, cbias), (lbias_h, lbias),
        (qb_h, qb), (kb_h, kb), (qg_h, qg), (kg_h, kg), (packing_h, packing),
    ]
    copies = [pltpu.make_async_copy(s, d, lsem.at[i]) for i, (s, d) in enumerate(early + late)]
    first, later = copies[: len(early)], copies[len(early) :]
    runs = [(0, 2), (2, 2), (4, 2), (6, 2), (8, 1)]
    taps = [
        pltpu.make_async_copy(conv_h.at[pl.ds(i, n)], conv.at[pl.ds(i, n)], csem.at[k]) for k, (i, n) in enumerate(runs)
    ]
    for c in first + taps + later:
        c.start()
    loads = [
        pltpu.make_async_copy(w.at[:, pl.ds(n * tile, tile)], w_all.at[h * count_n + n], wsem.at[(h * count_n + n) // 2])
        for h, w in enumerate((wq_h, wk_h)) for n in range(count_n)
    ]

    barrier = pltpu.get_barrier_semaphore()

    def greet(i, c):
        other = lax.rem(own + i, count)
        pl.semaphore_signal(barrier, inc=1, device_id=(other // count_r, lax.rem(other, count_r)), device_id_type=MESH)
        return c

    lax.fori_loop(1, count, greet, 0)
    nt = (((1,), (1,)), ((), ()))

    for c in first:
        c.wait()
    lwv = lw[...]
    gain_v = gain[...].reshape(1, chans)
    row_at = lax.broadcasted_iota(jnp.int32, (half, 128), 0)
    for f in range(2):
        for w in range(2):
            v = feat[f, w].astype(F32)
            sm = jnp.mean(v * v, axis=-1, keepdims=True)
            x = v * lax.rsqrt(sm + epsilon) * gain_v
            act = (x / (1.0 + jnp.exp(-x))).astype(BF16).astype(F32)
            base = (f * 2 + w) * cols
            for l in range(chans // 128):
                scr[0, l] = act[:, l * 128 : (l + 1) * 128]
                scr[1, l] = v[:, l * 128 : (l + 1) * 128]
                even, odd = scr[0, l, pl.ds(0, half, 2), :], scr[0, l, pl.ds(1, half, 2), :]
                before = jnp.where(row_at == 0, 0.0, pltpu.roll(odd, 1, 0))
                after = jnp.where(row_at == half - 1, 0.0, pltpu.roll(even, half - 1, 0))
                plain = (scr[1, l, pl.ds(0, half, 2), :], scr[1, l, pl.ds(1, half, 2), :])
                for k, (low, high) in enumerate(((before, even), (even, odd), (odd, after), plain)):
                    lhs[pl.ds(base, half), pl.ds(k * chans + l * 128, 128)] = low.astype(BF16)
                    lhs[pl.ds(base + half, half), pl.ds(k * chans + l * 128, 128)] = high.astype(BF16)

    none = jnp.zeros((lats, chans), BF16)
    pair = jnp.concatenate(
        [jnp.concatenate([lwv, none], axis=1), jnp.concatenate([none, lwv], axis=1)], axis=0
    )
    km[:, pl.ds(3 * chans, chans)] = jnp.zeros((9 * lats, chans), BF16)
    km[pl.ds(7 * lats, lats), pl.ds(3 * chans, chans)] = lwv
    started = 0
    for p, (i, n) in enumerate(runs):
        ids = range(i, i + n)
        taps[p].wait()
        more = min(len(loads), (p + 1) * -(-len(loads) // 5))
        for c in loads[started:more]:
            c.start()
        started = more
        for e in range(3):
            rhs = jnp.concatenate([conv[i, e] for i in ids], axis=1)
            left = pair if len(ids) == 2 else lwv
            folded = lax.dot_general(left, rhs, nt, preferred_element_type=F32)
            km[pl.ds(ids[0] * lats, lats * len(ids)), pl.ds(e * chans, chans)] = folded.astype(BF16)
    y_ref[...] = lax.dot_general(km[...], lhs[...], nt, preferred_element_type=F32)

    def total(d, q):
        out = None
        for f in range(2):
            for w in range(2):
                a, b = f + 2 - d, w + 1 - q
                if 0 <= a < 3 and 0 <= b < 3:
                    term = y_ref[pl.ds((a * 3 + b) * lats, lats), pl.ds((f * 2 + w) * cols, cols)]
                    out = term if out is None else out + term
        return out

    sent = [(0, -1), (1, -1), (0, 2), (1, 2), (2, 0), (2, 1), (3, 0), (3, 1), (2, -1), (3, -1), (2, 2), (3, 2)]
    for i, (d, q) in enumerate(sent):
        snd[pl.ds(i * lats, lats), :] = total(d, q)

    pl.semaphore_wait(barrier, count - 1)

    has_up, has_down = r > 0, r < count_r - 1
    has_next, has_prev = t < count_t - 1, t > 0
    plan = [
        (0, 2, t, r - 1, has_up, has_down, (1, 3)),
        (2, 2, t, r + 1, has_down, has_up, (0, 2)),
        (4, 4, t + 1, r, has_next, has_prev, (0, 1, 2, 3)),
        (8, 2, t + 1, r - 1, has_next & has_up, has_prev & has_down, (1, 3)),
        (10, 2, t + 1, r + 1, has_next & has_down, has_prev & has_up, (0, 2)),
    ]
    halo = []
    for k, (at, n, dt, dr, _, _, _) in enumerate(plan):
        rows = pl.ds(at * lats, n * lats)
        halo.append(pltpu.make_async_remote_copy(
            src_ref=snd.at[rows], dst_ref=rcv.at[rows], send_sem=hs_sem.at[k], recv_sem=hr_sem.at[k],
            device_id=(dt, dr), device_id_type=MESH,
        ))
    for copy, p in zip(halo, plan):
        pl.when(p[4])(copy.start)

    for c in later:
        c.wait()
    offset = jnp.sum(lwv.astype(F32) * cbias[...].reshape(1, chans), axis=1, keepdims=True)
    at_l = lax.broadcasted_iota(jnp.int32, (lats, lats), 0) == lax.broadcasted_iota(jnp.int32, (lats, lats), 1)
    offset = offset + jnp.sum(jnp.where(at_l, lbias[...].reshape(1, lats), 0.0), axis=1, keepdims=True)
    for i, (d, q) in enumerate(((0, 0), (0, 1), (1, 0), (1, 1))):
        tot[pl.ds(i * lats, lats), :] = total(d, q) + offset

    step = 512

    def lanes_sum(v):
        out = v[:, 0:128]
        for i in range(1, v.shape[1] // 128):
            out = out + v[:, i * 128 : (i + 1) * 128]
        return out

    total_w = jnp.zeros((feats, 128), F32)
    total_b = jnp.zeros((1, 128), F32)
    groups = feats // lats
    for c in range(0, width, step):
        for l in range(step // 128):
            bounce[l] = pw[:, c + l * 128 : c + (l + 1) * 128].astype(F32)
        mixed = jnp.concatenate([
            jnp.concatenate([bounce[l, pl.ds(k, lats, groups), :] for k in range(groups)], axis=0)
            for l in range(step // 128)
        ], axis=1)
        pwf[:, c : c + step] = mixed
        total_w = total_w + lanes_sum(mixed)
        total_b = total_b + lanes_sum(pb[pl.ds(c, step)].reshape(1, step))
    mean = jnp.sum(total_w, axis=1, keepdims=True) / width
    mean_b = jnp.sum(total_b, axis=1, keepdims=True) / width
    at16 = lax.broadcasted_iota(jnp.int32, (16, step), 0)
    for c in range(0, width, step):
        gains = 1.0 + scale[pl.ds(c, step)].reshape(1, step)
        center = pwf[:, c : c + step] - mean
        center_b = pb[pl.ds(c, step)].reshape(1, step) - mean_b
        moved = shift[pl.ds(c, step)].reshape(1, step)
        last = jnp.where(at16 == 0, center_b * gains, jnp.where(at16 == 1, moved, 0.0))
        for k, piece in enumerate(split(center * gains)):
            mod[pl.ds(k * rows_m, feats), c : c + step] = piece
        for k, piece in enumerate(split(last)):
            mod[pl.ds(k * rows_m + feats, 16), c : c + step] = piece

    def gram_of(v):
        g = lax.dot_general(v, v, nt, preferred_element_type=F32)
        return g[0:rows_m, 0:rows_m] + g[0:rows_m, rows_m:] + g[rows_m:, 0:rows_m] + g[rows_m:, rows_m:]

    lower = lax.broadcasted_iota(jnp.int32, (feats // 2, 128), 1) < feats

    def pack(v, ref):
        gram[:, 0:rows_m] = gram_of(v)
        ref[pl.ds(0, feats // 2), :] = jnp.where(
            lower, gram[0 : feats // 2, :], pltpu.roll(gram[feats // 2 : feats, :], feats, 1)
        )
        ref[pl.ds(feats // 2, 8), :] = gram[feats : feats + 8, :]

    gram[...] = jnp.zeros(gram.shape, F32)
    for h, (bias, gains) in enumerate(((qb, qg), (kb, kg))):
        for n in range(count_n):
            at = pl.ds(n * tile, tile)
            rows_qk[h * count_n + n, 0:1, :] = bias[at].reshape(1, tile)
            rows_qk[h * count_n + n, 1:2, :] = gains[at].reshape(1, tile)
    mat[pl.ds(2 * feats + 16, 2 * feats - 16), :] = jnp.zeros((2 * feats - 16, 2 * part), BF16)
    at_row = lax.broadcasted_iota(jnp.int32, (rows_m, tile), 0)
    at_last = lax.broadcasted_iota(jnp.int32, (16, tile), 0)

    def project(g):
        to = pl.ds(pl.multiple_of(g * tile, tile), tile)
        v = dot(mod[...], w_all[g])
        v = v[0:rows_m] + v[rows_m:] + jnp.where(at_row == feats + 1, rows_qk[g, 0:1, :], 0.0)
        for k, piece in enumerate(split(v)):
            m_all[pl.ds(k * rows_m, rows_m), to] = piece
        v = v * rows_qk[g, 1:2, :]
        for k, piece in enumerate(split(v[0:feats])):
            mat[pl.ds(k * feats, feats), to] = piece
        m, c = v[feats : feats + 1], v[feats + 1 : feats + 2]
        m_hi, c_hi = m.astype(BF16).astype(F32), c.astype(BF16).astype(F32)
        last = jnp.where(at_last % 2 == 0, c_hi, c - c_hi)
        last = jnp.where(at_last == 0, m_hi, jnp.where(at_last == 1, m - m_hi, last))
        mat[pl.ds(2 * feats, 16), to] = jnp.where(at_last < 8, last, 0.0).astype(BF16)

    def both(p, carry):
        pair_at = w_all.at[pl.ds(2 * p, 2)]
        pltpu.make_async_copy(pair_at, pair_at, wsem.at[p]).wait()
        for g in (2 * p, 2 * p + 1):
            project(g)
        return carry

    def share(h):
        pack(m_all[:, pl.ds(h * part, part)], gram_s.at[h])
        out = [
            pltpu.make_async_remote_copy(
                src_ref=gram_s.at[h], dst_ref=gram_r.at[h, i - 1], send_sem=ss_sem.at[h],
                recv_sem=sr_sem.at[h], device_id=(lax.rem(t + i, count_t), r), device_id_type=MESH,
            )
            for i in range(1, count_t)
        ]
        for c in out:
            c.start()
        return pltpu.make_async_remote_copy(
            src_ref=gram_r.at[h], dst_ref=gram_r.at[h], send_sem=ss_sem.at[h], recv_sem=sr_sem.at[h],
            device_id=(t, r), device_id_type=MESH,
        )

    middle = -(-count_n // 2)
    ahead = min(1, middle)
    lax.fori_loop(0, ahead, both, 0)
    for copy, p in zip(halo, plan):
        def take(copy=copy, p=p):
            copy.wait_recv()
            for k, i in enumerate(p[6]):
                tot[pl.ds(i * lats, lats), :] += rcv[pl.ds((p[0] + k) * lats, lats), :]
        pl.when(p[5])(take)

    lane = lax.broadcasted_iota(jnp.int32, (lats, cols), 1)
    for q in range(2):
        f0, f1 = tot[pl.ds(q * lats, lats), :], tot[pl.ds((2 + q) * lats, lats), :]
        lat_all[own, pl.ds(2 * q * lats, lats), :] = jnp.where(lane < half, f0, pltpu.roll(f1, half, 1)).astype(BF16)
        lat_all[own, pl.ds((2 * q + 1) * lats, lats), :] = jnp.where(lane < half, pltpu.roll(f0, half, 1), f1).astype(BF16)

    inner = 1
    while inner * inner * 4 <= count_r and count_r % (inner * 2) == 0:
        inner *= 2
    outer = count_r // inner
    flat = count_t // 2 * inner
    group, away = outer * flat, (outer - 1) * flat
    side = lax.rem(t, 2)
    mate = t + 1 - 2 * side
    far, spot = r // inner, t // 2 * inner + lax.rem(r, inner)
    flip = lax.min(far // max(outer // 2, 1), 1)
    mirror = far + flip * (outer - 1 - 2 * far)

    def place(i):
        v = outer - 1 - i // flat
        v = v - lax.max(0, lax.min(1, mirror - v + 1))
        v = v + lax.max(0, i // flat - outer + 2) * (mirror - v)
        p = lax.rem(spot + lax.rem(i, flat), flat)
        return p // inner * 2, (v + flip * (outer - 1 - 2 * v)) * inner + lax.rem(p, inner)

    def ident_of(i, s):
        pt, pr = place(i)
        return (pt + s) * count_r + pr

    def send(at, dt, dr, sent, got):
        return pltpu.make_async_remote_copy(
            src_ref=lat_all.at[at], dst_ref=lat_all.at[at], send_sem=as_sem.at[sent], recv_sem=ar_sem.at[got],
            device_id=(dt, dr), device_id_type=MESH,
        )

    def spread(i):
        pt, pr = place(i)
        return send(own, pt + side, pr, 0, far)

    def to_mate(i):
        return send(ident_of(i, side), mate, r, 1, outer)

    def all_of(n, sent, got):
        return send(pl.ds(0, n), mate, r, sent, got)

    def loop(first, last, body):
        lax.fori_loop(first, last, lambda i, c: (body(i), c)[1], 0)

    to_mate(away).start()
    loop(0, away, lambda i: spread(i).start())
    loop(away + 1, group, lambda i: spread(i).start())

    def relay(j, first):
        _, pr = place(j * flat)
        all_of(flat - first, 0, pr // inner).wait_recv()
        loop(j * flat + first, (j + 1) * flat, lambda i: to_mate(i).start())

    lax.fori_loop(ahead, middle, both, 0)
    shares = [share(0)]
    lax.fori_loop(middle, count_n, both, 0)
    shares.append(share(1))
    for c in range(0, width, step):
        center_b = jnp.where(at16 == 0, pb[pl.ds(c, step)].reshape(1, step) - mean_b, 0.0)
        for k, piece in enumerate(split(pwf[:, c : c + step] - mean)):
            cen[pl.ds(k * rows_m, feats), c : c + step] = piece
        for k, piece in enumerate(split(center_b)):
            cen[pl.ds(k * rows_m + feats, 16), c : c + step] = piece
    pack(cen[...], gram_out.at[0])

    relay(outer - 1, 1)
    for j in range(outer - 2, -1, -1):
        relay(j, 0)
    all_of(group, 1, outer).wait_recv()

    for h in range(2):
        gram_out[1 + h] = gram_s[h]
        shares[h].wait_recv()
        for i in range(count_t - 1):
            gram_out[1 + h] += gram_r[h, i]

    def pick(j, carry):
        x_out[j] = lat_all[packing[r * count_t + j]]
        return carry

    lax.fori_loop(0, count_t, pick, 0)

    for copy, p in zip(halo, plan):
        pl.when(p[4])(copy.wait_send)
    all_of(group - 1, 0, outer).wait_send()
    all_of(group, 1, outer).wait_send()
    for c in shares:
        c.wait_send()


def per_device(
    features, block_gain, conv_weight, conv_bias, latent_weight, latent_bias, patch_weight, patch_bias,
    shift_mod, scale_mod, query_weight, query_bias, query_gain, key_weight, key_bias, key_gain, packing,
):
    count_t, count_r = lax.axis_size("tm"), lax.axis_size("rows")
    count = count_t * count_r
    _, _, cols, chans = features.shape
    feats, width = patch_weight.shape
    lats = latent_weight.shape[1]
    part = query_weight.shape[1]
    tile = 256 if part % 256 == 0 else 128
    V = pltpu.VMEM
    rows_m = feats + 16
    operands = (
        packing, features, block_gain, conv_weight.reshape(9, 3, chans, chans), conv_bias, latent_weight.T, latent_bias, patch_weight, patch_bias,
        shift_mod, scale_mod, query_weight, query_bias, query_gain, key_weight, key_bias, key_gain,
    )
    like = lambda a: V(a.shape, a.dtype)
    scratch = [pltpu.SMEM(packing.shape, packing.dtype)] + [like(a) for a in operands[1:11]]
    scratch += [
        V((2 * part // tile, width, tile), BF16),
        V((part,), F32),
        V((part,), F32),
        V((part,), F32),
        V((part,), F32),
        V((2 * part // tile, 8, tile), F32),
        V((2, chans // 128, cols, 128), F32),
        V((9 * lats, 4 * chans), BF16),
        V((4 * cols, 4 * chans), BF16),
        V((9 * lats, 4 * cols), F32),
        V((12 * lats, cols), F32),
        V((12 * lats, cols), F32),
        V((4 * lats, cols), F32),
        V((count, feats, cols), BF16),
        V((feats, width), F32),
        V((4, feats, 128), F32),
        V((2 * rows_m, width), BF16),
        V((2 * rows_m, width), BF16),
        V((2 * rows_m, 2 * part), BF16),
        V((rows_m, 128), F32),
        V((2, feats // 2 + 8, 128), F32),
        V((2, count_t - 1, feats // 2 + 8, 128), F32),
    ]
    dma = pltpu.SemaphoreType.DMA
    scratch += [
        dma((14,)), dma((5,)), dma((part // tile,)), dma((5,)), dma((5,)), dma((2,)), dma((count_r + 1,)), dma((2,)), dma((2,)),
    ]
    outs = (
        jax.ShapeDtypeStruct((count_t, feats, cols), BF16),
        jax.ShapeDtypeStruct((4 * feats, 2 * part), BF16),
        jax.ShapeDtypeStruct((3, feats // 2 + 8, 128), F32),
    )
    x, mat, gram = pl.pallas_call(
        functools.partial(kernel, count_t, count_r),
        out_shape=outs,
        in_specs=[pl.BlockSpec(memory_space=pltpu.HBM)] * 17,
        out_specs=(pl.BlockSpec(memory_space=V),) * 3,
        scratch_shapes=scratch,
        compiler_params=pltpu.CompilerParams(collective_id=0, has_side_effects=True, vmem_limit_bytes=52 * 2**20),
    )(*[pltpu.with_memory_space_constraint(a, pltpu.HBM) for a in operands])
    return finish(width, x, mat, gram)


def final(width, x_ref, mat, gram, q_h, k_h, left, coef, tiles, osem):
    count_t, feats, cols = x_ref.shape
    part = mat.shape[1] // 2
    tokens = left.shape[0]
    tile = tiles.shape[2]
    lane = lax.broadcasted_iota(jnp.int32, (1, 128), 1)
    hf = feats // 2
    quads, ends = [], []
    for h in range(3):
        top, tail = gram[h, 0:hf, :], gram[h, hf : hf + 8, :]
        square = jnp.where(lane < feats, jnp.concatenate([top, pltpu.roll(top, feats, 1)], axis=0), 0.0)
        quads.append(square)
        ends.append(jnp.where(lane < feats, tail, 0.0))

    def entry(h, row, at):
        return jnp.sum(jnp.where(lane == at, gram[h, hf + row : hf + row + 1, :], 0.0), axis=1, keepdims=True)

    hi, lo = split(jnp.concatenate(quads + ends, axis=0))
    lo_at = pltpu.roll(lo.astype(F32), feats, 1).astype(BF16)
    stacked = hi + lo_at
    at16 = lax.broadcasted_iota(jnp.int32, (16, cols), 0)
    for j in range(count_t):
        x = x_ref[j]
        prod = dot(stacked, jnp.concatenate([x, x], axis=0))
        x = x.astype(F32)
        line = lambda h, row: prod[3 * feats + 8 * h + row : 3 * feats + 8 * h + row + 1, :]
        square = lambda h: jnp.sum(x * prod[h * feats : (h + 1) * feats, :], axis=0, keepdims=True)
        var = (square(0) + 2.0 * line(0, 0) + entry(0, 0, feats)) / width + epsilon
        inv = lax.rsqrt(var)
        sigma = var * inv
        high = sigma.astype(BF16).astype(F32)
        mid = (sigma - high).astype(BF16).astype(F32)
        more = jnp.where(at16 < 4, high, jnp.where(at16 < 6, mid, sigma - high - mid))
        more = jnp.where(at16 < 2, 1.0, jnp.where(at16 < 8, more, 0.0))
        at = pl.ds(j * cols, cols)
        rest = jnp.zeros((2 * feats - 16, cols), F32)
        left[at, :] = jnp.concatenate([x, x, more, rest], axis=0).T.astype(BF16)
        for h in range(1, 3):
            ss = inv * inv * (square(h) + 2.0 * line(h, 0) + entry(h, 0, feats))
            ss = ss + 2.0 * inv * (line(h, 1) + entry(h, 0, feats + 1)) + entry(h, 1, feats + 1)
            coef[h - 1, at, :] = jnp.broadcast_to(lax.rsqrt(ss / width + epsilon) * inv, (128, cols)).T
    count_n = part // tile

    def out_copy(i, n, dst):
        return pltpu.make_async_copy(tiles.at[i * count_n + n], dst.at[:, pl.ds(n * tile, tile)], osem.at[i, n])

    for i, dst in enumerate((q_h, k_h)):
        for n in range(count_n):
            for c in range(0, tokens, 256):
                at = pl.ds(c, 256)
                v = dot(left[at, :], mat[:, pl.ds(i * part + n * tile, tile)])
                for l in range(0, tile, 128):
                    o = coef[i, at, :] * v[:, l : l + 128]
                    tiles[i * count_n + n, at, pl.ds(l, 128)] = o.astype(BF16)
            out_copy(i, n, dst).start()
    for i, dst in enumerate((q_h, k_h)):
        for n in range(count_n):
            out_copy(i, n, dst).wait()


def finish(width, x, mat, gram):
    count_t, feats, cols = x.shape
    tokens, part = count_t * cols, mat.shape[1] // 2
    tile = 256 if part % 256 == 0 else 128
    out = jax.ShapeDtypeStruct((tokens, part), BF16)
    V, dma = pltpu.VMEM, pltpu.SemaphoreType.DMA
    return pl.pallas_call(
        functools.partial(final, width),
        out_shape=(out, out),
        in_specs=[pl.BlockSpec(memory_space=V)] * 3,
        out_specs=(pl.BlockSpec(memory_space=pl.ANY),) * 2,
        scratch_shapes=[
            V((tokens, 4 * feats), BF16), V((2, tokens, 128), F32), V((2 * part // tile, tokens, tile), BF16),
            dma((2, part // tile)),
        ],
        compiler_params=pltpu.CompilerParams(vmem_limit_bytes=24 * 2**20),
    )(x, mat, gram)


def solution(mesh):
    in_specs = (
        P("tm", "rows", None, None), P(), P(), P(), P(), P(), P(), P(), P(), P(),
        P(None, "tm"), P("tm"), P("tm"), P(None, "tm"), P("tm"), P("tm"), P(),
    )
    out_specs = (P("rows", "tm"), P("rows", "tm"))
    return jax.shard_map(per_device, mesh=mesh, in_specs=in_specs, out_specs=out_specs, check_vma=False)
```

```python
import functools

import jax
import jax.numpy as jnp
from jax import lax
from jax.experimental import pallas as pl
from jax.experimental.pallas import tpu as pltpu
from jax.sharding import PartitionSpec as P

epsilon = 1e-06
MESH = pl.DeviceIdType.MESH
F32, BF16 = jnp.float32, jnp.bfloat16


def dot(a, b, **kw):
    return jnp.dot(a, b, preferred_element_type=F32, **kw)


def split(v):
    hi = v.astype(BF16)
    return hi, (v - hi.astype(F32)).astype(BF16)


def kernel(
    count_t, count_r,
    packing_h, feat_h, gain_h, conv_h, cbias_h, lw_h, lbias_h, pw_h, pb_h, shift_h, scale_h,
    wq_h, qb_h, qg_h, wk_h, kb_h, kg_h,
    left, coef, mat,
    packing, feat, gain, conv, cbias, lw, lbias, pw, pb, shift, scale, w_all, qb, kb, qg, kg, rows_qk,
    scr, km, lhs, y_ref, snd, rcv, tot, lat_all, pwf, bounce, mod, cen, m_all, gram, gram_out, gram_s, gram_r,
    lsem, csem, wsem, hs_sem, hr_sem, as_sem, ar_sem, ss_sem, sr_sem,
):
    t, r = lax.axis_index("tm"), lax.axis_index("rows")
    count = count_t * count_r
    own = t * count_r + r
    _, _, cols, chans = feat.shape
    feats, width = pw.shape
    lats = lw.shape[0]
    half = cols // 2
    part = wq_h.shape[1]
    tile = w_all.shape[2]
    count_n = part // tile
    rows_m = mod.shape[0] // 2

    early = [(feat_h, feat), (gain_h, gain), (lw_h, lw)]
    late = [
        (pw_h, pw), (pb_h, pb), (shift_h, shift), (scale_h, scale), (cbias_h, cbias), (lbias_h, lbias),
        (qb_h, qb), (kb_h, kb), (qg_h, qg), (kg_h, kg), (packing_h, packing),
    ]
    copies = [pltpu.make_async_copy(s, d, lsem.at[i]) for i, (s, d) in enumerate(early + late)]
    first, later = copies[: len(early)], copies[len(early) :]
    runs = [(0, 2), (2, 2), (4, 2), (6, 2), (8, 1)]
    taps = [
        pltpu.make_async_copy(conv_h.at[pl.ds(i, n)], conv.at[pl.ds(i, n)], csem.at[k]) for k, (i, n) in enumerate(runs)
    ]
    for c in first + taps + later:
        c.start()
    loads = [
        pltpu.make_async_copy(w.at[:, pl.ds(n * tile, tile)], w_all.at[h * count_n + n], wsem.at[(h * count_n + n) // 2])
        for h, w in enumerate((wq_h, wk_h)) for n in range(count_n)
    ]

    barrier = pltpu.get_barrier_semaphore()

    def greet(i, c):
        other = lax.rem(own + i, count)
        pl.semaphore_signal(barrier, inc=1, device_id=(other // count_r, lax.rem(other, count_r)), device_id_type=MESH)
        return c

    lax.fori_loop(1, count, greet, 0)
    nt = (((1,), (1,)), ((), ()))

    for c in first:
        c.wait()
    lwv = lw[...]
    gain_v = gain[...].reshape(1, chans)
    row_at = lax.broadcasted_iota(jnp.int32, (half, 128), 0)
    for f in range(2):
        for w in range(2):
            v = feat[f, w].astype(F32)
            sm = jnp.mean(v * v, axis=-1, keepdims=True)
            x = v * lax.rsqrt(sm + epsilon) * gain_v
            act = (x / (1.0 + jnp.exp(-x))).astype(BF16).astype(F32)
            base = (f * 2 + w) * cols
            for l in range(chans // 128):
                scr[0, l] = act[:, l * 128 : (l + 1) * 128]
                scr[1, l] = v[:, l * 128 : (l + 1) * 128]
                even, odd = scr[0, l, pl.ds(0, half, 2), :], scr[0, l, pl.ds(1, half, 2), :]
                before = jnp.where(row_at == 0, 0.0, pltpu.roll(odd, 1, 0))
                after = jnp.where(row_at == half - 1, 0.0, pltpu.roll(even, half - 1, 0))
                plain = (scr[1, l, pl.ds(0, half, 2), :], scr[1, l, pl.ds(1, half, 2), :])
                for k, (low, high) in enumerate(((before, even), (even, odd), (odd, after), plain)):
                    lhs[pl.ds(base, half), pl.ds(k * chans + l * 128, 128)] = low.astype(BF16)
                    lhs[pl.ds(base + half, half), pl.ds(k * chans + l * 128, 128)] = high.astype(BF16)

    none = jnp.zeros((lats, chans), BF16)
    pair = jnp.concatenate(
        [jnp.concatenate([lwv, none], axis=1), jnp.concatenate([none, lwv], axis=1)], axis=0
    )
    km[:, pl.ds(3 * chans, chans)] = jnp.zeros((9 * lats, chans), BF16)
    km[pl.ds(7 * lats, lats), pl.ds(3 * chans, chans)] = lwv
    started = 0
    for p, (i, n) in enumerate(runs):
        ids = range(i, i + n)
        taps[p].wait()
        more = min(len(loads), (p + 1) * -(-len(loads) // 5))
        for c in loads[started:more]:
            c.start()
        started = more
        for e in range(3):
            rhs = jnp.concatenate([conv[i, e] for i in ids], axis=1)
            folded = lax.dot_general(pair if n == 2 else lwv, rhs, nt, preferred_element_type=F32)
            km[pl.ds(ids[0] * lats, lats * len(ids)), pl.ds(e * chans, chans)] = folded.astype(BF16)
    y_ref[...] = lax.dot_general(km[...], lhs[...], nt, preferred_element_type=F32)

    def total(d, q):
        out = None
        for f in range(2):
            for w in range(2):
                a, b = f + 2 - d, w + 1 - q
                if 0 <= a < 3 and 0 <= b < 3:
                    term = y_ref[pl.ds((a * 3 + b) * lats, lats), pl.ds((f * 2 + w) * cols, cols)]
                    out = term if out is None else out + term
        return out

    sent = [(0, -1), (1, -1), (0, 2), (1, 2), (2, 0), (2, 1), (3, 0), (3, 1), (2, -1), (3, -1), (2, 2), (3, 2)]
    for i, (d, q) in enumerate(sent):
        snd[pl.ds(i * lats, lats), :] = total(d, q)

    pl.semaphore_wait(barrier, count - 1)

    has_up, has_down = r > 0, r < count_r - 1
    has_next, has_prev = t < count_t - 1, t > 0
    plan = [
        (0, 2, t, r - 1, has_up, has_down, (1, 3)),
        (2, 2, t, r + 1, has_down, has_up, (0, 2)),
        (4, 4, t + 1, r, has_next, has_prev, (0, 1, 2, 3)),
        (8, 2, t + 1, r - 1, has_next & has_up, has_prev & has_down, (1, 3)),
        (10, 2, t + 1, r + 1, has_next & has_down, has_prev & has_up, (0, 2)),
    ]
    halo = []
    for k, (at, n, dt, dr, _, _, _) in enumerate(plan):
        rows = pl.ds(at * lats, n * lats)
        halo.append(pltpu.make_async_remote_copy(
            src_ref=snd.at[rows], dst_ref=rcv.at[rows], send_sem=hs_sem.at[k], recv_sem=hr_sem.at[k],
            device_id=(dt, dr), device_id_type=MESH,
        ))
    for copy, p in zip(halo, plan):
        pl.when(p[4])(copy.start)

    for c in later:
        c.wait()
    offset = jnp.sum(lwv.astype(F32) * cbias[...].reshape(1, chans), axis=1, keepdims=True)
    at_l = lax.broadcasted_iota(jnp.int32, (lats, lats), 0) == lax.broadcasted_iota(jnp.int32, (lats, lats), 1)
    offset = offset + jnp.sum(jnp.where(at_l, lbias[...].reshape(1, lats), 0.0), axis=1, keepdims=True)
    for i, (d, q) in enumerate(((0, 0), (0, 1), (1, 0), (1, 1))):
        tot[pl.ds(i * lats, lats), :] = total(d, q) + offset

    step = 512

    def lanes_sum(v):
        out = v[:, 0:128]
        for i in range(1, v.shape[1] // 128):
            out = out + v[:, i * 128 : (i + 1) * 128]
        return out

    total_w = jnp.zeros((feats, 128), F32)
    total_b = jnp.zeros((1, 128), F32)
    groups = feats // lats
    for c in range(0, width, step):
        for l in range(step // 128):
            bounce[l] = pw[:, c + l * 128 : c + (l + 1) * 128].astype(F32)
        mixed = jnp.concatenate([
            jnp.concatenate([bounce[l, pl.ds(k, lats, groups), :] for k in range(groups)], axis=0)
            for l in range(step // 128)
        ], axis=1)
        pwf[:, c : c + step] = mixed
        total_w = total_w + lanes_sum(mixed)
        total_b = total_b + lanes_sum(pb[pl.ds(c, step)].reshape(1, step))
    mean = jnp.sum(total_w, axis=1, keepdims=True) / width
    mean_b = jnp.sum(total_b, axis=1, keepdims=True) / width
    at16 = lax.broadcasted_iota(jnp.int32, (16, step), 0)
    for c in range(0, width, step):
        gains = 1.0 + scale[pl.ds(c, step)].reshape(1, step)
        center = pwf[:, c : c + step] - mean
        center_b = pb[pl.ds(c, step)].reshape(1, step) - mean_b
        moved = shift[pl.ds(c, step)].reshape(1, step)
        last = jnp.where(at16 == 0, center_b * gains, jnp.where(at16 == 1, moved, 0.0))
        for k, piece in enumerate(split(center * gains)):
            mod[pl.ds(k * rows_m, feats), c : c + step] = piece
        for k, piece in enumerate(split(last)):
            mod[pl.ds(k * rows_m + feats, 16), c : c + step] = piece

    def gram_of(v):
        g = lax.dot_general(v, v, nt, preferred_element_type=F32)
        return g[0:rows_m, 0:rows_m] + g[0:rows_m, rows_m:] + g[rows_m:, 0:rows_m] + g[rows_m:, rows_m:]

    lower = lax.broadcasted_iota(jnp.int32, (feats // 2, 128), 1) < feats

    def pack(v, ref):
        gram[:, 0:rows_m] = gram_of(v)
        ref[pl.ds(0, feats // 2), :] = jnp.where(
            lower, gram[0 : feats // 2, :], pltpu.roll(gram[feats // 2 : feats, :], feats, 1)
        )
        ref[pl.ds(feats // 2, 8), :] = gram[feats : feats + 8, :]

    gram[...] = jnp.zeros(gram.shape, F32)
    for h, (bias, gains) in enumerate(((qb, qg), (kb, kg))):
        for n in range(count_n):
            at = pl.ds(n * tile, tile)
            rows_qk[h * count_n + n, 0:1, :] = bias[at].reshape(1, tile)
            rows_qk[h * count_n + n, 1:2, :] = gains[at].reshape(1, tile)
    mat[pl.ds(2 * feats + 16, 2 * feats - 16), :] = jnp.zeros((2 * feats - 16, 2 * part), BF16)
    at_row = lax.broadcasted_iota(jnp.int32, (rows_m, tile), 0)
    at_last = lax.broadcasted_iota(jnp.int32, (16, tile), 0)

    def project(g):
        to = pl.ds(pl.multiple_of(g * tile, tile), tile)
        v = dot(mod[...], w_all[g])
        v = v[0:rows_m] + v[rows_m:] + jnp.where(at_row == feats + 1, rows_qk[g, 0:1, :], 0.0)
        for k, piece in enumerate(split(v)):
            m_all[pl.ds(k * rows_m, rows_m), to] = piece
        v = v * rows_qk[g, 1:2, :]
        for k, piece in enumerate(split(v[0:feats])):
            mat[pl.ds(k * feats, feats), to] = piece
        m, c = v[feats : feats + 1], v[feats + 1 : feats + 2]
        m_hi, c_hi = m.astype(BF16).astype(F32), c.astype(BF16).astype(F32)
        last = jnp.where(at_last % 2 == 0, c_hi, c - c_hi)
        last = jnp.where(at_last == 0, m_hi, jnp.where(at_last == 1, m - m_hi, last))
        mat[pl.ds(2 * feats, 16), to] = jnp.where(at_last < 8, last, 0.0).astype(BF16)

    def both(p, carry):
        pair_at = w_all.at[pl.ds(2 * p, 2)]
        pltpu.make_async_copy(pair_at, pair_at, wsem.at[p]).wait()
        for g in (2 * p, 2 * p + 1):
            project(g)
        return carry

    def share(h):
        pack(m_all[:, pl.ds(h * part, part)], gram_s.at[h])
        out = [
            pltpu.make_async_remote_copy(
                src_ref=gram_s.at[h], dst_ref=gram_r.at[h, i - 1], send_sem=ss_sem.at[h],
                recv_sem=sr_sem.at[h], device_id=(lax.rem(t + i, count_t), r), device_id_type=MESH,
            )
            for i in range(1, count_t)
        ]
        for c in out:
            c.start()
        return pltpu.make_async_remote_copy(
            src_ref=gram_r.at[h], dst_ref=gram_r.at[h], send_sem=ss_sem.at[h], recv_sem=sr_sem.at[h],
            device_id=(t, r), device_id_type=MESH,
        )

    middle = -(-count_n // 2)
    ahead = min(2, middle)
    lax.fori_loop(0, ahead, both, 0)
    for copy, p in zip(halo, plan):
        def take(copy=copy, p=p):
            copy.wait_recv()
            for k, i in enumerate(p[6]):
                tot[pl.ds(i * lats, lats), :] += rcv[pl.ds((p[0] + k) * lats, lats), :]
        pl.when(p[5])(take)

    lane = lax.broadcasted_iota(jnp.int32, (lats, cols), 1)
    for q in range(2):
        f0, f1 = tot[pl.ds(q * lats, lats), :], tot[pl.ds((2 + q) * lats, lats), :]
        lat_all[own, pl.ds(2 * q * lats, lats), :] = jnp.where(lane < half, f0, pltpu.roll(f1, half, 1)).astype(BF16)
        lat_all[own, pl.ds((2 * q + 1) * lats, lats), :] = jnp.where(lane < half, pltpu.roll(f0, half, 1), f1).astype(BF16)

    inner = 1
    while inner * inner * 4 <= count_r and count_r % (inner * 2) == 0:
        inner *= 2
    outer = count_r // inner
    flat = count_t // 2 * inner
    group, away = outer * flat, (outer - 1) * flat
    side = lax.rem(t, 2)
    mate = t + 1 - 2 * side
    far, near, chip, chips = r // inner, lax.rem(r, inner), t // 2, count_t // 2
    flip = lax.min(far // max(outer // 2, 1), 1)
    mirror = far + flip * (outer - 1 - 2 * far)

    def place(i):
        v = outer - 1 - i // flat
        v = v - lax.max(0, lax.min(1, mirror - v + 1))
        v = v + lax.max(0, i // flat - outer + 2) * (mirror - v)
        k = flat - 1 - lax.rem(i, flat)
        other = lax.rem(chip + k // inner, chips)
        return other * 2, (v + flip * (outer - 1 - 2 * v)) * inner + lax.rem(near + lax.rem(k, inner), inner)

    def ident_of(i, s):
        pt, pr = place(i)
        return (pt + s) * count_r + pr

    def send(at, dt, dr, sent, got):
        return pltpu.make_async_remote_copy(
            src_ref=lat_all.at[at], dst_ref=lat_all.at[at], send_sem=as_sem.at[sent], recv_sem=ar_sem.at[got],
            device_id=(dt, dr), device_id_type=MESH,
        )

    def spread(i):
        pt, pr = place(i)
        return send(own, pt + side, pr, 0, far)

    def to_mate(i):
        return send(ident_of(i, side), mate, r, 1, outer)

    def all_of(n, sent, got):
        return send(pl.ds(0, n), mate, r, sent, got)

    def loop(first, last, body):
        lax.fori_loop(first, last, lambda i, c: (body(i), c)[1], 0)

    to_mate(group - 1).start()
    loop(0, away, lambda i: spread(i).start())
    loop(away, group - 1, lambda i: spread(i).start())

    def relay(j, skip):
        _, pr = place(j * flat)
        all_of(flat - skip, 0, pr // inner).wait_recv()
        loop(j * flat, (j + 1) * flat - skip, lambda i: to_mate(i).start())

    lax.fori_loop(ahead, middle, both, 0)
    shares = [share(0)]
    lax.fori_loop(middle, count_n, both, 0)
    shares.append(share(1))
    for c in range(0, width, step):
        center_b = jnp.where(at16 == 0, pb[pl.ds(c, step)].reshape(1, step) - mean_b, 0.0)
        for k, piece in enumerate(split(pwf[:, c : c + step] - mean)):
            cen[pl.ds(k * rows_m, feats), c : c + step] = piece
        for k, piece in enumerate(split(center_b)):
            cen[pl.ds(k * rows_m + feats, 16), c : c + step] = piece
    pack(cen[...], gram_out.at[0])

    relay(outer - 1, 1)
    for j in range(outer - 2, -1, -1):
        relay(j, 0)
    all_of(group, 1, outer).wait_recv()

    for h in range(2):
        gram_out[1 + h] = gram_s[h]
        shares[h].wait_recv()
        for i in range(count_t - 1):
            gram_out[1 + h] += gram_r[h, i]

    lane1 = lax.broadcasted_iota(jnp.int32, (1, 128), 1)
    hf = feats // 2
    quads, ends = [], []
    for h in range(3):
        top, tail = gram_out[h, 0:hf, :], gram_out[h, hf : hf + 8, :]
        square = jnp.where(lane1 < feats, jnp.concatenate([top, pltpu.roll(top, feats, 1)], axis=0), 0.0)
        quads.append(square)
        ends.append(jnp.where(lane1 < feats, tail, 0.0))

    def entry(h, row, at):
        return jnp.sum(jnp.where(lane1 == at, gram_out[h, hf + row : hf + row + 1, :], 0.0), axis=1, keepdims=True)

    hi, lo = split(jnp.concatenate(quads + ends, axis=0))
    lo_at = pltpu.roll(lo.astype(F32), feats, 1).astype(BF16)
    stacked = hi + lo_at
    at16 = lax.broadcasted_iota(jnp.int32, (16, cols), 0)
    for j in range(count_t):
        x = lat_all[packing[r * count_t + j]]
        prod = dot(stacked, jnp.concatenate([x, x], axis=0))
        x = x.astype(F32)
        line = lambda h, row: prod[3 * feats + 8 * h + row : 3 * feats + 8 * h + row + 1, :]
        square = lambda h: jnp.sum(x * prod[h * feats : (h + 1) * feats, :], axis=0, keepdims=True)
        var = (square(0) + 2.0 * line(0, 0) + entry(0, 0, feats)) / width + epsilon
        inv = lax.rsqrt(var)
        sigma = var * inv
        high = sigma.astype(BF16).astype(F32)
        mid = (sigma - high).astype(BF16).astype(F32)
        more = jnp.where(at16 < 4, high, jnp.where(at16 < 6, mid, sigma - high - mid))
        more = jnp.where(at16 < 2, 1.0, jnp.where(at16 < 8, more, 0.0))
        at = pl.ds(j * cols, cols)
        rest = jnp.zeros((2 * feats - 16, cols), F32)
        left[at, :] = jnp.concatenate([x, x, more, rest], axis=0).T.astype(BF16)
        for h in range(1, 3):
            ss = inv * inv * (square(h) + 2.0 * line(h, 0) + entry(h, 0, feats))
            ss = ss + 2.0 * inv * (line(h, 1) + entry(h, 0, feats + 1)) + entry(h, 1, feats + 1)
            coef[h - 1, at, :] = jnp.broadcast_to(lax.rsqrt(ss / width + epsilon) * inv, (128, cols)).T

    for copy, p in zip(halo, plan):
        pl.when(p[4])(copy.wait_send)
    all_of(group - 1, 0, outer).wait_send()
    all_of(group, 1, outer).wait_send()
    for c in shares:
        c.wait_send()


def per_device(
    features, block_gain, conv_weight, conv_bias, latent_weight, latent_bias, patch_weight, patch_bias,
    shift_mod, scale_mod, query_weight, query_bias, query_gain, key_weight, key_bias, key_gain, packing,
):
    count_t, count_r = lax.axis_size("tm"), lax.axis_size("rows")
    count = count_t * count_r
    _, _, cols, chans = features.shape
    feats, width = patch_weight.shape
    lats = latent_weight.shape[1]
    part = query_weight.shape[1]
    tile = 256 if part % 256 == 0 else 128
    V = pltpu.VMEM
    rows_m = feats + 16
    operands = (
        packing, features, block_gain, conv_weight.reshape(9, 3, chans, chans), conv_bias, latent_weight.T, latent_bias, patch_weight, patch_bias,
        shift_mod, scale_mod, query_weight, query_bias, query_gain, key_weight, key_bias, key_gain,
    )
    like = lambda a: V(a.shape, a.dtype)
    scratch = [pltpu.SMEM(packing.shape, packing.dtype)] + [like(a) for a in operands[1:11]]
    scratch += [
        V((2 * part // tile, width, tile), BF16),
        V((part,), F32),
        V((part,), F32),
        V((part,), F32),
        V((part,), F32),
        V((2 * part // tile, 8, tile), F32),
        V((2, chans // 128, cols, 128), F32),
        V((9 * lats, 4 * chans), BF16),
        V((4 * cols, 4 * chans), BF16),
        V((9 * lats, 4 * cols), F32),
        V((12 * lats, cols), F32),
        V((12 * lats, cols), F32),
        V((4 * lats, cols), F32),
        V((count, feats, cols), BF16),
        V((feats, width), F32),
        V((4, feats, 128), F32),
        V((2 * rows_m, width), BF16),
        V((2 * rows_m, width), BF16),
        V((2 * rows_m, 2 * part), BF16),
        V((rows_m, 128), F32),
        V((3, feats // 2 + 8, 128), F32),
        V((2, feats // 2 + 8, 128), F32),
        V((2, count_t - 1, feats // 2 + 8, 128), F32),
    ]
    dma = pltpu.SemaphoreType.DMA
    scratch += [
        dma((14,)), dma((5,)), dma((part // tile,)), dma((5,)), dma((5,)), dma((2,)), dma((count_r + 1,)), dma((2,)), dma((2,)),
    ]
    outs = (
        jax.ShapeDtypeStruct((count_t * cols, 4 * feats), BF16),
        jax.ShapeDtypeStruct((2, count_t * cols, 128), F32),
        jax.ShapeDtypeStruct((4 * feats, 2 * part), BF16),
    )
    left, coef, mat = pl.pallas_call(
        functools.partial(kernel, count_t, count_r),
        out_shape=outs,
        in_specs=[pl.BlockSpec(memory_space=pltpu.HBM)] * 17,
        out_specs=(pl.BlockSpec(memory_space=V),) * 3,
        scratch_shapes=scratch,
        compiler_params=pltpu.CompilerParams(collective_id=0, has_side_effects=True, vmem_limit_bytes=47 * 2**20),
    )(*[pltpu.with_memory_space_constraint(a, pltpu.HBM) for a in operands])
    return finish(left, coef, mat)


def final(left, coef, mat, q_h, k_h, tiles, osem):
    part = mat.shape[1] // 2
    tokens = left.shape[0]
    tile = tiles.shape[2]
    count_n = part // tile

    def out_copy(i, n, dst):
        return pltpu.make_async_copy(tiles.at[i * count_n + n], dst.at[:, pl.ds(n * tile, tile)], osem.at[i])

    for i, dst in enumerate((q_h, k_h)):
        for n in range(count_n):
            for c in range(0, tokens, 256):
                at = pl.ds(c, 256)
                v = dot(left[at, :], mat[:, pl.ds(i * part + n * tile, tile)])
                for l in range(0, tile, 128):
                    o = coef[i, at, :] * v[:, l : l + 128]
                    tiles[i * count_n + n, at, pl.ds(l, 128)] = o.astype(BF16)
            out_copy(i, n, dst).start()
    for i in range(2):
        done = tiles.at[pl.ds(i * count_n, count_n)]
        pltpu.make_async_copy(done, done, osem.at[i]).wait()


def finish(left, coef, mat):
    tokens, part = left.shape[0], mat.shape[1] // 2
    tile = 256 if part % 256 == 0 else 128
    out = jax.ShapeDtypeStruct((tokens, part), BF16)
    V, dma = pltpu.VMEM, pltpu.SemaphoreType.DMA
    return pl.pallas_call(
        final,
        out_shape=(out, out),
        in_specs=[pl.BlockSpec(memory_space=V)] * 3,
        out_specs=(pl.BlockSpec(memory_space=pl.ANY),) * 2,
        scratch_shapes=[V((2 * part // tile, tokens, tile), BF16), dma((2,))],
        compiler_params=pltpu.CompilerParams(vmem_limit_bytes=12 * 2**20),
    )(left, coef, mat)


def solution(mesh):
    in_specs = (
        P("tm", "rows", None, None), P(), P(), P(), P(), P(), P(), P(), P(), P(),
        P(None, "tm"), P("tm"), P("tm"), P(None, "tm"), P("tm"), P("tm"), P(),
    )
    out_specs = (P("rows", "tm"), P("rows", "tm"))
    return jax.shard_map(per_device, mesh=mesh, in_specs=in_specs, out_specs=out_specs, check_vma=False)
```

```python
import functools

import jax
import jax.numpy as jnp
from jax import lax
from jax.experimental import pallas as pl
from jax.experimental.pallas import tpu as pltpu
from jax.sharding import PartitionSpec as P

epsilon = 1e-06
MESH = pl.DeviceIdType.MESH
F32, BF16 = jnp.float32, jnp.bfloat16


def dot(a, b, **kw):
    return jnp.dot(a, b, preferred_element_type=F32, **kw)


def split(v):
    hi = v.astype(BF16)
    return hi, (v - hi.astype(F32)).astype(BF16)


def planes(count_r):
    inner = 1
    while inner * inner * 4 <= count_r and count_r % (inner * 2) == 0:
        inner *= 2
    return count_r // inner if count_r // inner % 2 == 0 else 1


def kernel(
    count_t, count_r,
    packing_h, feat_h, gain_h, conv_h, cbias_h, lw_h, lbias_h, pw_h, pb_h, shift_h, scale_h,
    wq_h, qb_h, qg_h, wk_h, kb_h, kg_h,
    left, coef, mat,
    packing, feat, gain, conv, cbias, lw, lbias, pw, pb, shift, scale, w_all, qb, kb, qg, kg, rows_qk,
    scr, km, lhs, y_ref, snd, rcv, tot, lat_all, pwf, bounce, mod, cen, m_all, gram, gram_out, gram_s, gram_r,
    lsem, csem, wsem, hs_sem, hr_sem, as_sem, ar_sem, ss_sem, sr_sem,
):
    t, r = lax.axis_index("tm"), lax.axis_index("rows")
    count = count_t * count_r
    own = t * count_r + r
    _, _, cols, chans = feat.shape
    feats, width = pw.shape
    lats = lw.shape[0]
    half = cols // 2
    part = wq_h.shape[1]
    tile = w_all.shape[2]
    count_n = part // tile
    rows_m = mod.shape[0] // 2

    early = [(feat_h, feat), (gain_h, gain), (lw_h, lw)]
    late = [
        (pw_h, pw), (pb_h, pb), (shift_h, shift), (scale_h, scale), (cbias_h, cbias), (lbias_h, lbias),
        (qb_h, qb), (kb_h, kb), (qg_h, qg), (kg_h, kg), (packing_h, packing),
    ]
    copies = [pltpu.make_async_copy(s, d, lsem.at[i]) for i, (s, d) in enumerate(early + late)]
    first, later = copies[: len(early)], copies[len(early) :]
    runs = [(0, 1), (1, 2), (3, 2), (5, 2), (7, 2)]
    taps = [
        pltpu.make_async_copy(conv_h.at[pl.ds(i, n)], conv.at[pl.ds(i, n)], csem.at[k]) for k, (i, n) in enumerate(runs)
    ]
    for c in first + taps + later:
        c.start()
    loads = [
        pltpu.make_async_copy(w.at[:, pl.ds(n * tile, tile)], w_all.at[h * count_n + n], wsem.at[(h * count_n + n) // 2])
        for h, w in enumerate((wq_h, wk_h)) for n in range(count_n)
    ]

    barrier = pltpu.get_barrier_semaphore()

    def greet(i, c):
        other = lax.rem(own + i, count)
        pl.semaphore_signal(barrier, inc=1, device_id=(other // count_r, lax.rem(other, count_r)), device_id_type=MESH)
        return c

    lax.fori_loop(1, count, greet, 0)
    nt = (((1,), (1,)), ((), ()))

    for c in first:
        c.wait()
    lwv = lw[...]
    gain_v = gain[...].reshape(1, chans)
    row_at = lax.broadcasted_iota(jnp.int32, (half, 128), 0)
    for f in range(2):
        for w in range(2):
            v = feat[f, w].astype(F32)
            sm = jnp.mean(v * v, axis=-1, keepdims=True)
            x = v * lax.rsqrt(sm + epsilon) * gain_v
            act = (x / (1.0 + jnp.exp(-x))).astype(BF16).astype(F32)
            base = (f * 2 + w) * cols
            for l in range(chans // 128):
                scr[0, l] = act[:, l * 128 : (l + 1) * 128]
                scr[1, l] = v[:, l * 128 : (l + 1) * 128]
                even, odd = scr[0, l, pl.ds(0, half, 2), :], scr[0, l, pl.ds(1, half, 2), :]
                before = jnp.where(row_at == 0, 0.0, pltpu.roll(odd, 1, 0))
                after = jnp.where(row_at == half - 1, 0.0, pltpu.roll(even, half - 1, 0))
                plain = (scr[1, l, pl.ds(0, half, 2), :], scr[1, l, pl.ds(1, half, 2), :])
                for k, (low, high) in enumerate(((before, even), (even, odd), (odd, after), plain)):
                    lhs[pl.ds(base, half), pl.ds(k * chans + l * 128, 128)] = low.astype(BF16)
                    lhs[pl.ds(base + half, half), pl.ds(k * chans + l * 128, 128)] = high.astype(BF16)

    none = jnp.zeros((lats, chans), BF16)
    pair = jnp.concatenate(
        [jnp.concatenate([lwv, none], axis=1), jnp.concatenate([none, lwv], axis=1)], axis=0
    )
    km[:, pl.ds(3 * chans, chans)] = jnp.zeros((9 * lats, chans), BF16)
    km[pl.ds(7 * lats, lats), pl.ds(3 * chans, chans)] = lwv
    started = 0
    for p, (i, n) in enumerate(runs):
        ids = range(i, i + n)
        taps[p].wait()
        more = min(len(loads), (p + 1) * -(-len(loads) // 5))
        for c in loads[started:more]:
            c.start()
        started = more
        for e in range(3):
            rhs = jnp.concatenate([conv[i, e] for i in ids], axis=1)
            folded = lax.dot_general(pair if n == 2 else lwv, rhs, nt, preferred_element_type=F32)
            km[pl.ds(ids[0] * lats, lats * len(ids)), pl.ds(e * chans, chans)] = folded.astype(BF16)
    y_ref[...] = lax.dot_general(km[...], lhs[...], nt, preferred_element_type=F32)

    def total(d, q):
        out = None
        for f in range(2):
            for w in range(2):
                a, b = f + 2 - d, w + 1 - q
                if 0 <= a < 3 and 0 <= b < 3:
                    term = y_ref[pl.ds((a * 3 + b) * lats, lats), pl.ds((f * 2 + w) * cols, cols)]
                    out = term if out is None else out + term
        return out

    sent = [(0, -1), (1, -1), (0, 2), (1, 2), (2, 0), (2, 1), (3, 0), (3, 1), (2, -1), (3, -1), (2, 2), (3, 2)]
    for i, (d, q) in enumerate(sent):
        snd[pl.ds(i * lats, lats), :] = total(d, q)

    pl.semaphore_wait(barrier, count - 1)

    has_up, has_down = r > 0, r < count_r - 1
    has_next, has_prev = t < count_t - 1, t > 0
    plan = [
        (0, 2, t, r - 1, has_up, has_down, (1, 3)),
        (2, 2, t, r + 1, has_down, has_up, (0, 2)),
        (4, 4, t + 1, r, has_next, has_prev, (0, 1, 2, 3)),
        (8, 2, t + 1, r - 1, has_next & has_up, has_prev & has_down, (1, 3)),
        (10, 2, t + 1, r + 1, has_next & has_down, has_prev & has_up, (0, 2)),
    ]
    halo = []
    for k, (at, n, dt, dr, _, _, _) in enumerate(plan):
        rows = pl.ds(at * lats, n * lats)
        halo.append(pltpu.make_async_remote_copy(
            src_ref=snd.at[rows], dst_ref=rcv.at[rows], send_sem=hs_sem.at[k], recv_sem=hr_sem.at[k],
            device_id=(dt, dr), device_id_type=MESH,
        ))
    for copy, p in zip(halo, plan):
        pl.when(p[4])(copy.start)

    for c in later:
        c.wait()
    offset = jnp.sum(lwv.astype(F32) * cbias[...].reshape(1, chans), axis=1, keepdims=True)
    at_l = lax.broadcasted_iota(jnp.int32, (lats, lats), 0) == lax.broadcasted_iota(jnp.int32, (lats, lats), 1)
    offset = offset + jnp.sum(jnp.where(at_l, lbias[...].reshape(1, lats), 0.0), axis=1, keepdims=True)
    for i, (d, q) in enumerate(((0, 0), (0, 1), (1, 0), (1, 1))):
        tot[pl.ds(i * lats, lats), :] = total(d, q) + offset

    step = 512

    def lanes_sum(v):
        out = v[:, 0:128]
        for i in range(1, v.shape[1] // 128):
            out = out + v[:, i * 128 : (i + 1) * 128]
        return out

    total_w = jnp.zeros((feats, 128), F32)
    total_b = jnp.zeros((1, 128), F32)
    groups = feats // lats
    for c in range(0, width, step):
        for l in range(step // 128):
            bounce[l] = pw[:, c + l * 128 : c + (l + 1) * 128].astype(F32)
        mixed = jnp.concatenate([
            jnp.concatenate([bounce[l, pl.ds(k, lats, groups), :] for k in range(groups)], axis=0)
            for l in range(step // 128)
        ], axis=1)
        pwf[:, c : c + step] = mixed
        total_w = total_w + lanes_sum(mixed)
        total_b = total_b + lanes_sum(pb[pl.ds(c, step)].reshape(1, step))
    mean = jnp.sum(total_w, axis=1, keepdims=True) / width
    mean_b = jnp.sum(total_b, axis=1, keepdims=True) / width
    at16 = lax.broadcasted_iota(jnp.int32, (16, step), 0)
    for c in range(0, width, step):
        gains = 1.0 + scale[pl.ds(c, step)].reshape(1, step)
        center = pwf[:, c : c + step] - mean
        center_b = pb[pl.ds(c, step)].reshape(1, step) - mean_b
        moved = shift[pl.ds(c, step)].reshape(1, step)
        last = jnp.where(at16 == 0, center_b * gains, jnp.where(at16 == 1, moved, 0.0))
        for k, piece in enumerate(split(center * gains)):
            mod[pl.ds(k * rows_m, feats), c : c + step] = piece
        for k, piece in enumerate(split(last)):
            mod[pl.ds(k * rows_m + feats, 16), c : c + step] = piece

    def gram_of(v):
        g = lax.dot_general(v, v, nt, preferred_element_type=F32)
        return g[0:rows_m, 0:rows_m] + g[0:rows_m, rows_m:] + g[rows_m:, 0:rows_m] + g[rows_m:, rows_m:]

    lower = lax.broadcasted_iota(jnp.int32, (feats // 2, 128), 1) < feats

    def pack(v, ref):
        gram[:, 0:rows_m] = gram_of(v)
        ref[pl.ds(0, feats // 2), :] = jnp.where(
            lower, gram[0 : feats // 2, :], pltpu.roll(gram[feats // 2 : feats, :], feats, 1)
        )
        ref[pl.ds(feats // 2, 8), :] = gram[feats : feats + 8, :]

    gram[...] = jnp.zeros(gram.shape, F32)
    for h, (bias, gains) in enumerate(((qb, qg), (kb, kg))):
        for n in range(count_n):
            at = pl.ds(n * tile, tile)
            rows_qk[h * count_n + n, 0:1, :] = bias[at].reshape(1, tile)
            rows_qk[h * count_n + n, 1:2, :] = gains[at].reshape(1, tile)
    mat[pl.ds(2 * feats + 16, 2 * feats - 16), :] = jnp.zeros((2 * feats - 16, 2 * part), BF16)
    at_row = lax.broadcasted_iota(jnp.int32, (rows_m, tile), 0)
    at_last = lax.broadcasted_iota(jnp.int32, (16, tile), 0)

    def project(g):
        to = pl.ds(pl.multiple_of(g * tile, tile), tile)
        v = dot(mod[...], w_all[g])
        v = v[0:rows_m] + v[rows_m:] + jnp.where(at_row == feats + 1, rows_qk[g, 0:1, :], 0.0)
        for k, piece in enumerate(split(v)):
            m_all[pl.ds(k * rows_m, rows_m), to] = piece
        v = v * rows_qk[g, 1:2, :]
        for k, piece in enumerate(split(v[0:feats])):
            mat[pl.ds(k * feats, feats), to] = piece
        m, c = v[feats : feats + 1], v[feats + 1 : feats + 2]
        m_hi, c_hi = m.astype(BF16).astype(F32), c.astype(BF16).astype(F32)
        last = jnp.where(at_last % 2 == 0, c_hi, c - c_hi)
        last = jnp.where(at_last == 0, m_hi, jnp.where(at_last == 1, m - m_hi, last))
        mat[pl.ds(2 * feats, 16), to] = jnp.where(at_last < 8, last, 0.0).astype(BF16)

    def both(p, carry):
        pair_at = w_all.at[pl.ds(2 * p, 2)]
        pltpu.make_async_copy(pair_at, pair_at, wsem.at[p]).wait()
        for g in (2 * p, 2 * p + 1):
            project(g)
        return carry

    def share(h):
        pack(m_all[:, pl.ds(h * part, part)], gram_s.at[h])
        out = [
            pltpu.make_async_remote_copy(
                src_ref=gram_s.at[h], dst_ref=gram_r.at[h, i - 1], send_sem=ss_sem.at[h],
                recv_sem=sr_sem.at[h], device_id=(lax.rem(t + i, count_t), r), device_id_type=MESH,
            )
            for i in range(1, count_t)
        ]
        for c in out:
            c.start()
        return pltpu.make_async_remote_copy(
            src_ref=gram_r.at[h], dst_ref=gram_r.at[h], send_sem=ss_sem.at[h], recv_sem=sr_sem.at[h],
            device_id=(t, r), device_id_type=MESH,
        )

    middle = -(-count_n // 2)
    ahead = min(2, middle)
    lax.fori_loop(0, ahead, both, 0)
    for copy, p in zip(halo, plan):
        def take(copy=copy, p=p):
            copy.wait_recv()
            for k, i in enumerate(p[6]):
                tot[pl.ds(i * lats, lats), :] += rcv[pl.ds((p[0] + k) * lats, lats), :]
        pl.when(p[5])(take)

    lane = lax.broadcasted_iota(jnp.int32, (lats, cols), 1)
    for q in range(2):
        f0, f1 = tot[pl.ds(q * lats, lats), :], tot[pl.ds((2 + q) * lats, lats), :]
        lat_all[own, pl.ds(2 * q * lats, lats), :] = jnp.where(lane < half, f0, pltpu.roll(f1, half, 1)).astype(BF16)
        lat_all[own, pl.ds((2 * q + 1) * lats, lats), :] = jnp.where(lane < half, pltpu.roll(f0, half, 1), f1).astype(BF16)

    outer = planes(count_r)
    inner, flat = count_r // outer, count_t // 2 * (count_r // outer)
    group, cross = outer * flat, outer // 2
    side = lax.rem(t, 2)
    mate = t + 1 - 2 * side
    far, near, chip, chips = r // inner, lax.rem(r, inner), t // 2, count_t // 2
    flip = lax.min(far // max(outer // 2, 1), 1)
    mirror = far + flip * (outer - 1 - 2 * far)

    def place(i):
        v = outer - 1 - i // flat
        v = v - lax.max(0, lax.min(1, mirror - v + 1))
        v = v + lax.max(0, i // flat - outer + 2) * (mirror - v)
        k = flat - 1 - lax.rem(i, flat)
        other = lax.rem(chip + k // inner, chips)
        return other * 2, (v + flip * (outer - 1 - 2 * v)) * inner + lax.rem(near + lax.rem(k, inner), inner)

    def send(at, dt, dr, sent, got):
        return pltpu.make_async_remote_copy(
            src_ref=lat_all.at[at], dst_ref=lat_all.at[at], send_sem=as_sem.at[sent], recv_sem=ar_sem.at[got],
            device_id=(dt, dr), device_id_type=MESH,
        )

    def all_of(n, sent, got):
        return send(pl.ds(0, n), mate, r, sent, got)

    def loop(first, last, body):
        lax.fori_loop(first, last, lambda i, c: (body(i), c)[1], 0)

    spans = ((cross * flat, group - 1), (0, cross * flat))

    def each(body):
        for s in range(2):
            if spans[s][1] > spans[s][0]:
                pl.when(side == s)(functools.partial(body, s))

    def spread(ident):
        def one(i):
            pt, pr = place(i)
            send(ident, pt + side, pr, 0, far).start()

        each(lambda s: loop(*spans[s], one))

    def relay(s):
        for j in range(outer - 1, -1, -1):
            first, last = max(j * flat, spans[s][0]), min((j + 1) * flat, spans[s][1])
            if last <= first:
                continue
            _, pr = place(first)
            all_of(2 * (last - first), 0, pr // inner).wait_recv()

            def one(i):
                pt, pr = place(i)
                for h in range(2):
                    send((pt + h) * count_r + pr, mate, r, 1, outer + 1).start()

            loop(first, last, one)

    send(own, mate, r, 1, outer).start()
    spread(own)

    lax.fori_loop(ahead, middle, both, 0)
    all_of(1, 1, outer).wait_recv()
    spread(mate * count_r + r)
    shares = [share(0)]
    lax.fori_loop(middle, count_n, both, 0)
    shares.append(share(1))
    for c in range(0, width, step):
        center_b = jnp.where(at16 == 0, pb[pl.ds(c, step)].reshape(1, step) - mean_b, 0.0)
        for k, piece in enumerate(split(pwf[:, c : c + step] - mean)):
            cen[pl.ds(k * rows_m, feats), c : c + step] = piece
        for k, piece in enumerate(split(center_b)):
            cen[pl.ds(k * rows_m + feats, 16), c : c + step] = piece
    pack(cen[...], gram_out.at[0])

    each(relay)
    counts = [2 * (last - first) for first, last in spans]
    for s in range(2):
        if counts[1 - s]:
            pl.when(side == s)(lambda s=s: all_of(counts[1 - s], 1, outer + 1).wait_recv())

    for h in range(2):
        gram_out[1 + h] = gram_s[h]
        shares[h].wait_recv()
        for i in range(count_t - 1):
            gram_out[1 + h] += gram_r[h, i]

    lane1 = lax.broadcasted_iota(jnp.int32, (1, 128), 1)
    hf = feats // 2
    quads, ends = [], []
    for h in range(3):
        top, tail = gram_out[h, 0:hf, :], gram_out[h, hf : hf + 8, :]
        square = jnp.where(lane1 < feats, jnp.concatenate([top, pltpu.roll(top, feats, 1)], axis=0), 0.0)
        quads.append(square)
        ends.append(jnp.where(lane1 < feats, tail, 0.0))

    def entry(h, row, at):
        return jnp.sum(jnp.where(lane1 == at, gram_out[h, hf + row : hf + row + 1, :], 0.0), axis=1, keepdims=True)

    hi, lo = split(jnp.concatenate(quads + ends, axis=0))
    lo_at = pltpu.roll(lo.astype(F32), feats, 1).astype(BF16)
    stacked = hi + lo_at
    at16 = lax.broadcasted_iota(jnp.int32, (16, cols), 0)
    for j in range(count_t):
        x = lat_all[packing[r * count_t + j]]
        prod = dot(stacked, jnp.concatenate([x, x], axis=0))
        x = x.astype(F32)
        line = lambda h, row: prod[3 * feats + 8 * h + row : 3 * feats + 8 * h + row + 1, :]
        square = lambda h: jnp.sum(x * prod[h * feats : (h + 1) * feats, :], axis=0, keepdims=True)
        var = (square(0) + 2.0 * line(0, 0) + entry(0, 0, feats)) / width + epsilon
        inv = lax.rsqrt(var)
        sigma = var * inv
        high = sigma.astype(BF16).astype(F32)
        mid = (sigma - high).astype(BF16).astype(F32)
        more = jnp.where(at16 < 4, high, jnp.where(at16 < 6, mid, sigma - high - mid))
        more = jnp.where(at16 < 2, 1.0, jnp.where(at16 < 8, more, 0.0))
        at = pl.ds(j * cols, cols)
        rest = jnp.zeros((2 * feats - 16, cols), F32)
        left[at, :] = jnp.concatenate([x, x, more, rest], axis=0).T.astype(BF16)
        for h in range(1, 3):
            ss = inv * inv * (square(h) + 2.0 * line(h, 0) + entry(h, 0, feats))
            ss = ss + 2.0 * inv * (line(h, 1) + entry(h, 0, feats + 1)) + entry(h, 1, feats + 1)
            coef[h - 1, at, :] = jnp.broadcast_to(lax.rsqrt(ss / width + epsilon) * inv, (128, cols)).T

    for copy, p in zip(halo, plan):
        pl.when(p[4])(copy.wait_send)
    each(lambda s: all_of(counts[s], 0, outer).wait_send())
    for s in range(2):
        pl.when(side == s)(lambda s=s: all_of(counts[s] + 1, 1, outer).wait_send())
    for c in shares:
        c.wait_send()


def per_device(
    features, block_gain, conv_weight, conv_bias, latent_weight, latent_bias, patch_weight, patch_bias,
    shift_mod, scale_mod, query_weight, query_bias, query_gain, key_weight, key_bias, key_gain, packing,
):
    count_t, count_r = lax.axis_size("tm"), lax.axis_size("rows")
    count = count_t * count_r
    _, _, cols, chans = features.shape
    feats, width = patch_weight.shape
    lats = latent_weight.shape[1]
    part = query_weight.shape[1]
    tile = 256 if part % 256 == 0 else 128
    V = pltpu.VMEM
    rows_m = feats + 16
    operands = (
        packing, features, block_gain, conv_weight.reshape(9, 3, chans, chans), conv_bias, latent_weight.T, latent_bias, patch_weight, patch_bias,
        shift_mod, scale_mod, query_weight, query_bias, query_gain, key_weight, key_bias, key_gain,
    )
    like = lambda a: V(a.shape, a.dtype)
    scratch = [pltpu.SMEM(packing.shape, packing.dtype)] + [like(a) for a in operands[1:11]]
    scratch += [
        V((2 * part // tile, width, tile), BF16),
        V((part,), F32),
        V((part,), F32),
        V((part,), F32),
        V((part,), F32),
        V((2 * part // tile, 8, tile), F32),
        V((2, chans // 128, cols, 128), F32),
        V((9 * lats, 4 * chans), BF16),
        V((4 * cols, 4 * chans), BF16),
        V((9 * lats, 4 * cols), F32),
        V((12 * lats, cols), F32),
        V((12 * lats, cols), F32),
        V((4 * lats, cols), F32),
        V((count, feats, cols), BF16),
        V((feats, width), F32),
        V((4, feats, 128), F32),
        V((2 * rows_m, width), BF16),
        V((2 * rows_m, width), BF16),
        V((2 * rows_m, 2 * part), BF16),
        V((rows_m, 128), F32),
        V((3, feats // 2 + 8, 128), F32),
        V((2, feats // 2 + 8, 128), F32),
        V((2, count_t - 1, feats // 2 + 8, 128), F32),
    ]
    dma = pltpu.SemaphoreType.DMA
    scratch += [
        dma((14,)), dma((5,)), dma((part // tile,)), dma((5,)), dma((5,)), dma((2,)), dma((planes(count_r) + 2,)), dma((2,)), dma((2,)),
    ]
    outs = (
        jax.ShapeDtypeStruct((count_t * cols, 4 * feats), BF16),
        jax.ShapeDtypeStruct((2, count_t * cols, 128), F32),
        jax.ShapeDtypeStruct((4 * feats, 2 * part), BF16),
    )
    left, coef, mat = pl.pallas_call(
        functools.partial(kernel, count_t, count_r),
        out_shape=outs,
        in_specs=[pl.BlockSpec(memory_space=pltpu.HBM)] * 17,
        out_specs=(pl.BlockSpec(memory_space=V),) * 3,
        scratch_shapes=scratch,
        compiler_params=pltpu.CompilerParams(collective_id=0, has_side_effects=True, vmem_limit_bytes=47 * 2**20),
    )(*[pltpu.with_memory_space_constraint(a, pltpu.HBM) for a in operands])
    return finish(left, coef, mat)


def final(left, coef, mat, q_h, k_h, tiles, osem):
    part = mat.shape[1] // 2
    tokens = left.shape[0]
    tile = tiles.shape[2]
    count_n = part // tile

    def out_copy(i, n, dst):
        return pltpu.make_async_copy(tiles.at[i * count_n + n], dst.at[:, pl.ds(n * tile, tile)], osem.at[i])

    for i, dst in enumerate((q_h, k_h)):
        for n in range(count_n):
            for c in range(0, tokens, 256):
                at = pl.ds(c, 256)
                v = dot(left[at, :], mat[:, pl.ds(i * part + n * tile, tile)])
                for l in range(0, tile, 128):
                    o = coef[i, at, :] * v[:, l : l + 128]
                    tiles[i * count_n + n, at, pl.ds(l, 128)] = o.astype(BF16)
            out_copy(i, n, dst).start()
    for i in range(2):
        done = tiles.at[pl.ds(i * count_n, count_n)]
        pltpu.make_async_copy(done, done, osem.at[i]).wait()


def finish(left, coef, mat):
    tokens, part = left.shape[0], mat.shape[1] // 2
    tile = 256 if part % 256 == 0 else 128
    out = jax.ShapeDtypeStruct((tokens, part), BF16)
    V, dma = pltpu.VMEM, pltpu.SemaphoreType.DMA
    return pl.pallas_call(
        final,
        out_shape=(out, out),
        in_specs=[pl.BlockSpec(memory_space=V)] * 3,
        out_specs=(pl.BlockSpec(memory_space=pl.ANY),) * 2,
        scratch_shapes=[V((2 * part // tile, tokens, tile), BF16), dma((2,))],
        compiler_params=pltpu.CompilerParams(vmem_limit_bytes=12 * 2**20),
    )(left, coef, mat)


def solution(mesh):
    in_specs = (
        P("tm", "rows", None, None), P(), P(), P(), P(), P(), P(), P(), P(), P(),
        P(None, "tm"), P("tm"), P("tm"), P(None, "tm"), P("tm"), P("tm"), P(),
    )
    out_specs = (P("rows", "tm"), P("rows", "tm"))
    return jax.shard_map(per_device, mesh=mesh, in_specs=in_specs, out_specs=out_specs, check_vma=False)
```

```python
import functools

import jax
import jax.numpy as jnp
from jax import lax
from jax.experimental import pallas as pl
from jax.experimental.pallas import tpu as pltpu
from jax.sharding import PartitionSpec as P

epsilon = 1e-06
MESH = pl.DeviceIdType.MESH
F32, BF16 = jnp.float32, jnp.bfloat16


def dot(a, b, **kw):
    return jnp.dot(a, b, preferred_element_type=F32, **kw)


def split(v):
    hi = v.astype(BF16)
    return hi, (v - hi.astype(F32)).astype(BF16)


def kernel(
    count_t, count_r,
    packing_h, feat_h, gain_h, conv_h, cbias_h, lw_h, lbias_h, pw_h, pb_h, shift_h, scale_h,
    wq_h, qb_h, qg_h, wk_h, kb_h, kg_h,
    left, coef, mat,
    packing, feat, gain, conv, cbias, lw, lbias, pw, pb, shift, scale, w_all, qb, kb, qg, kg, rows_qk,
    scr, km, lhs, y_ref, snd, rcv, tot, lat_all, pwf, bounce, mod, cen, m_all, gram, gram_out, gram_s, gram_r,
    lsem, csem, wsem, hs_sem, hr_sem, as_sem, ar_sem, ss_sem, sr_sem,
):
    t, r = lax.axis_index("tm"), lax.axis_index("rows")
    count = count_t * count_r
    own = t * count_r + r
    _, _, cols, chans = feat.shape
    feats, width = pw.shape
    lats = lw.shape[0]
    half = cols // 2
    part = wq_h.shape[1]
    tile = w_all.shape[2]
    count_n = part // tile
    rows_m = mod.shape[0] // 2

    early = [(feat_h, feat), (gain_h, gain), (lw_h, lw)]
    late = [
        (pw_h, pw), (pb_h, pb), (shift_h, shift), (scale_h, scale), (cbias_h, cbias), (lbias_h, lbias),
        (qb_h, qb), (kb_h, kb), (qg_h, qg), (kg_h, kg), (packing_h, packing),
    ]
    copies = [pltpu.make_async_copy(s, d, lsem.at[i]) for i, (s, d) in enumerate(early + late)]
    first, later = copies[: len(early)], copies[len(early) :]
    runs = [(0, 1), (1, 2), (3, 2), (5, 2), (7, 2)]
    taps = [
        pltpu.make_async_copy(conv_h.at[pl.ds(i, n)], conv.at[pl.ds(i, n)], csem.at[k]) for k, (i, n) in enumerate(runs)
    ]
    for c in first + taps + later:
        c.start()
    loads = [
        pltpu.make_async_copy(w.at[:, pl.ds(n * tile, tile)], w_all.at[h * count_n + n], wsem.at[(h * count_n + n) // 2])
        for h, w in enumerate((wq_h, wk_h)) for n in range(count_n)
    ]

    barrier = pltpu.get_barrier_semaphore()

    def greet(i, c):
        other = lax.rem(own + i, count)
        pl.semaphore_signal(barrier, inc=1, device_id=(other // count_r, lax.rem(other, count_r)), device_id_type=MESH)
        return c

    lax.fori_loop(1, count, greet, 0)
    nt = (((1,), (1,)), ((), ()))

    for c in first:
        c.wait()
    lwv = lw[...]
    gain_v = gain[...].reshape(1, chans)
    row_at = lax.broadcasted_iota(jnp.int32, (half, 128), 0)
    for f in range(2):
        for w in range(2):
            v = feat[f, w].astype(F32)
            sm = jnp.mean(v * v, axis=-1, keepdims=True)
            x = v * lax.rsqrt(sm + epsilon) * gain_v
            act = (x / (1.0 + jnp.exp(-x))).astype(BF16).astype(F32)
            base = (f * 2 + w) * cols
            for l in range(chans // 128):
                scr[0, l] = act[:, l * 128 : (l + 1) * 128]
                scr[1, l] = v[:, l * 128 : (l + 1) * 128]
                even, odd = scr[0, l, pl.ds(0, half, 2), :], scr[0, l, pl.ds(1, half, 2), :]
                before = jnp.where(row_at == 0, 0.0, pltpu.roll(odd, 1, 0))
                after = jnp.where(row_at == half - 1, 0.0, pltpu.roll(even, half - 1, 0))
                plain = (scr[1, l, pl.ds(0, half, 2), :], scr[1, l, pl.ds(1, half, 2), :])
                for k, (low, high) in enumerate(((before, even), (even, odd), (odd, after), plain)):
                    lhs[pl.ds(base, half), pl.ds(k * chans + l * 128, 128)] = low.astype(BF16)
                    lhs[pl.ds(base + half, half), pl.ds(k * chans + l * 128, 128)] = high.astype(BF16)

    none = jnp.zeros((lats, chans), BF16)
    pair = jnp.concatenate(
        [jnp.concatenate([lwv, none], axis=1), jnp.concatenate([none, lwv], axis=1)], axis=0
    )
    km[:, pl.ds(3 * chans, chans)] = jnp.zeros((9 * lats, chans), BF16)
    km[pl.ds(7 * lats, lats), pl.ds(3 * chans, chans)] = lwv
    started = 0
    for p, (i, n) in enumerate(runs):
        ids = range(i, i + n)
        taps[p].wait()
        more = min(len(loads), (p + 1) * -(-len(loads) // 5))
        for c in loads[started:more]:
            c.start()
        started = more
        for e in range(3):
            rhs = jnp.concatenate([conv[i, e] for i in ids], axis=1)
            folded = lax.dot_general(pair if n == 2 else lwv, rhs, nt, preferred_element_type=F32)
            km[pl.ds(ids[0] * lats, lats * len(ids)), pl.ds(e * chans, chans)] = folded.astype(BF16)
    y_ref[...] = lax.dot_general(km[...], lhs[...], nt, preferred_element_type=F32)

    def total(d, q):
        out = None
        for f in range(2):
            for w in range(2):
                a, b = f + 2 - d, w + 1 - q
                if 0 <= a < 3 and 0 <= b < 3:
                    term = y_ref[pl.ds((a * 3 + b) * lats, lats), pl.ds((f * 2 + w) * cols, cols)]
                    out = term if out is None else out + term
        return out

    sent = [(0, -1), (1, -1), (0, 2), (1, 2), (2, 0), (2, 1), (3, 0), (3, 1), (2, -1), (3, -1), (2, 2), (3, 2)]
    for i, (d, q) in enumerate(sent):
        snd[pl.ds(i * lats, lats), :] = total(d, q)

    pl.semaphore_wait(barrier, count - 1)

    has_up, has_down = r > 0, r < count_r - 1
    has_next, has_prev = t < count_t - 1, t > 0
    plan = [
        (0, 2, t, r - 1, has_up, has_down, (1, 3)),
        (2, 2, t, r + 1, has_down, has_up, (0, 2)),
        (4, 4, t + 1, r, has_next, has_prev, (0, 1, 2, 3)),
        (8, 2, t + 1, r - 1, has_next & has_up, has_prev & has_down, (1, 3)),
        (10, 2, t + 1, r + 1, has_next & has_down, has_prev & has_up, (0, 2)),
    ]
    halo = []
    for k, (at, n, dt, dr, _, _, _) in enumerate(plan):
        rows = pl.ds(at * lats, n * lats)
        halo.append(pltpu.make_async_remote_copy(
            src_ref=snd.at[rows], dst_ref=rcv.at[rows], send_sem=hs_sem.at[k], recv_sem=hr_sem.at[k],
            device_id=(dt, dr), device_id_type=MESH,
        ))
    for copy, p in zip(halo, plan):
        pl.when(p[4])(copy.start)

    for c in later:
        c.wait()
    offset = jnp.sum(lwv.astype(F32) * cbias[...].reshape(1, chans), axis=1, keepdims=True)
    at_l = lax.broadcasted_iota(jnp.int32, (lats, lats), 0) == lax.broadcasted_iota(jnp.int32, (lats, lats), 1)
    offset = offset + jnp.sum(jnp.where(at_l, lbias[...].reshape(1, lats), 0.0), axis=1, keepdims=True)
    for i, (d, q) in enumerate(((0, 0), (0, 1), (1, 0), (1, 1))):
        tot[pl.ds(i * lats, lats), :] = total(d, q) + offset

    step = 512

    def lanes_sum(v):
        out = v[:, 0:128]
        for i in range(1, v.shape[1] // 128):
            out = out + v[:, i * 128 : (i + 1) * 128]
        return out

    total_w = jnp.zeros((feats, 128), F32)
    total_b = jnp.zeros((1, 128), F32)
    groups = feats // lats
    for c in range(0, width, step):
        for l in range(step // 128):
            bounce[l] = pw[:, c + l * 128 : c + (l + 1) * 128].astype(F32)
        mixed = jnp.concatenate([
            jnp.concatenate([bounce[l, pl.ds(k, lats, groups), :] for k in range(groups)], axis=0)
            for l in range(step // 128)
        ], axis=1)
        pwf[:, c : c + step] = mixed
        total_w = total_w + lanes_sum(mixed)
        total_b = total_b + lanes_sum(pb[pl.ds(c, step)].reshape(1, step))
    mean = jnp.sum(total_w, axis=1, keepdims=True) / width
    mean_b = jnp.sum(total_b, axis=1, keepdims=True) / width
    at16 = lax.broadcasted_iota(jnp.int32, (16, step), 0)
    for c in range(0, width, step):
        gains = 1.0 + scale[pl.ds(c, step)].reshape(1, step)
        center = pwf[:, c : c + step] - mean
        center_b = pb[pl.ds(c, step)].reshape(1, step) - mean_b
        moved = shift[pl.ds(c, step)].reshape(1, step)
        last = jnp.where(at16 == 0, center_b * gains, jnp.where(at16 == 1, moved, 0.0))
        for k, piece in enumerate(split(center * gains)):
            mod[pl.ds(k * rows_m, feats), c : c + step] = piece
        for k, piece in enumerate(split(last)):
            mod[pl.ds(k * rows_m + feats, 16), c : c + step] = piece

    def gram_of(v):
        g = lax.dot_general(v, v, nt, preferred_element_type=F32)
        return g[0:rows_m, 0:rows_m] + g[0:rows_m, rows_m:] + g[rows_m:, 0:rows_m] + g[rows_m:, rows_m:]

    lower = lax.broadcasted_iota(jnp.int32, (feats // 2, 128), 1) < feats

    def pack(v, ref):
        gram[:, 0:rows_m] = gram_of(v)
        ref[pl.ds(0, feats // 2), :] = jnp.where(
            lower, gram[0 : feats // 2, :], pltpu.roll(gram[feats // 2 : feats, :], feats, 1)
        )
        ref[pl.ds(feats // 2, 8), :] = gram[feats : feats + 8, :]

    gram[...] = jnp.zeros(gram.shape, F32)
    for h, (bias, gains) in enumerate(((qb, qg), (kb, kg))):
        for n in range(count_n):
            at = pl.ds(n * tile, tile)
            rows_qk[h * count_n + n, 0:1, :] = bias[at].reshape(1, tile)
            rows_qk[h * count_n + n, 1:2, :] = gains[at].reshape(1, tile)
    mat[pl.ds(2 * feats + 16, 2 * feats - 16), :] = jnp.zeros((2 * feats - 16, 2 * part), BF16)
    at_row = lax.broadcasted_iota(jnp.int32, (rows_m, tile), 0)
    at_last = lax.broadcasted_iota(jnp.int32, (16, tile), 0)

    def project(g):
        to = pl.ds(pl.multiple_of(g * tile, tile), tile)
        v = dot(mod[...], w_all[g])
        v = v[0:rows_m] + v[rows_m:] + jnp.where(at_row == feats + 1, rows_qk[g, 0:1, :], 0.0)
        for k, piece in enumerate(split(v)):
            m_all[pl.ds(k * rows_m, rows_m), to] = piece
        v = v * rows_qk[g, 1:2, :]
        for k, piece in enumerate(split(v[0:feats])):
            mat[pl.ds(k * feats, feats), to] = piece
        m, c = v[feats : feats + 1], v[feats + 1 : feats + 2]
        m_hi, c_hi = m.astype(BF16).astype(F32), c.astype(BF16).astype(F32)
        last = jnp.where(at_last % 2 == 0, c_hi, c - c_hi)
        last = jnp.where(at_last == 0, m_hi, jnp.where(at_last == 1, m - m_hi, last))
        mat[pl.ds(2 * feats, 16), to] = jnp.where(at_last < 8, last, 0.0).astype(BF16)

    def both(p, carry):
        pair_at = w_all.at[pl.ds(2 * p, 2)]
        pltpu.make_async_copy(pair_at, pair_at, wsem.at[p]).wait()
        for g in (2 * p, 2 * p + 1):
            project(g)
        return carry

    def share(h):
        pack(m_all[:, pl.ds(h * part, part)], gram_s.at[h])
        out = [
            pltpu.make_async_remote_copy(
                src_ref=gram_s.at[h], dst_ref=gram_r.at[h, i - 1], send_sem=ss_sem.at[h],
                recv_sem=sr_sem.at[h], device_id=(lax.rem(t + i, count_t), r), device_id_type=MESH,
            )
            for i in range(1, count_t)
        ]
        for c in out:
            c.start()
        return pltpu.make_async_remote_copy(
            src_ref=gram_r.at[h], dst_ref=gram_r.at[h], send_sem=ss_sem.at[h], recv_sem=sr_sem.at[h],
            device_id=(t, r), device_id_type=MESH,
        )

    middle = -(-count_n // 2)
    ahead = min(2, middle)
    lax.fori_loop(0, ahead, both, 0)
    for copy, p in zip(halo, plan):
        def take(copy=copy, p=p):
            copy.wait_recv()
            for k, i in enumerate(p[6]):
                tot[pl.ds(i * lats, lats), :] += rcv[pl.ds((p[0] + k) * lats, lats), :]
        pl.when(p[5])(take)

    lane = lax.broadcasted_iota(jnp.int32, (lats, cols), 1)
    for q in range(2):
        f0, f1 = tot[pl.ds(q * lats, lats), :], tot[pl.ds((2 + q) * lats, lats), :]
        lat_all[own, pl.ds(2 * q * lats, lats), :] = jnp.where(lane < half, f0, pltpu.roll(f1, half, 1)).astype(BF16)
        lat_all[own, pl.ds((2 * q + 1) * lats, lats), :] = jnp.where(lane < half, pltpu.roll(f0, half, 1), f1).astype(BF16)

    inner = 1
    while inner * inner * 4 <= count_r and count_r % (inner * 2) == 0:
        inner *= 2
    outer = count_r // inner
    flat = count_t // 2 * inner
    group, away = outer * flat, (outer - 1) * flat
    side = lax.rem(t, 2)
    mate = t + 1 - 2 * side
    far, near, chip, chips = r // inner, lax.rem(r, inner), t // 2, count_t // 2
    flip = lax.min(far // max(outer // 2, 1), 1)
    mirror = far + flip * (outer - 1 - 2 * far)

    def place(i):
        v = outer - 1 - i // flat
        v = v - lax.max(0, lax.min(1, mirror - v + 1))
        v = v + lax.max(0, i // flat - outer + 2) * (mirror - v)
        k = flat - 1 - lax.rem(i, flat)
        other = lax.rem(chip + k // inner, chips)
        return other * 2, (v + flip * (outer - 1 - 2 * v)) * inner + lax.rem(near + lax.rem(k, inner), inner)

    def ident_of(i, s):
        pt, pr = place(i)
        return (pt + s) * count_r + pr

    def send(at, dt, dr, sent, got):
        return pltpu.make_async_remote_copy(
            src_ref=lat_all.at[at], dst_ref=lat_all.at[at], send_sem=as_sem.at[sent], recv_sem=ar_sem.at[got],
            device_id=(dt, dr), device_id_type=MESH,
        )

    def spread(i):
        pt, pr = place(i)
        return send(own, pt + side, pr, 0, far)

    def to_mate(i):
        return send(ident_of(i, side), mate, r, 1, outer)

    def all_of(n, sent, got):
        return send(pl.ds(0, n), mate, r, sent, got)

    def loop(first, last, body):
        lax.fori_loop(first, last, lambda i, c: (body(i), c)[1], 0)

    to_mate(group - 1).start()
    cuts = (0, min(flat, group - 1), min(2 * flat, group - 1), group - 1)

    def release(k):
        loop(cuts[k], cuts[k + 1], lambda i: spread(i).start())

    release(0)

    def relay(j, skip):
        _, pr = place(j * flat)
        all_of(flat - skip, 0, pr // inner).wait_recv()
        loop(j * flat, (j + 1) * flat - skip, lambda i: to_mate(i).start())

    lax.fori_loop(ahead, middle, both, 0)
    release(1)
    shares = [share(0)]
    release(2)
    lax.fori_loop(middle, count_n, both, 0)
    shares.append(share(1))
    for c in range(0, width, step):
        center_b = jnp.where(at16 == 0, pb[pl.ds(c, step)].reshape(1, step) - mean_b, 0.0)
        for k, piece in enumerate(split(pwf[:, c : c + step] - mean)):
            cen[pl.ds(k * rows_m, feats), c : c + step] = piece
        for k, piece in enumerate(split(center_b)):
            cen[pl.ds(k * rows_m + feats, 16), c : c + step] = piece
    pack(cen[...], gram_out.at[0])

    relay(outer - 1, 1)
    for j in range(outer - 2, -1, -1):
        relay(j, 0)
    for h in range(2):
        gram_out[1 + h] = gram_s[h]
        shares[h].wait_recv()
        for i in range(count_t - 1):
            gram_out[1 + h] += gram_r[h, i]

    lane1 = lax.broadcasted_iota(jnp.int32, (1, 128), 1)
    hf = feats // 2
    quads, tails = [], []
    for h in range(3):
        top, tail = gram_out[h, 0:hf, :], gram_out[h, hf : hf + 8, :]
        square = jnp.where(lane1 < feats, jnp.concatenate([top, pltpu.roll(top, feats, 1)], axis=0), 0.0)
        quads.append(square)
        tails.append(jnp.where(lane1 < feats, tail, 0.0))

    def entry(h, row, at):
        return jnp.sum(jnp.where(lane1 == at, gram_out[h, hf + row : hf + row + 1, :], 0.0), axis=1, keepdims=True)

    hi, lo = split(jnp.concatenate(quads + tails, axis=0))
    lo_at = pltpu.roll(lo.astype(F32), feats, 1).astype(BF16)
    stacked = hi + lo_at
    var_end = entry(0, 0, feats)
    ends = [(entry(h, 0, feats), entry(h, 0, feats + 1), entry(h, 1, feats + 1)) for h in (1, 2)]

    all_of(group, 1, outer).wait_recv()

    tokens = count_t * cols
    xs = jnp.concatenate([lat_all[packing[r * count_t + j]] for j in range(count_t)], axis=1)
    prod = dot(stacked, jnp.concatenate([xs, xs], axis=0))
    x = xs.astype(F32)

    def line(h, row):
        return prod[3 * feats + 8 * h + row : 3 * feats + 8 * h + row + 1, :]

    def square(h):
        return jnp.sum(x * prod[h * feats : (h + 1) * feats, :], axis=0, keepdims=True)

    var = (square(0) + 2.0 * line(0, 0) + var_end) / width + epsilon
    inv = lax.rsqrt(var)
    sigma = var * inv
    high = sigma.astype(BF16).astype(F32)
    mid = (sigma - high).astype(BF16).astype(F32)
    at16 = lax.broadcasted_iota(jnp.int32, (16, tokens), 0)
    more = jnp.where(at16 < 4, high, jnp.where(at16 < 6, mid, sigma - high - mid))
    more = jnp.where(at16 < 2, 1.0, jnp.where(at16 < 8, more, 0.0))
    scales = []
    for h in range(1, 3):
        e0, e1, e2 = ends[h - 1]
        ss = inv * inv * (square(h) + 2.0 * line(h, 0) + e0) + 2.0 * inv * (line(h, 1) + e1) + e2
        scales.append(lax.rsqrt(ss / width + epsilon) * inv)
    rest = jnp.zeros((2 * feats - 16, cols), F32)
    for j in range(count_t):
        at = slice(j * cols, (j + 1) * cols)
        left[at, :] = jnp.concatenate([x[:, at], x[:, at], more[:, at], rest], axis=0).T.astype(BF16)
        for h in range(2):
            coef[h, at, :] = jnp.broadcast_to(scales[h][:, at], (128, cols)).T

    for copy, p in zip(halo, plan):
        pl.when(p[4])(copy.wait_send)
    all_of(group - 1, 0, outer).wait_send()
    all_of(group, 1, outer).wait_send()
    for c in shares:
        c.wait_send()


def per_device(
    features, block_gain, conv_weight, conv_bias, latent_weight, latent_bias, patch_weight, patch_bias,
    shift_mod, scale_mod, query_weight, query_bias, query_gain, key_weight, key_bias, key_gain, packing,
):
    count_t, count_r = lax.axis_size("tm"), lax.axis_size("rows")
    count = count_t * count_r
    _, _, cols, chans = features.shape
    feats, width = patch_weight.shape
    lats = latent_weight.shape[1]
    part = query_weight.shape[1]
    tile = 256 if part % 256 == 0 else 128
    V = pltpu.VMEM
    rows_m = feats + 16
    operands = (
        packing, features, block_gain, conv_weight.reshape(9, 3, chans, chans), conv_bias, latent_weight.T, latent_bias, patch_weight, patch_bias,
        shift_mod, scale_mod, query_weight, query_bias, query_gain, key_weight, key_bias, key_gain,
    )
    like = lambda a: V(a.shape, a.dtype)
    scratch = [pltpu.SMEM(packing.shape, packing.dtype)] + [like(a) for a in operands[1:11]]
    scratch += [
        V((2 * part // tile, width, tile), BF16),
        V((part,), F32),
        V((part,), F32),
        V((part,), F32),
        V((part,), F32),
        V((2 * part // tile, 8, tile), F32),
        V((2, chans // 128, cols, 128), F32),
        V((9 * lats, 4 * chans), BF16),
        V((4 * cols, 4 * chans), BF16),
        V((9 * lats, 4 * cols), F32),
        V((12 * lats, cols), F32),
        V((12 * lats, cols), F32),
        V((4 * lats, cols), F32),
        V((count, feats, cols), BF16),
        V((feats, width), F32),
        V((4, feats, 128), F32),
        V((2 * rows_m, width), BF16),
        V((2 * rows_m, width), BF16),
        V((2 * rows_m, 2 * part), BF16),
        V((rows_m, 128), F32),
        V((3, feats // 2 + 8, 128), F32),
        V((2, feats // 2 + 8, 128), F32),
        V((2, count_t - 1, feats // 2 + 8, 128), F32),
    ]
    dma = pltpu.SemaphoreType.DMA
    scratch += [
        dma((14,)), dma((5,)), dma((part // tile,)), dma((5,)), dma((5,)), dma((2,)), dma((count_r + 1,)), dma((2,)), dma((2,)),
    ]
    outs = (
        jax.ShapeDtypeStruct((count_t * cols, 4 * feats), BF16),
        jax.ShapeDtypeStruct((2, count_t * cols, 128), F32),
        jax.ShapeDtypeStruct((4 * feats, 2 * part), BF16),
    )
    left, coef, mat = pl.pallas_call(
        functools.partial(kernel, count_t, count_r),
        out_shape=outs,
        in_specs=[pl.BlockSpec(memory_space=pltpu.HBM)] * 17,
        out_specs=(pl.BlockSpec(memory_space=V),) * 3,
        scratch_shapes=scratch,
        compiler_params=pltpu.CompilerParams(collective_id=0, has_side_effects=True, vmem_limit_bytes=47 * 2**20),
    )(*[pltpu.with_memory_space_constraint(a, pltpu.HBM) for a in operands])
    return finish(left, coef, mat)


def final(left, coef, mat, q_h, k_h, tiles, osem):
    part = mat.shape[1] // 2
    tokens = left.shape[0]
    tile = tiles.shape[2]
    count_n = part // tile

    def out_copy(i, n, dst):
        return pltpu.make_async_copy(tiles.at[i * count_n + n], dst.at[:, pl.ds(n * tile, tile)], osem.at[i])

    for i, dst in enumerate((q_h, k_h)):
        for n in range(count_n):
            for c in range(0, tokens, 256):
                at = pl.ds(c, 256)
                v = dot(left[at, :], mat[:, pl.ds(i * part + n * tile, tile)])
                for l in range(0, tile, 128):
                    o = coef[i, at, :] * v[:, l : l + 128]
                    tiles[i * count_n + n, at, pl.ds(l, 128)] = o.astype(BF16)
            out_copy(i, n, dst).start()
    for i in range(2):
        done = tiles.at[pl.ds(i * count_n, count_n)]
        pltpu.make_async_copy(done, done, osem.at[i]).wait()


def finish(left, coef, mat):
    tokens, part = left.shape[0], mat.shape[1] // 2
    tile = 256 if part % 256 == 0 else 128
    out = jax.ShapeDtypeStruct((tokens, part), BF16)
    V, dma = pltpu.VMEM, pltpu.SemaphoreType.DMA
    return pl.pallas_call(
        final,
        out_shape=(out, out),
        in_specs=[pl.BlockSpec(memory_space=V)] * 3,
        out_specs=(pl.BlockSpec(memory_space=pl.ANY),) * 2,
        scratch_shapes=[V((2 * part // tile, tokens, tile), BF16), dma((2,))],
        compiler_params=pltpu.CompilerParams(vmem_limit_bytes=12 * 2**20),
    )(left, coef, mat)


def solution(mesh):
    in_specs = (
        P("tm", "rows", None, None), P(), P(), P(), P(), P(), P(), P(), P(), P(),
        P(None, "tm"), P("tm"), P("tm"), P(None, "tm"), P("tm"), P("tm"), P(),
    )
    out_specs = (P("rows", "tm"), P("rows", "tm"))
    return jax.shard_map(per_device, mesh=mesh, in_specs=in_specs, out_specs=out_specs, check_vma=False)
```

```python
import functools

import jax
import jax.numpy as jnp
from jax import lax
from jax.experimental import pallas as pl
from jax.experimental.pallas import tpu as pltpu
from jax.sharding import PartitionSpec as P

epsilon = 1e-06
MESH = pl.DeviceIdType.MESH
F32, BF16 = jnp.float32, jnp.bfloat16


def dot(a, b, **kw):
    return jnp.dot(a, b, preferred_element_type=F32, **kw)


def split(v):
    hi = v.astype(BF16)
    return hi, (v - hi.astype(F32)).astype(BF16)


def kernel(
    count_t, count_r,
    packing_h, feat_h, gain_h, conv_h, cbias_h, lw_h, lbias_h, pw_h, pb_h, shift_h, scale_h,
    wq_h, qb_h, qg_h, wk_h, kb_h, kg_h,
    left, coef, mat,
    packing, feat, gain, conv, cbias, lw, lbias, pw, pb, shift, scale, w_all, qb, kb, qg, kg, rows_qk,
    scr, km, lhs, y_ref, snd, rcv, tot, lat_all, pwf, bounce, mod, cen, m_all, gram, gram_out, gram_s, gram_r,
    lsem, csem, wsem, hs_sem, hr_sem, as_sem, ar_sem, ss_sem, sr_sem,
):
    t, r = lax.axis_index("tm"), lax.axis_index("rows")
    count = count_t * count_r
    own = t * count_r + r
    _, _, cols, chans = feat.shape
    feats, width = pw.shape
    lats = lw.shape[0]
    half = cols // 2
    part = wq_h.shape[1]
    tile = w_all.shape[2]
    count_n = part // tile
    rows_m = mod.shape[0] // 2

    early = [(feat_h, feat), (gain_h, gain), (lw_h, lw)]
    late = [
        (pw_h, pw), (pb_h, pb), (shift_h, shift), (scale_h, scale), (cbias_h, cbias), (lbias_h, lbias),
        (qb_h, qb), (kb_h, kb), (qg_h, qg), (kg_h, kg), (packing_h, packing),
    ]
    copies = [pltpu.make_async_copy(s, d, lsem.at[i]) for i, (s, d) in enumerate(early + late)]
    first, later = copies[: len(early)], copies[len(early) :]
    runs = [(0, 1), (1, 2), (3, 2), (5, 2), (7, 2)]
    taps = [
        pltpu.make_async_copy(conv_h.at[pl.ds(i, n)], conv.at[pl.ds(i, n)], csem.at[k]) for k, (i, n) in enumerate(runs)
    ]
    for c in first + taps + later:
        c.start()
    loads = [
        pltpu.make_async_copy(w.at[:, pl.ds(n * tile, tile)], w_all.at[h * count_n + n], wsem.at[(h * count_n + n) // 2])
        for h, w in enumerate((wq_h, wk_h)) for n in range(count_n)
    ]

    barrier = pltpu.get_barrier_semaphore()

    def greet(i, c):
        other = lax.rem(own + i, count)
        pl.semaphore_signal(barrier, inc=1, device_id=(other // count_r, lax.rem(other, count_r)), device_id_type=MESH)
        return c

    lax.fori_loop(1, count, greet, 0)
    nt = (((1,), (1,)), ((), ()))

    for c in first:
        c.wait()
    lwv = lw[...]
    gain_v = gain[...].reshape(1, chans)
    row_at = lax.broadcasted_iota(jnp.int32, (half, 128), 0)
    for f in range(2):
        for w in range(2):
            v = feat[f, w].astype(F32)
            sm = jnp.mean(v * v, axis=-1, keepdims=True)
            x = v * lax.rsqrt(sm + epsilon) * gain_v
            act = (x / (1.0 + jnp.exp(-x))).astype(BF16).astype(F32)
            base = (f * 2 + w) * cols
            for l in range(chans // 128):
                scr[0, l] = act[:, l * 128 : (l + 1) * 128]
                scr[1, l] = v[:, l * 128 : (l + 1) * 128]
                even, odd = scr[0, l, pl.ds(0, half, 2), :], scr[0, l, pl.ds(1, half, 2), :]
                before = jnp.where(row_at == 0, 0.0, pltpu.roll(odd, 1, 0))
                after = jnp.where(row_at == half - 1, 0.0, pltpu.roll(even, half - 1, 0))
                plain = (scr[1, l, pl.ds(0, half, 2), :], scr[1, l, pl.ds(1, half, 2), :])
                for k, (low, high) in enumerate(((before, even), (even, odd), (odd, after), plain)):
                    lhs[pl.ds(base, half), pl.ds(k * chans + l * 128, 128)] = low.astype(BF16)
                    lhs[pl.ds(base + half, half), pl.ds(k * chans + l * 128, 128)] = high.astype(BF16)

    none = jnp.zeros((lats, chans), BF16)
    pair = jnp.concatenate(
        [jnp.concatenate([lwv, none], axis=1), jnp.concatenate([none, lwv], axis=1)], axis=0
    )
    km[:, pl.ds(3 * chans, chans)] = jnp.zeros((9 * lats, chans), BF16)
    km[pl.ds(7 * lats, lats), pl.ds(3 * chans, chans)] = lwv
    started = 0
    for p, (i, n) in enumerate(runs):
        ids = range(i, i + n)
        taps[p].wait()
        more = min(len(loads), (p + 1) * -(-len(loads) // 5))
        for c in loads[started:more]:
            c.start()
        started = more
        for e in range(3):
            rhs = jnp.concatenate([conv[i, e] for i in ids], axis=1)
            folded = lax.dot_general(pair if n == 2 else lwv, rhs, nt, preferred_element_type=F32)
            km[pl.ds(ids[0] * lats, lats * len(ids)), pl.ds(e * chans, chans)] = folded.astype(BF16)
    y_ref[...] = lax.dot_general(km[...], lhs[...], nt, preferred_element_type=F32)

    def total(d, q):
        out = None
        for f in range(2):
            for w in range(2):
                a, b = f + 2 - d, w + 1 - q
                if 0 <= a < 3 and 0 <= b < 3:
                    term = y_ref[pl.ds((a * 3 + b) * lats, lats), pl.ds((f * 2 + w) * cols, cols)]
                    out = term if out is None else out + term
        return out

    sent = [(0, -1), (1, -1), (0, 2), (1, 2), (2, 0), (2, 1), (3, 0), (3, 1), (2, -1), (3, -1), (2, 2), (3, 2)]
    for i, (d, q) in enumerate(sent):
        snd[pl.ds(i * lats, lats), :] = total(d, q)

    pl.semaphore_wait(barrier, count - 1)

    has_up, has_down = r > 0, r < count_r - 1
    has_next, has_prev = t < count_t - 1, t > 0
    plan = [
        (0, 2, t, r - 1, has_up, has_down, (1, 3)),
        (2, 2, t, r + 1, has_down, has_up, (0, 2)),
        (4, 4, t + 1, r, has_next, has_prev, (0, 1, 2, 3)),
        (8, 2, t + 1, r - 1, has_next & has_up, has_prev & has_down, (1, 3)),
        (10, 2, t + 1, r + 1, has_next & has_down, has_prev & has_up, (0, 2)),
    ]
    halo = []
    for k, (at, n, dt, dr, _, _, _) in enumerate(plan):
        rows = pl.ds(at * lats, n * lats)
        halo.append(pltpu.make_async_remote_copy(
            src_ref=snd.at[rows], dst_ref=rcv.at[rows], send_sem=hs_sem.at[k], recv_sem=hr_sem.at[k],
            device_id=(dt, dr), device_id_type=MESH,
        ))
    for k in (3, 4, 0, 1, 2):
        pl.when(plan[k][4])(halo[k].start)

    for c in later:
        c.wait()
    offset = jnp.sum(lwv.astype(F32) * cbias[...].reshape(1, chans), axis=1, keepdims=True)
    at_l = lax.broadcasted_iota(jnp.int32, (lats, lats), 0) == lax.broadcasted_iota(jnp.int32, (lats, lats), 1)
    offset = offset + jnp.sum(jnp.where(at_l, lbias[...].reshape(1, lats), 0.0), axis=1, keepdims=True)
    for i, (d, q) in enumerate(((0, 0), (0, 1), (1, 0), (1, 1))):
        tot[pl.ds(i * lats, lats), :] = total(d, q) + offset

    step = 512

    def lanes_sum(v):
        out = v[:, 0:128]
        for i in range(1, v.shape[1] // 128):
            out = out + v[:, i * 128 : (i + 1) * 128]
        return out

    total_w = jnp.zeros((feats, 128), F32)
    total_b = jnp.zeros((1, 128), F32)
    groups = feats // lats
    for c in range(0, width, step):
        for l in range(step // 128):
            bounce[l] = pw[:, c + l * 128 : c + (l + 1) * 128].astype(F32)
        mixed = jnp.concatenate([
            jnp.concatenate([bounce[l, pl.ds(k, lats, groups), :] for k in range(groups)], axis=0)
            for l in range(step // 128)
        ], axis=1)
        pwf[:, c : c + step] = mixed
        total_w = total_w + lanes_sum(mixed)
        total_b = total_b + lanes_sum(pb[pl.ds(c, step)].reshape(1, step))
    mean = jnp.sum(total_w, axis=1, keepdims=True) / width
    mean_b = jnp.sum(total_b, axis=1, keepdims=True) / width
    at16 = lax.broadcasted_iota(jnp.int32, (16, step), 0)
    for c in range(0, width, step):
        gains = 1.0 + scale[pl.ds(c, step)].reshape(1, step)
        center = pwf[:, c : c + step] - mean
        center_b = pb[pl.ds(c, step)].reshape(1, step) - mean_b
        moved = shift[pl.ds(c, step)].reshape(1, step)
        last = jnp.where(at16 == 0, center_b * gains, jnp.where(at16 == 1, moved, 0.0))
        for k, piece in enumerate(split(center * gains)):
            mod[pl.ds(k * rows_m, feats), c : c + step] = piece
        for k, piece in enumerate(split(last)):
            mod[pl.ds(k * rows_m + feats, 16), c : c + step] = piece

    def gram_of(v):
        g = lax.dot_general(v, v, nt, preferred_element_type=F32)
        return g[0:rows_m, 0:rows_m] + g[0:rows_m, rows_m:] + g[rows_m:, 0:rows_m] + g[rows_m:, rows_m:]

    lower = lax.broadcasted_iota(jnp.int32, (feats // 2, 128), 1) < feats

    def pack(v, ref):
        gram[:, 0:rows_m] = gram_of(v)
        ref[pl.ds(0, feats // 2), :] = jnp.where(
            lower, gram[0 : feats // 2, :], pltpu.roll(gram[feats // 2 : feats, :], feats, 1)
        )
        ref[pl.ds(feats // 2, 8), :] = gram[feats : feats + 8, :]

    gram[...] = jnp.zeros(gram.shape, F32)
    for h, (bias, gains) in enumerate(((qb, qg), (kb, kg))):
        for n in range(count_n):
            at = pl.ds(n * tile, tile)
            rows_qk[h * count_n + n, 0:1, :] = bias[at].reshape(1, tile)
            rows_qk[h * count_n + n, 1:2, :] = gains[at].reshape(1, tile)
    mat[pl.ds(2 * feats + 16, 2 * feats - 16), :] = jnp.zeros((2 * feats - 16, 2 * part), BF16)
    at_row = lax.broadcasted_iota(jnp.int32, (rows_m, tile), 0)
    at_last = lax.broadcasted_iota(jnp.int32, (16, tile), 0)

    def project(g):
        to = pl.ds(pl.multiple_of(g * tile, tile), tile)
        v = dot(mod[...], w_all[g])
        v = v[0:rows_m] + v[rows_m:] + jnp.where(at_row == feats + 1, rows_qk[g, 0:1, :], 0.0)
        for k, piece in enumerate(split(v)):
            m_all[pl.ds(k * rows_m, rows_m), to] = piece
        v = v * rows_qk[g, 1:2, :]
        for k, piece in enumerate(split(v[0:feats])):
            mat[pl.ds(k * feats, feats), to] = piece
        m, c = v[feats : feats + 1], v[feats + 1 : feats + 2]
        m_hi, c_hi = m.astype(BF16).astype(F32), c.astype(BF16).astype(F32)
        last = jnp.where(at_last % 2 == 0, c_hi, c - c_hi)
        last = jnp.where(at_last == 0, m_hi, jnp.where(at_last == 1, m - m_hi, last))
        mat[pl.ds(2 * feats, 16), to] = jnp.where(at_last < 8, last, 0.0).astype(BF16)

    def both(p, carry):
        pair_at = w_all.at[pl.ds(2 * p, 2)]
        pltpu.make_async_copy(pair_at, pair_at, wsem.at[p]).wait()
        for g in (2 * p, 2 * p + 1):
            project(g)
        return carry

    def share(h):
        pack(m_all[:, pl.ds(h * part, part)], gram_s.at[h])
        out = [
            pltpu.make_async_remote_copy(
                src_ref=gram_s.at[h], dst_ref=gram_r.at[h, i - 1], send_sem=ss_sem.at[h],
                recv_sem=sr_sem.at[h], device_id=(lax.rem(t + i, count_t), r), device_id_type=MESH,
            )
            for i in range(1, count_t)
        ]
        for c in out:
            c.start()
        return pltpu.make_async_remote_copy(
            src_ref=gram_r.at[h], dst_ref=gram_r.at[h], send_sem=ss_sem.at[h], recv_sem=sr_sem.at[h],
            device_id=(t, r), device_id_type=MESH,
        )

    middle = -(-count_n // 2)
    ahead = min(2, middle)
    lax.fori_loop(0, ahead, both, 0)
    for copy, p in zip(halo, plan):
        def take(copy=copy, p=p):
            copy.wait_recv()
            for k, i in enumerate(p[6]):
                tot[pl.ds(i * lats, lats), :] += rcv[pl.ds((p[0] + k) * lats, lats), :]
        pl.when(p[5])(take)

    lane = lax.broadcasted_iota(jnp.int32, (lats, cols), 1)
    for q in range(2):
        f0, f1 = tot[pl.ds(q * lats, lats), :], tot[pl.ds((2 + q) * lats, lats), :]
        lat_all[own, pl.ds(2 * q * lats, lats), :] = jnp.where(lane < half, f0, pltpu.roll(f1, half, 1)).astype(BF16)
        lat_all[own, pl.ds((2 * q + 1) * lats, lats), :] = jnp.where(lane < half, pltpu.roll(f0, half, 1), f1).astype(BF16)

    inner = 1
    while inner * inner * 4 <= count_r and count_r % (inner * 2) == 0:
        inner *= 2
    outer = count_r // inner
    flat = count_t // 2 * inner
    group, away = outer * flat, (outer - 1) * flat
    side = lax.rem(t, 2)
    mate = t + 1 - 2 * side
    far, near, chip, chips = r // inner, lax.rem(r, inner), t // 2, count_t // 2
    flip = lax.min(far // max(outer // 2, 1), 1)
    mirror = far + flip * (outer - 1 - 2 * far)

    def place(i):
        v = outer - 1 - i // flat
        v = v - lax.max(0, lax.min(1, mirror - v + 1))
        v = v + lax.max(0, i // flat - outer + 2) * (mirror - v)
        k = flat - 1 - lax.rem(i, flat)
        other = lax.rem(chip + k // inner, chips)
        return other * 2, (v + flip * (outer - 1 - 2 * v)) * inner + lax.rem(near + lax.rem(k, inner), inner)

    def ident_of(i, s):
        pt, pr = place(i)
        return (pt + s) * count_r + pr

    def send(at, dt, dr, sent, got):
        return pltpu.make_async_remote_copy(
            src_ref=lat_all.at[at], dst_ref=lat_all.at[at], send_sem=as_sem.at[sent], recv_sem=ar_sem.at[got],
            device_id=(dt, dr), device_id_type=MESH,
        )

    def spread(i):
        pt, pr = place(i)
        return send(own, pt + side, pr, 0, far)

    def to_mate(i):
        return send(ident_of(i, side), mate, r, 1, outer)

    def all_of(n, sent, got):
        return send(pl.ds(0, n), mate, r, sent, got)

    def loop(first, last, body):
        lax.fori_loop(first, last, lambda i, c: (body(i), c)[1], 0)

    cuts = (0, min(flat, group - 1), min(2 * flat, group - 1), group - 1)

    def release(k):
        loop(cuts[k], cuts[k + 1], lambda i: spread(i).start())

    release(0)
    to_mate(group - 1).start()

    def relay(j, skip):
        _, pr = place(j * flat)
        all_of(flat - skip, 0, pr // inner).wait_recv()
        loop(j * flat, (j + 1) * flat - skip, lambda i: to_mate(i).start())

    lax.fori_loop(ahead, middle, both, 0)
    release(1)
    shares = [share(0)]
    release(2)
    lax.fori_loop(middle, count_n, both, 0)
    shares.append(share(1))
    for c in range(0, width, step):
        center_b = jnp.where(at16 == 0, pb[pl.ds(c, step)].reshape(1, step) - mean_b, 0.0)
        for k, piece in enumerate(split(pwf[:, c : c + step] - mean)):
            cen[pl.ds(k * rows_m, feats), c : c + step] = piece
        for k, piece in enumerate(split(center_b)):
            cen[pl.ds(k * rows_m + feats, 16), c : c + step] = piece
    pack(cen[...], gram_out.at[0])

    relay(outer - 1, 1)
    for j in range(outer - 2, -1, -1):
        relay(j, 0)
    for h in range(2):
        gram_out[1 + h] = gram_s[h]
        shares[h].wait_recv()
        for i in range(count_t - 1):
            gram_out[1 + h] += gram_r[h, i]

    lane1 = lax.broadcasted_iota(jnp.int32, (1, 128), 1)
    hf = feats // 2
    quads, tails = [], []
    for h in range(3):
        top, tail = gram_out[h, 0:hf, :], gram_out[h, hf : hf + 8, :]
        square = jnp.where(lane1 < feats, jnp.concatenate([top, pltpu.roll(top, feats, 1)], axis=0), 0.0)
        quads.append(square)
        tails.append(jnp.where(lane1 < feats, tail, 0.0))

    def entry(h, row, at):
        return jnp.sum(jnp.where(lane1 == at, gram_out[h, hf + row : hf + row + 1, :], 0.0), axis=1, keepdims=True)

    hi, lo = split(jnp.concatenate(quads + tails, axis=0))
    lo_at = pltpu.roll(lo.astype(F32), feats, 1).astype(BF16)
    stacked = hi + lo_at
    var_end = entry(0, 0, feats)
    ends = [(entry(h, 0, feats), entry(h, 0, feats + 1), entry(h, 1, feats + 1)) for h in (1, 2)]

    all_of(group, 1, outer).wait_recv()

    tokens = count_t * cols
    xs = jnp.concatenate([lat_all[packing[r * count_t + j]] for j in range(count_t)], axis=1)
    prod = dot(stacked, jnp.concatenate([xs, xs], axis=0))
    x = xs.astype(F32)

    def line(h, row):
        return prod[3 * feats + 8 * h + row : 3 * feats + 8 * h + row + 1, :]

    def square(h):
        return jnp.sum(x * prod[h * feats : (h + 1) * feats, :], axis=0, keepdims=True)

    var = (square(0) + 2.0 * line(0, 0) + var_end) / width + epsilon
    inv = lax.rsqrt(var)
    sigma = var * inv
    high = sigma.astype(BF16).astype(F32)
    mid = (sigma - high).astype(BF16).astype(F32)
    at16 = lax.broadcasted_iota(jnp.int32, (16, tokens), 0)
    more = jnp.where(at16 < 4, high, jnp.where(at16 < 6, mid, sigma - high - mid))
    more = jnp.where(at16 < 2, 1.0, jnp.where(at16 < 8, more, 0.0))
    scales = []
    for h in range(1, 3):
        e0, e1, e2 = ends[h - 1]
        ss = inv * inv * (square(h) + 2.0 * line(h, 0) + e0) + 2.0 * inv * (line(h, 1) + e1) + e2
        scales.append(lax.rsqrt(ss / width + epsilon) * inv)
    rest = jnp.zeros((2 * feats - 16, cols), F32)
    for j in range(count_t):
        at = slice(j * cols, (j + 1) * cols)
        left[at, :] = jnp.concatenate([x[:, at], x[:, at], more[:, at], rest], axis=0).T.astype(BF16)
        for h in range(2):
            coef[h, at, :] = jnp.broadcast_to(scales[h][:, at], (128, cols)).T

    for copy, p in zip(halo, plan):
        pl.when(p[4])(copy.wait_send)
    all_of(group - 1, 0, outer).wait_send()
    all_of(group, 1, outer).wait_send()
    for c in shares:
        c.wait_send()


def per_device(
    features, block_gain, conv_weight, conv_bias, latent_weight, latent_bias, patch_weight, patch_bias,
    shift_mod, scale_mod, query_weight, query_bias, query_gain, key_weight, key_bias, key_gain, packing,
):
    count_t, count_r = lax.axis_size("tm"), lax.axis_size("rows")
    count = count_t * count_r
    _, _, cols, chans = features.shape
    feats, width = patch_weight.shape
    lats = latent_weight.shape[1]
    part = query_weight.shape[1]
    tile = 256 if part % 256 == 0 else 128
    V = pltpu.VMEM
    rows_m = feats + 16
    operands = (
        packing, features, block_gain, conv_weight.reshape(9, 3, chans, chans), conv_bias, latent_weight.T, latent_bias, patch_weight, patch_bias,
        shift_mod, scale_mod, query_weight, query_bias, query_gain, key_weight, key_bias, key_gain,
    )
    like = lambda a: V(a.shape, a.dtype)
    scratch = [pltpu.SMEM(packing.shape, packing.dtype)] + [like(a) for a in operands[1:11]]
    scratch += [
        V((2 * part // tile, width, tile), BF16),
        V((part,), F32),
        V((part,), F32),
        V((part,), F32),
        V((part,), F32),
        V((2 * part // tile, 8, tile), F32),
        V((2, chans // 128, cols, 128), F32),
        V((9 * lats, 4 * chans), BF16),
        V((4 * cols, 4 * chans), BF16),
        V((9 * lats, 4 * cols), F32),
        V((12 * lats, cols), F32),
        V((12 * lats, cols), F32),
        V((4 * lats, cols), F32),
        V((count, feats, cols), BF16),
        V((feats, width), F32),
        V((4, feats, 128), F32),
        V((2 * rows_m, width), BF16),
        V((2 * rows_m, width), BF16),
        V((2 * rows_m, 2 * part), BF16),
        V((rows_m, 128), F32),
        V((3, feats // 2 + 8, 128), F32),
        V((2, feats // 2 + 8, 128), F32),
        V((2, count_t - 1, feats // 2 + 8, 128), F32),
    ]
    dma = pltpu.SemaphoreType.DMA
    scratch += [
        dma((14,)), dma((5,)), dma((part // tile,)), dma((5,)), dma((5,)), dma((2,)), dma((count_r + 1,)), dma((2,)), dma((2,)),
    ]
    outs = (
        jax.ShapeDtypeStruct((count_t * cols, 4 * feats), BF16),
        jax.ShapeDtypeStruct((2, count_t * cols, 128), F32),
        jax.ShapeDtypeStruct((4 * feats, 2 * part), BF16),
    )
    left, coef, mat = pl.pallas_call(
        functools.partial(kernel, count_t, count_r),
        out_shape=outs,
        in_specs=[pl.BlockSpec(memory_space=pltpu.HBM)] * 17,
        out_specs=(pl.BlockSpec(memory_space=V),) * 3,
        scratch_shapes=scratch,
        compiler_params=pltpu.CompilerParams(collective_id=0, has_side_effects=True, vmem_limit_bytes=47 * 2**20),
    )(*[pltpu.with_memory_space_constraint(a, pltpu.HBM) for a in operands])
    return finish(left, coef, mat)


def final(left, coef, mat, q_h, k_h, tiles, osem):
    part = mat.shape[1] // 2
    tokens = left.shape[0]
    tile = tiles.shape[2]
    count_n = part // tile

    def out_copy(i, n, dst):
        return pltpu.make_async_copy(tiles.at[i * count_n + n], dst.at[:, pl.ds(n * tile, tile)], osem.at[i])

    for i, dst in enumerate((q_h, k_h)):
        for n in range(count_n):
            for c in range(0, tokens, 256):
                at = pl.ds(c, 256)
                v = dot(left[at, :], mat[:, pl.ds(i * part + n * tile, tile)])
                for l in range(0, tile, 128):
                    o = coef[i, at, :] * v[:, l : l + 128]
                    tiles[i * count_n + n, at, pl.ds(l, 128)] = o.astype(BF16)
            out_copy(i, n, dst).start()
    for i in range(2):
        done = tiles.at[pl.ds(i * count_n, count_n)]
        pltpu.make_async_copy(done, done, osem.at[i]).wait()


def finish(left, coef, mat):
    tokens, part = left.shape[0], mat.shape[1] // 2
    tile = 256 if part % 256 == 0 else 128
    out = jax.ShapeDtypeStruct((tokens, part), BF16)
    V, dma = pltpu.VMEM, pltpu.SemaphoreType.DMA
    return pl.pallas_call(
        final,
        out_shape=(out, out),
        in_specs=[pl.BlockSpec(memory_space=V)] * 3,
        out_specs=(pl.BlockSpec(memory_space=pl.ANY),) * 2,
        scratch_shapes=[V((2 * part // tile, tokens, tile), BF16), dma((2,))],
        compiler_params=pltpu.CompilerParams(vmem_limit_bytes=12 * 2**20),
    )(left, coef, mat)


def solution(mesh):
    in_specs = (
        P("tm", "rows", None, None), P(), P(), P(), P(), P(), P(), P(), P(), P(),
        P(None, "tm"), P("tm"), P("tm"), P(None, "tm"), P("tm"), P("tm"), P(),
    )
    out_specs = (P("rows", "tm"), P("rows", "tm"))
    return jax.shard_map(per_device, mesh=mesh, in_specs=in_specs, out_specs=out_specs, check_vma=False)
```
